128 devices in a mesh: member: 4 (over z), tile: 32 (over y, x, core).
Axes of the slice: x: 4, y: 4, z: 4, core: 2. Of those that a mesh axis runs over, the one named last changes fastest.
Arguments:
- teacher_logits: bfloat16 [16, 4096, 4096], P('member', 'tile'), may hold values from -8 to 260
- coverage: int32 [4096], P('tile'), may hold values from 0 to 31, as said below
- features: bfloat16 [4, 1024, 64, 256], P('member', 'tile'), may hold values from -6 to 6
- labels: int32 [4, 1024, 64], P('member', 'tile'), may hold values from 0 to 63
- first_weight: bfloat16 [3, 3, 256, 256], replicated, may hold values from -0.125 to 0.125
- second_weight: bfloat16 [3, 3, 256, 256], replicated, may hold values from -0.125 to 0.125
- head_weight: bfloat16 [256, 64], replicated, may hold values from -0.375 to 0.375
Outputs:
- first_kernel_grad: float32 [3, 3, 256, 256], replicated
- second_kernel_grad: float32 [3, 3, 256, 256], replicated
- head_kernel_grad: float32 [256, 64], replicated
- loss_value: float32 [], replicated
The draws below stay inside these ranges and needn't reach their ends.
Inputs may be any that keep to these rules, and one draw needn't show every extreme that they name: Slot k of column t goes to column coverage[t * 128 + k]; for every slot each column receives it from exactly one column. Within each block of 32 consecutive slots a column sends at most 2 tiles to any one column and exactly 2 to one; over all 128 slots at most 8 to any one column, reached.
All inputs are finite; a program needn't handle non-finite values.
Results may differ from the reference program's by a relative error of at most 0.013.
The reference program's roundings to bfloat16 on the way (of `hidden_one`, `hidden_two`, `logit_grad`, `grad_two` and `grad_one`) count: a program that leaves them out, or rounds other values in their place, can miss the bound.
Values may be sent and summed in bfloat16 or wider, within the bound.
A program may use at most 128 MiB of HBM per device.

```python
import math
import jax
import jax.numpy as jnp
from jax import lax

C = 256
K = 64
TE = 8
W = 64
RD = 32
MEMBERS = 16
SD = 32
TD = 128
TILES = 4096
CAPB = 2
ROWS = 1024
N_MEMBER = 4
N_TILE = 32


def draw_teacher_logits(key, part):
    array_shape = (MEMBERS, TILES, TE * TE, K)
    values = jnp.clip(2.0 * jax.random.normal(key, array_shape, jnp.float32), -8.0, 8.0)
    return values.reshape(MEMBERS, TILES, TE * TE * K).astype(jnp.bfloat16)


def draw_coverage(key, part):
    source_column = jax.random.randint(jax.random.fold_in(key, 11), (), 0, N_TILE).astype(jnp.int32)
    target_column = jax.random.randint(jax.random.fold_in(key, 12), (), 0, N_TILE).astype(jnp.int32)
    columns = jnp.arange(N_TILE, dtype=jnp.int32)
    blocks = []
    for group_index in range(N_MEMBER):
        ordering = jax.random.permutation(jax.random.fold_in(key, 300 + group_index), N_TILE).astype(jnp.int32)
        mapping = jnp.zeros((N_TILE,), jnp.int32).at[ordering].set(columns)
        forced = (ordering[target_column] - source_column) % N_TILE
        others = (forced + 1 + jnp.arange(N_TILE - 1, dtype=jnp.int32)) % N_TILE
        offset_pool = jnp.repeat(others, CAPB)
        shuffled = jax.random.permutation(jax.random.fold_in(key, 100 + group_index), offset_pool)[:SD - CAPB]
        chosen = jnp.concatenate([jnp.full((CAPB,), forced, jnp.int32), shuffled.astype(jnp.int32)])
        offsets = jax.random.permutation(jax.random.fold_in(key, 200 + group_index), chosen)
        shifted = (columns[:, None] + offsets[None, :]) % N_TILE
        blocks.append(mapping[shifted])
    return jnp.concatenate(blocks, axis=1).reshape(TILES).astype(jnp.int32)


def plant(result, stream_key, smallest, largest):
    longest = result.shape.index(max(result.shape))
    spots = []
    for shift in (0, 1):
        where = [jax.random.randint(jax.random.fold_in(stream_key, axis), (), 0, length) for axis, length in enumerate(result.shape)]
        where[longest] = (where[longest] + shift) % result.shape[longest]
        spots.append(tuple(where))
    return result.at[spots[0]].set(smallest).at[spots[1]].set(largest)


def block_levels(own_key, extent, pieces, least, high):
    factor_of, own = 1.0, jax.random.fold_in(own_key, 6)
    for position, blocks in pieces:
        draws = jnp.exp(jax.random.uniform(jax.random.fold_in(own, position), (blocks,), jnp.float32, least / len(pieces), high / len(pieces)))
        factor_of = factor_of * jnp.repeat(draws, extent[position] // blocks).reshape([-1 if axis == position else 1 for axis in range(len(extent))])
    return factor_of


def bell_draw(key, shape, deviation, bound, pieces=(), kind=jnp.bfloat16):
    result = jax.random.normal(key, shape, jnp.float32) * deviation
    if len(pieces) > 0:
        result = block_levels(key, shape, pieces, -0.22, 0.18) * result
    return jnp.clip(result, min=-bound, max=bound).astype(kind)


def setup_inputs(seed: int = 0) -> dict:
    splits = jax.random.split(jax.random.key(seed), 8)
    teacher_logits = draw_teacher_logits(jax.random.fold_in(splits[7], 71), 0)
    coverage = draw_coverage(jax.random.fold_in(splits[7], 71), 0)
    features = bell_draw(splits[2], (N_MEMBER, ROWS, W, C), 1.0, 6.0, ((0, 4), (1, 32)))
    labels = plant(jax.random.randint(splits[3], (N_MEMBER, ROWS, W), 0, K), jax.random.fold_in(splits[3], 1), 0, K - 1).astype(jnp.int32)
    first_weight = bell_draw(splits[4], (3, 3, C, C), (9 * C) ** -0.5, 0.125)
    second_weight = bell_draw(splits[5], (3, 3, C, C), (9 * C) ** -0.5, 0.125)
    head_weight = bell_draw(splits[6], (C, K), C ** -0.5, 0.375)
    return {"teacher_logits": teacher_logits, "coverage": coverage, "features": features, "labels": labels, "first_weight": first_weight, "second_weight": second_weight, "head_weight": head_weight}


def conv_taps(padded, kernel, dilation, row_count, col_count):
    channels = padded.shape[-1]
    summed = jnp.zeros((row_count * col_count, kernel.shape[-1]), jnp.float32)
    for row_tap in range(3):
        for col_tap in range(3):
            window = padded[row_tap * dilation:row_tap * dilation + row_count, col_tap * dilation:col_tap * dilation + col_count]
            summed = summed + jnp.dot(window.reshape(-1, channels), kernel[row_tap, col_tap], preferred_element_type=jnp.float32)
    return summed

def kernel_grad(padded, grads, dilation, row_count, col_count):
    channels = padded.shape[-1]
    flat_grads = grads.reshape(row_count * col_count, -1)
    outer = []
    for row_tap in range(3):
        inner = []
        for col_tap in range(3):
            window = padded[row_tap * dilation:row_tap * dilation + row_count, col_tap * dilation:col_tap * dilation + col_count]
            inner.append(jnp.dot(window.reshape(-1, channels).T, flat_grads, preferred_element_type=jnp.float32))
        outer.append(jnp.stack(inner))
    return jnp.stack(outer)

def input_grad(padded_grads, kernel, dilation, row_count, col_count):
    channels = padded_grads.shape[-1]
    summed = jnp.zeros((row_count * col_count, kernel.shape[2]), jnp.float32)
    for row_tap in range(3):
        for col_tap in range(3):
            row_from = (2 - row_tap) * dilation
            col_from = (2 - col_tap) * dilation
            window = padded_grads[row_from:row_from + row_count, col_from:col_from + col_count]
            summed = summed + jnp.dot(window.reshape(-1, channels), kernel[row_tap, col_tap].T, preferred_element_type=jnp.float32)
    return summed

def head_terms(hidden_two, head_weight, teacher_mean, spread_sum, label_rows, scale):
    classes = head_weight.shape[1]
    logits = jnp.dot(hidden_two, head_weight, preferred_element_type=jnp.float32)
    log_student = jax.nn.log_softmax(logits, axis=-1)
    student_probs = jnp.exp(log_student)
    cell_weight = 1.0 / (0.1 + spread_sum)
    onehot = (label_rows[:, None] == jnp.arange(classes, dtype=jnp.int32)[None, :]).astype(jnp.float32)
    entropy_part = lax.optimization_barrier(jnp.sum(jax.scipy.special.xlogy(teacher_mean, teacher_mean), axis=-1))
    pixel_loss = cell_weight * (entropy_part - lax.optimization_barrier(jnp.sum(teacher_mean * log_student, axis=-1))) - lax.optimization_barrier(jnp.sum(onehot * log_student, axis=-1))
    logit_grad = ((cell_weight[:, None] * (student_probs - teacher_mean) + student_probs - onehot) * scale).astype(jnp.bfloat16)
    head_grad = jnp.dot(hidden_two.T, logit_grad, preferred_element_type=jnp.float32)
    return (jnp.sum(pixel_loss), logit_grad, head_grad)

def reference(teacher_logits, coverage, features, labels, first_weight, second_weight, head_weight):
    pixel_count = TE * TE

    def one_column(column):
        block_logits = lax.dynamic_slice_in_dim(teacher_logits, column * TD, TD, 1)
        probabilities = jax.nn.softmax(block_logits.astype(jnp.float32).reshape(MEMBERS, TD, pixel_count, K), axis=-1)
        return (lax.optimization_barrier(jnp.sum(probabilities, 0)), lax.optimization_barrier(jnp.sum(probabilities * probabilities, axis=(0, 3))))
    first_sum, second_sum = lax.map(one_column, jnp.arange(N_TILE, dtype=jnp.int32))
    teacher_mean = first_sum / MEMBERS
    spread_sum = second_sum / MEMBERS - lax.optimization_barrier(jnp.sum(teacher_mean * teacher_mean, axis=-1))
    slot_index = jnp.arange(TD, dtype=jnp.int32)
    destination = ((slot_index // SD)[None, :] * (N_TILE * SD) + coverage.reshape(N_TILE, TD) * SD + (slot_index % SD)[None, :]).reshape(-1)
    mean_tiles = jnp.zeros((N_MEMBER * N_TILE * SD, pixel_count, K), jnp.float32).at[destination].set(teacher_mean.reshape(-1, pixel_count, K))
    spread_tiles = jnp.zeros((N_MEMBER * N_TILE * SD, pixel_count), jnp.float32).at[destination].set(spread_sum.reshape(-1, pixel_count))
    mean_map = mean_tiles.reshape(N_MEMBER, N_TILE, RD // TE, W // TE, TE, TE, K).transpose(0, 1, 2, 4, 3, 5, 6).reshape(N_MEMBER, N_TILE * RD, W, K)
    spread_map = spread_tiles.reshape(N_MEMBER, N_TILE, RD // TE, W // TE, TE, TE).transpose(0, 1, 2, 4, 3, 5).reshape(N_MEMBER, N_TILE * RD, W)
    scale = 1.0 / math.sqrt(N_MEMBER * N_TILE * RD * W)
    row_total = N_TILE * RD

    def strip(inputs):
        strip_features, strip_labels, strip_mean, strip_spread = inputs
        padded = jnp.pad(strip_features, ((1, 1), (1, 1), (0, 0)))
        pre_one = conv_taps(padded, first_weight, 1, row_total, W)
        hidden_one = jnp.where(pre_one > 0, pre_one, 0.0).astype(jnp.bfloat16).reshape(row_total, W, C)
        padded_one = jnp.pad(hidden_one, ((2, 2), (2, 2), (0, 0)))
        pre_two = conv_taps(padded_one, second_weight, 2, row_total, W)
        hidden_two = jnp.where(pre_two > 0, pre_two, 0.0).astype(jnp.bfloat16)
        loss_sum, logit_grad, head_grad = head_terms(hidden_two, head_weight, strip_mean.reshape(-1, K), strip_spread.reshape(-1), strip_labels.reshape(-1), scale)
        hidden_grad = jnp.dot(logit_grad, head_weight.T, preferred_element_type=jnp.float32)
        grad_two = jnp.where(pre_two > 0, hidden_grad, 0.0).astype(jnp.bfloat16).reshape(row_total, W, C)
        second_grad = kernel_grad(padded_one, grad_two, 2, row_total, W)
        back_one = input_grad(jnp.pad(grad_two, ((2, 2), (2, 2), (0, 0))), second_weight, 2, row_total, W)
        grad_one = jnp.where(pre_one > 0, back_one, 0.0).astype(jnp.bfloat16).reshape(row_total, W, C)
        first_grad = kernel_grad(padded, grad_one, 1, row_total, W)
        return (first_grad, second_grad, head_grad, loss_sum)
    first_all, second_all, head_all, loss_all = lax.map(strip, (features, labels, mean_map, spread_map))
    return (lax.optimization_barrier(jnp.sum(first_all, 0)), lax.optimization_barrier(jnp.sum(second_all, 0)), lax.optimization_barrier(jnp.sum(head_all, 0)), jnp.sum(loss_all) / (N_MEMBER * N_TILE * RD * W))
```

```python
import math

import jax
import jax.numpy as jnp
from jax import lax
from jax.experimental import pallas as pl
from jax.experimental.pallas import tpu as pltpu
from jax.sharding import PartitionSpec as P

F32 = jnp.float32
BF16 = jnp.bfloat16
I32 = jnp.int32
MESH = pl.DeviceIdType.MESH

CH = 256
NCLS = 64
NZ = 4
NT = 32
ROWS = 32
COLS = 64
CELLS = ROWS * COLS
NSEM = 200


def iota(shape, dim):
    return lax.broadcasted_iota(I32, shape, dim)


def onehot(mask):
    return jnp.where(mask, 1.0, 0.0).astype(BF16)


def mm(a, b):
    return jnp.dot(a, b, preferred_element_type=F32)


def mm_dims(a, b, ca, cb):
    return lax.dot_general(a, b, (((ca,), (cb,)), ((), ())), preferred_element_type=F32)


def kernel(
    tl, cov, feat, lab, w1h, w2h, wh,
    o1, o2, ohead, oloss,
    tv, xb, a1, a1e, a1o, a2, a2t, ag, gp, w1, w2, w2t,
    hf, gf, df, gat,
    rel_s, rel_r, fin_s, fin_l, fin_r, own, part, sec_s, sec_r,
    mp, sb, rb, mean_t,
    csb, crb, acc, s1b, r1, a1c, s2b, r2, x3,
    hx, lx,
    ssem, rsem, lsem,
):
    z = lax.axis_index("member")
    t = lax.axis_index("tile")
    core = lax.rem(t, 2)
    xc = lax.rem(lax.div(t, 2), 4)
    yc = lax.div(t, 8)
    coords = {"x": xc, "y": yc, "z": z, "c": core}

    def peer(axis, j):
        if axis == "z":
            return (j, t)
        if axis == "x":
            return (z, yc * 8 + j * 2 + core)
        if axis == "y":
            return (z, j * 8 + xc * 2 + core)
        return (z, yc * 8 + xc * 2 + j)

    used = [0]
    sent = []

    def remote(src, dst, dev):
        i = used[0]
        used[0] += 1
        copy = pltpu.make_async_remote_copy(
            src_ref=src, dst_ref=dst, send_sem=ssem.at[i], recv_sem=rsem.at[i],
            device_id=dev, device_id_type=MESH,
        )
        copy.start()
        sent.append(copy)
        return copy

    def ring(axis, o):
        return lax.rem(coords[axis] + o, 4)

    barrier = pltpu.get_barrier_semaphore()
    for o in range(1, NT):
        pl.semaphore_signal(barrier, inc=1, device_id=(z, lax.rem(t + o, NT)), device_id_type=MESH)
    for o in range(1, NZ):
        pl.semaphore_signal(barrier, inc=1, device_id=(lax.rem(z + o, NZ), t), device_id_type=MESH)

    zr, zl, zf = lax.rem(z + 1, NZ), lax.rem(z + 3, NZ), lax.rem(z + 2, NZ)
    loads = []
    for ci, g in enumerate((zf, zr, zl, z)):
        c = pltpu.make_async_copy(
            tl.at[:, pl.ds(pl.multiple_of(g * 32, 32), 32), :], tv.at[ci], lsem.at[ci]
        )
        c.start()
        loads.append(c)
    load_x = pltpu.make_async_copy(feat, xb.at[pl.ds(192, CELLS), :], lsem.at[4])
    load_w1 = pltpu.make_async_copy(w1h, w1, lsem.at[5])
    load_w2 = pltpu.make_async_copy(w2h, w2, lsem.at[6])
    load_x.start()
    load_w1.start()
    load_w2.start()

    group = onehot(lax.div(iota((256, 256), 0), 64) == lax.div(iota((256, 256), 1), 64))
    squash = onehot(lax.div(iota((256, 128), 0), 64) == iota((256, 128), 1))

    def cell_sum(v):
        hi = v.astype(BF16)
        lo = (v - hi.astype(F32)).astype(BF16)
        both = mm(jnp.concatenate([hi, lo], axis=0), squash)
        return both[:32] + both[32:]

    def soft(ci, half, put, sec):
        def step(k, sec):
            lane = pl.multiple_of(half * 2048 + k * 256, 256)
            x = tv[ci, :, :, pl.ds(lane, 256)].reshape(128, 256).astype(F32)
            e4 = jnp.exp2(x * (math.log2(math.e) / 4.0))
            r = e4 / mm(e4.astype(BF16), group)
            r2 = r * r
            e = (r2 * r2).astype(BF16)
            p = e.astype(F32) / mm(e, group)
            p = p.reshape(4, 32, 256)
            sq = p * p
            put(k, (p[0] + p[1]) + (p[2] + p[3]))
            q = (sq[0] + sq[1]) + (sq[2] + sq[3])
            return sec + pltpu.roll(cell_sum(q), half * 32 + 4 * k, 1)

        return lax.fori_loop(0, 8, step, sec)

    def at(k):
        return pl.ds(pl.multiple_of(k * 256, 256), 256)

    def put_to(ref, *lead):
        def put(k, v):
            ref[(*lead, slice(None), at(k))] = v.astype(ref.dtype)

        return put

    zero_sec = jnp.zeros((32, 128), F32)
    loads[0].wait()
    sec_f = soft(0, 0, put_to(rel_s, 0), zero_sec)
    pl.semaphore_wait(barrier, NT - 1 + NZ - 1)
    relay_a = remote(rel_s.at[0], rel_r.at[0], (zr, t))
    up, down = lax.rem(t + 1, NT), lax.rem(t + NT - 1, NT)
    halo_up = remote(feat.at[pl.ds(CELLS - 192, 192), :], xb.at[pl.ds(0, 192), :], (z, up))
    halo_dn = remote(feat.at[pl.ds(0, 192), :], xb.at[pl.ds(192 + CELLS, 192), :], (z, down))
    sec_f = soft(0, 1, put_to(rel_s, 1), sec_f)
    relay_b = remote(rel_s.at[1], rel_r.at[1], (zl, t))
    sec_s[0] = sec_f
    sec_c = [remote(sec_s.at[0], sec_r.at[0], (zf, t))]
    loads[1].wait()
    sec_1 = soft(1, 1, put_to(fin_s, 0, 1), zero_sec)
    f0 = remote(fin_s.at[0, 1], fin_l.at[1], (zr, t))
    loads[2].wait()
    sec_2 = soft(2, 0, put_to(fin_s, 1, 0), zero_sec)
    f1 = remote(fin_s.at[1, 0], fin_r.at[0], (zl, t))
    sec_1 = soft(1, 0, put_to(part), sec_1)
    sec_s[1] = sec_1
    sec_c.append(remote(sec_s.at[1], sec_r.at[1], (zr, t)))

    def add_relay(side, half):
        def step(k, carry):
            fin_s[side, half, :, at(k)] = (
                part[:, at(k)] + rel_r[half, :, at(k)].astype(F32)
            ).astype(BF16)
            return carry

        lax.fori_loop(0, 8, step, 0)

    relay_a.wait_recv()
    add_relay(0, 0)
    f2 = remote(fin_s.at[0, 0], fin_l.at[0], (zr, t))
    sec_2 = soft(2, 1, put_to(part), sec_2)
    sec_s[2] = sec_2
    sec_c.append(remote(sec_s.at[2], sec_r.at[2], (zl, t)))
    relay_b.wait_recv()
    add_relay(1, 1)
    f3 = remote(fin_s.at[1, 1], fin_r.at[1], (zl, t))
    loads[3].wait()
    sec_m = soft(3, 0, put_to(own, 0), zero_sec)
    sec_m = soft(3, 1, put_to(own, 1), sec_m)

    def shifted(v, by, lo_col, hi_col, rows):
        col = lax.rem(iota((rows, CH), 0), COLS)
        before = jnp.where(col >= by, pltpu.roll(v, by, 0), 0.0)
        after = jnp.where(col < COLS - by, pltpu.roll(v, rows - by, 0), 0.0)
        return before.astype(BF16), after.astype(BF16)

    load_x.wait()
    load_w1.wait()
    halo_up.wait_recv()
    halo_dn.wait_recv()

    def build_one(k, carry):
        s = pl.ds(pl.multiple_of(k * 128, 128), 128)
        row = t * ROWS - 3 + 2 * k + lax.div(iota((128, CH), 0), COLS)
        v = xb[s, :].astype(F32)
        v = jnp.where((row >= 0) & (row < NT * ROWS), v, 0.0)
        before, after = shifted(v, 1, 0, 0, 128)
        a1[s, 0:CH] = before
        a1[s, CH:2 * CH] = v.astype(BF16)
        a1[s, 2 * CH:3 * CH] = after
        return carry

    lax.fori_loop(0, 19, build_one, 0)

    def conv_rows(a_ref, w_ref, start, rows, stride):
        total = None
        for a in range(3):
            s = pl.ds(pl.multiple_of(start + a * stride, 64), rows)
            d = mm(a_ref[s, :], w_ref[a])
            total = d if total is None else total + d
        return total

    def conv_one(k, carry):
        n = 256
        start = k * n
        pre = conv_rows(a1, w1, start, n, COLS)
        row = t * ROWS - 2 + 4 * k + lax.div(iota((n, CH), 0), COLS)
        h = jnp.where((row >= 0) & (row < NT * ROWS) & (pre > 0), pre, 0.0)
        h = h.astype(BF16).astype(F32)
        before, after = shifted(h, 2, 0, 0, n)
        s = pl.ds(pl.multiple_of(start, n), n)
        a2[s, 0:CH] = before
        a2[s, CH:2 * CH] = h.astype(BF16)
        a2[s, 2 * CH:3 * CH] = after
        return carry

    lax.fori_loop(0, 9, conv_one, 0)

    for c in (f0, f1, f2, f3, *sec_c):
        c.wait_recv()

    msq = zero_sec
    for half in range(2):
        def mean_step(k, msq, half=half):
            for sub in range(2):
                s = pl.ds(pl.multiple_of(k * 512 + sub * 256, 256), 256)
                m = (
                    own[half, :, s] + fin_l[half, :, s].astype(F32) + fin_r[half, :, s].astype(F32)
                ) * (1.0 / 16.0)
                mp[pl.ds(pl.multiple_of((half * 4 + k) * 32, 32), 32), sub * 256:(sub + 1) * 256] = (
                    m.astype(BF16)
                )
                msq = msq + pltpu.roll(cell_sum(m * m), half * 32 + 8 * k + 4 * sub, 1)
            return msq

        msq = lax.fori_loop(0, 4, mean_step, msq)
    second = (sec_m + sec_r[0]) + (sec_r[1] + sec_r[2])
    spread = second * (1.0 / 16.0) - msq
    lane = iota((32, 128), 1)
    slot_no = (iota((32, 128), 0) + 1).astype(F32)
    for a in range(8):
        sp = spread if a == 0 else pltpu.roll(spread, 128 - 8 * a, 1)
        sp = jnp.where(lane < 8, sp, 0.0)
        hi = sp.astype(BF16).astype(F32)
        mid = (sp - hi).astype(BF16).astype(F32)
        lo = sp - hi - mid
        ext = hi + pltpu.roll(mid, 8, 1) + pltpu.roll(lo, 16, 1)
        ext = jnp.where(lane == 24, slot_no, ext)
        mp[a * 32:(a + 1) * 32, 512:640] = ext.astype(BF16)

    crow = cov[...]
    i0, i1 = iota((128, 128), 0), iota((128, 128), 1)
    ccol = jnp.sum(jnp.where(i0 == i1, crow, 0), axis=1, keepdims=True)
    same = (ccol == crow) & (lax.div(i0, 32) == lax.div(i1, 32)) & (i0 < i1)
    rank = jnp.sum(jnp.where(same, 1, 0), axis=0, keepdims=True)
    slot = jnp.broadcast_to(crow * 2 + rank, (8, 128)).astype(F32)
    lane8 = iota((8, 128), 1)
    mine = jnp.zeros((8, 128), F32)
    for g in range(NZ):
        moved = slot if g == 0 else pltpu.roll(slot, 128 - 32 * g, 1)
        mine = jnp.where(z == g, moved, mine)
    mine = jnp.where(lane8 < 32, mine, 0.0)
    mine = mine + pltpu.roll(mine, 32, 1)
    mine = mine + pltpu.roll(mine, 64, 1)
    slots = jnp.concatenate([mine, mine], axis=1)[0:1, :]
    j0, j1 = iota((512, 256), 0), iota((512, 256), 1)
    pick = onehot(
        (lax.div(j0, 8).astype(F32) == slots) & (lax.rem(j0, 8) == lax.div(j1, 32))
    )
    sb[...] = mm(pick, mp[...]).astype(BF16).reshape(NT, 16, 640)
    exch = []
    for o in range(1, NT):
        d = lax.rem(t + o, NT)
        exch.append(remote(sb.at[d], rb.at[t], (z, d)))
    rb[t] = sb[t]

    load_w2.wait()

    def conv_two(k, carry):
        n = 256
        pre = conv_rows(a2, w2, k * n, n, 2 * COLS)
        h = jnp.where(pre > 0, pre, 0.0)
        s = pl.ds(pl.multiple_of(k * n, n), n)
        hf[0, s, :] = h[:, :128]
        hf[1, s, :] = h[:, 128:]
        return carry

    lax.fori_loop(0, 8, conv_two, 0)

    def transpose_two(k, carry):
        s = pl.ds(pl.multiple_of(k * 128, 128), 128)
        a2t[:, s] = a2[s, :].T
        a1e[:, s] = a1[pl.ds(pl.multiple_of(128 + k * 128, 128), 128), :].T
        return carry

    lax.fori_loop(0, 18, transpose_two, 0)

    def transpose_odd(k, carry):
        s = pl.ds(pl.multiple_of(k * 128, 128), 128)
        a1o[:, s] = a1[pl.ds(pl.multiple_of(192 + k * 128, 64), 128), :].T
        return carry

    lax.fori_loop(0, 16, transpose_odd, 0)
    for a in range(3):
        for b in range(3):
            w2t[a, b * CH:(b + 1) * CH, :] = w2[a, (2 - b) * CH:(3 - b) * CH, :].T

    l_rep = onehot(lax.div(iota((256, 32), 0), 8) == iota((256, 32), 1))
    rep = mm(l_rep, lab[...].astype(F32).astype(BF16))
    rep = jnp.where(
        lax.div(iota((256, 64), 1), 8) == lax.rem(iota((256, 64), 0), 8), rep, 0.0
    ).astype(BF16)
    l_sel = onehot(lax.rem(iota((8, 64), 1), 8) == iota((8, 64), 0))
    labels = mm_dims(l_sel, rep, 1, 1)

    for c in exch:
        c.wait_recv()
    got = rb[...].reshape(512, 640)
    from_slot = got[:, 512:640].astype(F32)[:, 24:25]
    n0, n1 = iota((512, 256), 0), iota((512, 256), 1)
    tile_no = (lax.div(n1, 64) * 8 + lax.rem(n1, 8) + 1).astype(F32)
    place = onehot((from_slot == tile_no) & (lax.rem(n0, 8) == lax.rem(lax.div(n1, 8), 8)))
    mean_t[...] = mm_dims(got, place, 0, 0)

    scale = 1.0 / math.sqrt(NZ * NT * CELLS)
    head_w = wh[...]
    classes = iota((NCLS, 256), 0)
    loss = jnp.zeros((1, 256), F32)
    head_t = jnp.zeros((NCLS, CH), F32)
    for b in range(8):
        s = pl.ds(b, 256, stride=8)
        h32 = jnp.concatenate([hf[0, s, :], hf[1, s, :]], axis=1)
        hb = h32.astype(BF16)
        logits = mm_dims(head_w, hb, 0, 1)
        top = jnp.max(logits, axis=0, keepdims=True)
        low = logits - top
        log_s = low - jnp.log(jnp.sum(jnp.exp(low), axis=0, keepdims=True))
        prob = jnp.exp(log_s)
        mean = mean_t[b * 64:(b + 1) * 64, :]
        spr = mean_t[512 + b:513 + b, :] + mean_t[520 + b:521 + b, :] + mean_t[528 + b:529 + b, :]
        wgt = 1.0 / (0.1 + spr)
        hot = classes.astype(F32) == labels[b:b + 1, :]
        ent = jnp.where(mean > 0, mean * jnp.log(jnp.where(mean > 0, mean, 1.0)), 0.0)
        kl = jnp.sum(ent - mean * log_s, axis=0, keepdims=True)
        nll = jnp.sum(jnp.where(hot, log_s, 0.0), axis=0, keepdims=True)
        loss = loss + (wgt * kl - nll)
        lg = ((wgt * (prob - mean) + prob - jnp.where(hot, 1.0, 0.0)) * scale).astype(BF16)
        head_t = head_t + mm(lg, hb)
        hg = mm_dims(lg, head_w, 0, 1)
        g2 = jnp.where(h32 > 0, hg, 0.0)
        gf[0, s, :] = g2[:, :128]
        gf[1, s, :] = g2[:, 128:]

    def round_grad(k, carry):
        s = pl.ds(pl.multiple_of(k * 128, 128), 128)
        d = pl.ds(pl.multiple_of(128 + k * 128, 128), 128)
        gp[d, 0:128] = gf[0, s, :].astype(BF16)
        gp[d, 128:256] = gf[1, s, :].astype(BF16)
        return carry

    lax.fori_loop(0, 16, round_grad, 0)
    gh_up = remote(gp.at[pl.ds(CELLS, 128), :], gp.at[pl.ds(0, 128), :], (z, up))
    gh_dn = remote(gp.at[pl.ds(128, 128), :], gp.at[pl.ds(128 + CELLS, 128), :], (z, down))

    small = {"head": jnp.concatenate([head_t[:, :128], head_t[:, 128:]], axis=0),
             "loss": jnp.broadcast_to(jnp.sum(loss, axis=1, keepdims=True), (8, 128))}

    def small_send(n, axis):
        me = coords[axis]
        hx[n, me] = small["head"].astype(BF16)
        lx[n, me] = small["loss"]
        size = 2 if axis == "c" else 4
        small["wait"] = []
        for o in range(1, size):
            dev = peer(axis, lax.rem(me + o, size))
            small["wait"].append(remote(hx.at[n, me], hx.at[n, me], dev))
            small["wait"].append(remote(lx.at[n, me], lx.at[n, me], dev))

    def small_recv(n, axis):
        for c in small["wait"]:
            c.wait_recv()
        size = 2 if axis == "c" else 4
        h, l = hx[n, 0].astype(F32), lx[n, 0]
        for j in range(1, size):
            h = h + hx[n, j].astype(F32)
            l = l + lx[n, j]
        small["head"], small["loss"] = h, l

    orders = (("x", "y", "z"), ("y", "z", "x"), ("z", "x", "y"))

    class Session:
        def __init__(self, n):
            self.n = n
            self.wait = []

        def done(self):
            for c in self.wait:
                c.wait_recv()
            self.wait = []

        def base(self, p):
            return 768 * p + 192 * coords[orders[p][0]]

        def c_send(self):
            n = self.n
            other = 1 - core

            def step(k, carry):
                s = pl.ds(pl.multiple_of(k * 256, 256), 256)
                csb[n, s, :] = df[n, other, s, :].astype(BF16)
                return carry

            lax.fori_loop(0, 9, step, 0)
            self.wait.append(remote(csb.at[n], crb.at[n], peer("c", other)))

        def s1(self):
            self.done()
            n = self.n

            def step(k, carry):
                s = pl.ds(pl.multiple_of(k * 256, 256), 256)
                v = df[n, core, s, :] + crb[n, s, :].astype(F32)
                acc[n, s, :] = v
                s1b[n, s, :] = v.astype(BF16)
                return carry

            lax.fori_loop(0, 9, step, 0)
            for o in (2, 1, 3):
                for p in range(3):
                    ax = orders[p][0]
                    j = ring(ax, o)
                    src = s1b.at[n, pl.ds(pl.multiple_of(768 * p + 192 * j, 64), 192), :]
                    self.wait.append(remote(src, r1.at[n, p, o], peer(ax, j)))

        def s2(self):
            self.done()
            n = self.n
            for p in range(3):
                s = pl.ds(pl.multiple_of(self.base(p), 64), 192)
                v = acc[n, s, :]
                for o in range(1, 4):
                    v = v + r1[n, p, o].astype(F32)
                a1c[n, p] = v
                s2b[n, p] = v.astype(BF16)
            for o in (2, 1, 3):
                for p in range(3):
                    ax = orders[p][1]
                    j = ring(ax, o)
                    src = s2b.at[n, p, pl.ds(pl.multiple_of(48 * j, 16), 48), :]
                    self.wait.append(remote(src, r2.at[n, p, o], peer(ax, j)))

        def s3(self):
            self.done()
            n = self.n
            for p in range(3):
                s = pl.ds(pl.multiple_of(48 * coords[orders[p][1]], 16), 48)
                v = a1c[n, p, s, :]
                for o in range(1, 4):
                    v = v + r2[n, p, o].astype(F32)
                x3[n, p, coords[orders[p][2]]] = v.astype(BF16)
            for o in (2, 1, 3):
                for p in range(3):
                    ax = orders[p][2]
                    ref = x3.at[n, p, coords[ax]]
                    self.wait.append(remote(ref, ref, peer(ax, ring(ax, o))))

        def g2(self):
            self.done()
            n = self.n
            for p in range(3):
                v = x3[n, p, 0].astype(F32)
                for j in range(1, 4):
                    v = v + x3[n, p, j].astype(F32)
                s = pl.ds(pl.multiple_of(self.base(p) + 48 * coords[orders[p][1]], 16), 48)
                gat[n, core, s, :] = v.astype(BF16)
            for o in (2, 1, 3):
                for p in range(3):
                    ax = orders[p][1]
                    s = pl.ds(pl.multiple_of(self.base(p) + 48 * coords[ax], 16), 48)
                    ref = gat.at[n, core, s, :]
                    self.wait.append(remote(ref, ref, peer(ax, ring(ax, o))))

        def g1(self):
            self.done()
            n = self.n
            for o in (2, 1, 3):
                for p in range(3):
                    ax = orders[p][0]
                    ref = gat.at[n, core, pl.ds(pl.multiple_of(self.base(p), 64), 192), :]
                    self.wait.append(remote(ref, ref, peer(ax, ring(ax, o))))

        def gc(self):
            self.done()
            ref = gat.at[self.n, core]
            self.wait.append(remote(ref, ref, peer("c", 1 - core)))

    second_s, first_s = Session(0), Session(1)

    def kernel_grad(n, a, lhs, rhs):
        d = mm(lhs, rhs)
        df[n, 0, 768 * a:768 * (a + 1), :] = d[:, :128]
        df[n, 1, 768 * a:768 * (a + 1), :] = d[:, 128:]

    small_send(0, "c")
    grad_two = gp[128:128 + CELLS, :]
    for a in range(3):
        kernel_grad(0, a, a2t[:, 128 * a:128 * a + CELLS], grad_two)
    second_s.c_send()
    small_recv(0, "c")
    small_send(1, "x")

    gh_up.wait_recv()
    gh_dn.wait_recv()

    def build_grad(k, carry):
        s = pl.ds(pl.multiple_of(k * 128, 128), 128)
        row = t * ROWS - 2 + 2 * k + lax.div(iota((128, CH), 0), COLS)
        v = jnp.where((row >= 0) & (row < NT * ROWS), gp[s, :].astype(F32), 0.0)
        before, after = shifted(v, 2, 0, 0, 128)
        ag[s, 0:CH] = before
        ag[s, CH:2 * CH] = v.astype(BF16)
        ag[s, 2 * CH:3 * CH] = after
        return carry

    lax.fori_loop(0, 18, build_grad, 0)
    second_s.s1()
    small_recv(1, "x")
    small_send(2, "y")

    def back(k, carry):
        n = 256
        total = None
        for a in range(3):
            s = pl.ds(pl.multiple_of(k * n + (2 - a) * 2 * COLS, 128), n)
            d = mm(ag[s, :], w2t[a])
            total = d if total is None else total + d
        h = a2[pl.ds(pl.multiple_of(128 + k * n, 128), n), CH:2 * CH].astype(F32)
        v = jnp.where(h > 0, total, 0.0).astype(BF16)
        xb[pl.ds(pl.multiple_of(k * n, n), n), :] = v
        return carry

    lax.fori_loop(0, 8, back, 0)
    second_s.s2()
    small_recv(2, "y")
    small_send(3, "z")
    grad_one = xb[0:CELLS, :]
    kernel_grad(1, 0, a1e[:, 0:CELLS], grad_one)
    second_s.s3()
    small_recv(3, "z")
    kernel_grad(1, 1, a1o[...], grad_one)
    kernel_grad(1, 2, a1e[:, 128:128 + CELLS], grad_one)
    first_s.c_send()
    second_s.g2()
    first_s.s1()
    second_s.g1()
    first_s.s2()
    second_s.gc()
    first_s.s3()
    second_s.done()
    outs = []
    for h in range(2):
        c = pltpu.make_async_copy(gat.at[0, h], o2.at[:, pl.ds(128 * h, 128)], lsem.at[7 + h])
        c.start()
        outs.append(c)
    ohead[...] = small["head"]
    oloss[...] = small["loss"]
    first_s.g2()
    first_s.g1()
    first_s.gc()
    first_s.done()
    for h in range(2):
        c = pltpu.make_async_copy(gat.at[1, h], o1.at[:, pl.ds(128 * h, 128)], lsem.at[9 + h])
        c.start()
        outs.append(c)
    for c in sent:
        c.wait_send()
    for c in outs:
        c.wait()


def body(teacher_logits, coverage, features, labels, first_weight, second_weight, head_weight):
    any_spec = pl.BlockSpec(memory_space=pl.ANY)
    vmem = pl.BlockSpec(memory_space=pltpu.VMEM)
    out = [
        jax.ShapeDtypeStruct((2304, 256), BF16),
        jax.ShapeDtypeStruct((2304, 256), BF16),
        jax.ShapeDtypeStruct((128, 128), F32),
        jax.ShapeDtypeStruct((8, 128), F32),
    ]
    V = pltpu.VMEM
    scratch = [
        V((4, 4, 32, 4096), BF16),
        V((2432, CH), BF16),
        V((2432, 3 * CH), BF16),
        V((3 * CH, 2304), BF16),
        V((3 * CH, 2048), BF16),
        V((2304, 3 * CH), BF16),
        V((3 * CH, 2304), BF16),
        V((2304, 3 * CH), BF16),
        V((2304, CH), BF16),
        V((3, 3 * CH, CH), BF16),
        V((3, 3 * CH, CH), BF16),
        V((3, 3 * CH, CH), BF16),
        V((2, CELLS, 128), F32),
        V((2, CELLS, 128), F32),
        V((2, 2, 2304, 128), F32),
        V((2, 2, 2304, 128), BF16),
        V((2, 32, 2048), BF16),
        V((2, 32, 2048), BF16),
        V((2, 2, 32, 2048), BF16),
        V((2, 32, 2048), BF16),
        V((2, 32, 2048), BF16),
        V((2, 32, 2048), F32),
        V((32, 2048), F32),
        V((3, 32, 128), F32),
        V((3, 32, 128), F32),
        V((256, 640), BF16),
        V((NT, 16, 640), BF16),
        V((NT, 16, 640), BF16),
        V((640, 256), F32),
        V((2, 2304, 128), BF16),
        V((2, 2304, 128), BF16),
        V((2, 2304, 128), F32),
        V((2, 2304, 128), BF16),
        V((2, 3, 4, 192, 128), BF16),
        V((2, 3, 192, 128), F32),
        V((2, 3, 192, 128), BF16),
        V((2, 3, 4, 48, 128), BF16),
        V((2, 3, 4, 48, 128), BF16),
        V((4, 4, 128, 128), BF16),
        V((4, 4, 8, 128), F32),
        pltpu.SemaphoreType.DMA((NSEM,)),
        pltpu.SemaphoreType.DMA((NSEM,)),
        pltpu.SemaphoreType.DMA((11,)),
    ]
    first, second, head, loss = pl.pallas_call(
        kernel,
        out_shape=out,
        in_specs=[any_spec, vmem, any_spec, vmem, any_spec, any_spec, vmem],
        out_specs=[any_spec, any_spec, vmem, vmem],
        scratch_shapes=scratch,
        compiler_params=pltpu.CompilerParams(
            collective_id=0, has_side_effects=True, vmem_limit_bytes=67043328
        ),
    )(
        teacher_logits,
        coverage.reshape(1, 128),
        features.reshape(CELLS, CH),
        labels.reshape(ROWS, COLS),
        first_weight.reshape(3, 3 * CH, CH),
        second_weight.reshape(3, 3 * CH, CH),
        head_weight,
    )
    first = first.astype(F32).reshape(3, 3, CH, CH)
    second = second.astype(F32).reshape(3, 3, CH, CH)
    head = jnp.concatenate([head[:64].T, head[64:].T], axis=0)
    return first, second, head, loss[0, 0] / (NZ * NT * CELLS)


def solution(mesh):
    return jax.shard_map(
        body,
        mesh=mesh,
        in_specs=(
            P("member", "tile", None),
            P("tile"),
            P("member", "tile", None, None),
            P("member", "tile", None),
            P(),
            P(),
            P(),
        ),
        out_specs=(P(), P(), P(), P()),
        check_vma=False,
    )
```

```python
import math

import jax
import jax.numpy as jnp
from jax import lax
from jax.experimental import pallas as pl
from jax.experimental.pallas import tpu as pltpu
from jax.sharding import PartitionSpec as P

F32 = jnp.float32
BF16 = jnp.bfloat16
I32 = jnp.int32
MESH = pl.DeviceIdType.MESH

CH = 256
NCLS = 64
NZ = 4
NT = 32
ROWS = 32
COLS = 64
CELLS = ROWS * COLS
NSEM = 300
PIECES = (2304, 768, 768, 768)


def iota(shape, dim):
    return lax.broadcasted_iota(I32, shape, dim)


def onehot(mask):
    return jnp.where(mask, 1.0, 0.0).astype(BF16)


def mm(a, b):
    return jnp.dot(a, b, preferred_element_type=F32)


def mm_dims(a, b, ca, cb):
    return lax.dot_general(a, b, (((ca,), (cb,)), ((), ())), preferred_element_type=F32)


def kernel(
    tl, cov, feat, lab, w1h, w2h, wh,
    o1, o2, ohead, oloss,
    tv, xb, a1, a1e, a1o, a2, a2t, ag, gp, w1, w2, w2t, hf, gf, gat,
    rel_s, rel_r, fin_s, fin_l, fin_r, own, part, sec_s, sec_r,
    mp, sb, rb, mean_t, hx, lx, wb, wq, pick_s,
    ssem, rsem, lsem, *piece_refs,
):
    z = lax.axis_index("member")
    t = lax.axis_index("tile")
    core = lax.rem(t, 2)
    xc = lax.rem(lax.div(t, 2), 4)
    yc = lax.div(t, 8)
    coords = {"x": xc, "y": yc, "z": z, "c": core}

    def peer(axis, j):
        if axis == "z":
            return (j, t)
        if axis == "x":
            return (z, yc * 8 + j * 2 + core)
        if axis == "y":
            return (z, j * 8 + xc * 2 + core)
        return (z, yc * 8 + xc * 2 + j)

    used = [0]
    sent = []

    def remote(src, dst, dev):
        i = used[0]
        used[0] += 1
        copy = pltpu.make_async_remote_copy(
            src_ref=src, dst_ref=dst, send_sem=ssem.at[i], recv_sem=rsem.at[i],
            device_id=dev, device_id_type=MESH,
        )
        copy.start()
        sent.append(copy)
        return copy

    def ring(axis, o):
        return lax.rem(coords[axis] + o, 4)

    barrier = pltpu.get_barrier_semaphore()
    for o in range(1, NT):
        pl.semaphore_signal(barrier, inc=1, device_id=(z, lax.rem(t + o, NT)), device_id_type=MESH)
    for o in range(1, NZ):
        pl.semaphore_signal(barrier, inc=1, device_id=(lax.rem(z + o, NZ), t), device_id_type=MESH)

    zr, zl, zf = lax.rem(z + 1, NZ), lax.rem(z + 3, NZ), lax.rem(z + 2, NZ)
    loads = []
    for ci, g in enumerate((zf, zr, zl, z)):
        c = pltpu.make_async_copy(
            tl.at[:, pl.ds(pl.multiple_of(g * 32, 32), 32), :], tv.at[ci], lsem.at[ci]
        )
        c.start()
        loads.append(c)
    load_x = pltpu.make_async_copy(feat, xb.at[pl.ds(192, CELLS), :], lsem.at[4])
    load_w1 = pltpu.make_async_copy(w1h, w1, lsem.at[5])
    load_w2 = pltpu.make_async_copy(w2h, w2, lsem.at[6])
    load_x.start()
    load_w1.start()
    load_w2.start()

    wb[...] = onehot(lax.div(iota((256, 256), 0), 64) == lax.div(iota((256, 256), 1), 64))
    wq[...] = onehot(lax.div(iota((256, 128), 0), 64) == iota((256, 128), 1))

    def cell_sums(v, half, total):
        hi = v.astype(BF16)
        lo = (v - hi.astype(F32)).astype(BF16)
        both = mm(jnp.concatenate([hi, lo], axis=0), wq[...])
        for j in range(8):
            s = both[32 * j:32 * (j + 1)] + both[256 + 32 * j:288 + 32 * j]
            shift = half * 32 + 4 * j
            total = total + (pltpu.roll(s, shift, 1) if shift else s)
        return total

    def soft(ci, half, put, sec):
        x = jnp.concatenate(
            [
                tv[ci, :, :, half * 2048 + 256 * j:half * 2048 + 256 * (j + 1)].reshape(128, 256)
                for j in range(8)
            ],
            axis=0,
        ).astype(F32)
        e4 = jnp.exp2(x * (math.log2(math.e) / 4.0))
        r = e4 / mm(e4.astype(BF16), wb[...])
        r2 = r * r
        e = (r2 * r2).astype(BF16)
        p = e.astype(F32) / mm(e, wb[...])
        p = p.reshape(8, 4, 32, 256)
        sq = p * p
        f = (p[:, 0] + p[:, 1]) + (p[:, 2] + p[:, 3])
        q = (sq[:, 0] + sq[:, 1]) + (sq[:, 2] + sq[:, 3])
        for j in range(8):
            put(j, f[j])
        return cell_sums(q.reshape(256, 256), half, sec)

    def put_to(ref, *lead):
        def put(j, v):
            ref[(*lead, slice(None), slice(256 * j, 256 * (j + 1)))] = v.astype(ref.dtype)

        return put

    zero_sec = jnp.zeros((32, 128), F32)
    loads[0].wait()
    sec_f = soft(0, 0, put_to(rel_s, 0), zero_sec)
    pl.semaphore_wait(barrier, NT - 1 + NZ - 1)
    relay_a = remote(rel_s.at[0], rel_r.at[0], (zr, t))
    up, down = lax.rem(t + 1, NT), lax.rem(t + NT - 1, NT)
    halo_up = remote(feat.at[pl.ds(CELLS - 192, 192), :], xb.at[pl.ds(0, 192), :], (z, up))
    halo_dn = remote(feat.at[pl.ds(0, 192), :], xb.at[pl.ds(192 + CELLS, 192), :], (z, down))
    sec_f = soft(0, 1, put_to(rel_s, 1), sec_f)
    relay_b = remote(rel_s.at[1], rel_r.at[1], (zl, t))
    loads[1].wait()
    sec_1 = soft(1, 1, put_to(fin_s, 0, 1), zero_sec)
    f0 = remote(fin_s.at[0, 1], fin_l.at[1], (zr, t))
    loads[2].wait()
    sec_2 = soft(2, 0, put_to(fin_s, 1, 0), zero_sec)
    f1 = remote(fin_s.at[1, 0], fin_r.at[0], (zl, t))
    sec_1 = soft(1, 0, put_to(part, 0), sec_1)
    sec_2 = soft(2, 1, put_to(part, 1), sec_2)

    def add_relay(side, half):
        fin_s[side, half] = (part[side] + rel_r[half].astype(F32)).astype(BF16)

    relay_a.wait_recv()
    add_relay(0, 0)
    f2 = remote(fin_s.at[0, 0], fin_l.at[0], (zr, t))
    relay_b.wait_recv()
    add_relay(1, 1)
    f3 = remote(fin_s.at[1, 1], fin_r.at[1], (zl, t))
    sec_c = []
    for i, (value, to) in enumerate(((sec_f, zf), (sec_1, zr), (sec_2, zl))):
        sec_s[i] = value
        sec_c.append(remote(sec_s.at[i], sec_r.at[i], (to, t)))
    loads[3].wait()
    sec_m = soft(3, 0, put_to(own, 0), zero_sec)
    sec_m = soft(3, 1, put_to(own, 1), sec_m)

    crow = cov[...]
    i0, i1 = iota((128, 128), 0), iota((128, 128), 1)
    ccol = jnp.sum(jnp.where(i0 == i1, crow, 0), axis=1, keepdims=True)
    same = (ccol == crow) & (lax.div(i0, 32) == lax.div(i1, 32)) & (i0 < i1)
    rank = jnp.sum(jnp.where(same, 1, 0), axis=0, keepdims=True)
    slot = jnp.broadcast_to(crow * 2 + rank, (8, 128)).astype(F32)
    lane8 = iota((8, 128), 1)
    mine = jnp.zeros((8, 128), F32)
    for g in range(NZ):
        moved = slot if g == 0 else pltpu.roll(slot, 128 - 32 * g, 1)
        mine = jnp.where(z == g, moved, mine)
    mine = jnp.where(lane8 < 32, mine, 0.0)
    mine = mine + pltpu.roll(mine, 32, 1)
    mine = mine + pltpu.roll(mine, 64, 1)
    slots = jnp.concatenate([mine, mine], axis=1)[0:1, :]
    j0, j1 = iota((512, 256), 0), iota((512, 256), 1)
    pick_s[...] = onehot(
        (lax.div(j0, 8).astype(F32) == slots) & (lax.rem(j0, 8) == lax.div(j1, 32))
    )

    def shifted(v, by, lo_col, hi_col, rows):
        col = lax.rem(iota((rows, CH), 0), COLS)
        before = jnp.where(col >= by, pltpu.roll(v, by, 0), 0.0)
        after = jnp.where(col < COLS - by, pltpu.roll(v, rows - by, 0), 0.0)
        return before.astype(BF16), after.astype(BF16)

    load_x.wait()
    load_w1.wait()
    halo_up.wait_recv()
    halo_dn.wait_recv()

    def build_one(k, carry):
        s = pl.ds(pl.multiple_of(k * 128, 128), 128)
        row = t * ROWS - 3 + 2 * k + lax.div(iota((128, CH), 0), COLS)
        v = xb[s, :].astype(F32)
        v = jnp.where((row >= 0) & (row < NT * ROWS), v, 0.0)
        before, after = shifted(v, 1, 0, 0, 128)
        a1[s, 0:CH] = before
        a1[s, CH:2 * CH] = v.astype(BF16)
        a1[s, 2 * CH:3 * CH] = after
        return carry

    lax.fori_loop(0, 19, build_one, 0)

    def conv_rows(a_ref, w_ref, start, rows, stride):
        total = None
        for a in range(3):
            s = pl.ds(pl.multiple_of(start + a * stride, 64), rows)
            d = mm(a_ref[s, :], w_ref[a])
            total = d if total is None else total + d
        return total

    def conv_one(k, carry):
        n = 256
        start = k * n
        pre = conv_rows(a1, w1, start, n, COLS)
        row = t * ROWS - 2 + 4 * k + lax.div(iota((n, CH), 0), COLS)
        h = jnp.where((row >= 0) & (row < NT * ROWS) & (pre > 0), pre, 0.0)
        h = h.astype(BF16).astype(F32)
        before, after = shifted(h, 2, 0, 0, n)
        s = pl.ds(pl.multiple_of(start, n), n)
        a2[s, 0:CH] = before
        a2[s, CH:2 * CH] = h.astype(BF16)
        a2[s, 2 * CH:3 * CH] = after
        a1e[:, s] = a1[pl.ds(pl.multiple_of(128 + start, 128), n), :].T
        odd = jnp.minimum(k, 7) * n
        a1o[:, pl.ds(pl.multiple_of(odd, n), n)] = a1[pl.ds(pl.multiple_of(192 + odd, 64), n), :].T
        return carry

    lax.fori_loop(0, 9, conv_one, 0)

    for c in (f0, f1, f2, f3, *sec_c):
        c.wait_recv()

    msq = zero_sec
    for half in range(2):
        m = (
            own[half] + fin_l[half].astype(F32) + fin_r[half].astype(F32)
        ) * (1.0 / 16.0)
        squares = []
        for j in range(8):
            mj = m[:, 256 * j:256 * (j + 1)]
            row = (half * 4 + j // 2) * 32
            mp[row:row + 32, (j % 2) * 256:(j % 2 + 1) * 256] = mj.astype(BF16)
            squares.append(mj * mj)
        msq = cell_sums(jnp.concatenate(squares, axis=0), half, msq)
    second = (sec_m + sec_r[0]) + (sec_r[1] + sec_r[2])
    spread = second * (1.0 / 16.0) - msq
    lane = iota((32, 128), 1)
    slot_no = (iota((32, 128), 0) + 1).astype(F32)
    for a in range(8):
        sp = spread if a == 0 else pltpu.roll(spread, 128 - 8 * a, 1)
        sp = jnp.where(lane < 8, sp, 0.0)
        hi = sp.astype(BF16).astype(F32)
        mid = (sp - hi).astype(BF16).astype(F32)
        lo = sp - hi - mid
        ext = hi + pltpu.roll(mid, 8, 1) + pltpu.roll(lo, 16, 1)
        ext = jnp.where(lane == 24, slot_no, ext)
        mp[a * 32:(a + 1) * 32, 512:640] = ext.astype(BF16)

    sb[...] = mm(pick_s[...], mp[...]).astype(BF16).reshape(NT, 16, 640)
    exch = []
    for o in range(1, NT):
        d = lax.rem(t + o, NT)
        exch.append(remote(sb.at[d], rb.at[t], (z, d)))
    rb[t] = sb[t]

    load_w2.wait()

    def conv_two(k, carry):
        n = 256
        pre = conv_rows(a2, w2, k * n, n, 2 * COLS)
        h = jnp.where(pre > 0, pre, 0.0)
        s = pl.ds(pl.multiple_of(k * n, n), n)
        hf[0, s, :] = h[:, :128]
        hf[1, s, :] = h[:, 128:]
        a2t[:, s] = a2[s, :].T
        return carry

    lax.fori_loop(0, 8, conv_two, 0)
    a2t[:, CELLS:CELLS + 256] = a2[CELLS:CELLS + 256, :].T

    for a in range(3):
        for b in range(3):
            w2t[a, b * CH:(b + 1) * CH, :] = w2[a, (2 - b) * CH:(3 - b) * CH, :].T

    l_rep = onehot(lax.div(iota((256, 32), 0), 8) == iota((256, 32), 1))
    rep = mm(l_rep, lab[...].astype(F32).astype(BF16))
    rep = jnp.where(
        lax.div(iota((256, 64), 1), 8) == lax.rem(iota((256, 64), 0), 8), rep, 0.0
    ).astype(BF16)
    l_sel = onehot(lax.rem(iota((8, 64), 1), 8) == iota((8, 64), 0))
    labels = mm_dims(l_sel, rep, 1, 1)

    for c in exch:
        c.wait_recv()
    got = rb[...].reshape(512, 640)
    from_slot = got[:, 512:640].astype(F32)[:, 24:25]
    n0, n1 = iota((512, 256), 0), iota((512, 256), 1)
    tile_no = (lax.div(n1, 64) * 8 + lax.rem(n1, 8) + 1).astype(F32)
    place = onehot((from_slot == tile_no) & (lax.rem(n0, 8) == lax.rem(lax.div(n1, 8), 8)))
    mean_t[...] = mm_dims(got, place, 0, 0)

    scale = 1.0 / math.sqrt(NZ * NT * CELLS)
    head_w = wh[...]
    classes = iota((NCLS, 256), 0)
    loss = jnp.zeros((1, 256), F32)
    head_t = jnp.zeros((NCLS, CH), F32)
    for b in range(8):
        s = pl.ds(b, 256, stride=8)
        h32 = jnp.concatenate([hf[0, s, :], hf[1, s, :]], axis=1)
        hb = h32.astype(BF16)
        logits = mm_dims(head_w, hb, 1, 1)
        top = jnp.max(logits, axis=0, keepdims=True)
        low = logits - top
        log_s = low - jnp.log(jnp.sum(jnp.exp(low), axis=0, keepdims=True))
        prob = jnp.exp(log_s)
        mean = mean_t[b * 64:(b + 1) * 64, :]
        spr = mean_t[512 + b:513 + b, :] + mean_t[520 + b:521 + b, :] + mean_t[528 + b:529 + b, :]
        wgt = 1.0 / (0.1 + spr)
        hot = classes.astype(F32) == labels[b:b + 1, :]
        ent = jnp.where(mean > 0, mean * jnp.log(jnp.where(mean > 0, mean, 1.0)), 0.0)
        kl = jnp.sum(ent - mean * log_s, axis=0, keepdims=True)
        nll = jnp.sum(jnp.where(hot, log_s, 0.0), axis=0, keepdims=True)
        loss = loss + (wgt * kl - nll)
        lg = ((wgt * (prob - mean) + prob - jnp.where(hot, 1.0, 0.0)) * scale).astype(BF16)
        head_t = head_t + mm(lg, hb)
        hg = mm_dims(lg, head_w, 0, 0)
        g2 = jnp.where(h32 > 0, hg, 0.0)
        gf[0, s, :] = g2[:, :128]
        gf[1, s, :] = g2[:, 128:]

    def round_grad(k, carry):
        s = pl.ds(pl.multiple_of(k * 128, 128), 128)
        d = pl.ds(pl.multiple_of(128 + k * 128, 128), 128)
        gp[d, 0:128] = gf[0, s, :].astype(BF16)
        gp[d, 128:256] = gf[1, s, :].astype(BF16)
        return carry

    lax.fori_loop(0, 16, round_grad, 0)
    gh_up = remote(gp.at[pl.ds(CELLS, 128), :], gp.at[pl.ds(0, 128), :], (z, up))
    gh_dn = remote(gp.at[pl.ds(128, 128), :], gp.at[pl.ds(128 + CELLS, 128), :], (z, down))

    small = {"head": jnp.concatenate([head_t[:, :128], head_t[:, 128:]], axis=0),
             "loss": jnp.broadcast_to(jnp.sum(loss, axis=1, keepdims=True), (8, 128))}

    def small_send(n, axis):
        me = coords[axis]
        hx[n, me] = small["head"].astype(BF16)
        lx[n, me] = small["loss"]
        size = 2 if axis == "c" else 4
        small["wait"] = []
        for o in range(1, size):
            dev = peer(axis, lax.rem(me + o, size))
            small["wait"].append(remote(hx.at[n, me], hx.at[n, me], dev))
            small["wait"].append(remote(lx.at[n, me], lx.at[n, me], dev))

    def small_recv(n, axis):
        for c in small["wait"]:
            c.wait_recv()
        size = 2 if axis == "c" else 4
        h, l = hx[n, 0].astype(F32), lx[n, 0]
        for j in range(1, size):
            h = h + hx[n, j].astype(F32)
            l = l + lx[n, j]
        small["head"], small["loss"] = h, l

    orders = (("x", "y", "z"), ("y", "z", "x"), ("z", "x", "y"))

    class Piece:
        def __init__(self, index):
            self.refs = piece_refs[9 * index:9 * index + 9]
            self.rows = PIECES[index]
            self.n, self.at = (0, 0) if index == 0 else (1, 768 * (index - 1))
            self.wait = []

        def done(self):
            for c in self.wait:
                c.wait_recv()
            self.wait = []

        def spread(self, level, p, j):
            one, two = self.rows // 12, self.rows // 48
            if level == 1:
                return pl.ds(pl.multiple_of(4 * one * p + one * j, 16), one)
            first = one * coords[orders[p][0]]
            return pl.ds(pl.multiple_of(self.at + 4 * one * p + first + two * j, 16), two)

        def product(self, row, lhs, rhs):
            csb, crb, acc = self.refs[:3]
            d = mm(lhs, rhs)
            low, high = d[:, :128], d[:, 128:]
            acc[row:row + 768, :] = jnp.where(core == 0, low, high)
            csb[row:row + 768, :] = jnp.where(core == 0, high, low).astype(BF16)
            s = pl.ds(row, 768)
            self.wait.append(remote(csb.at[s, :], crb.at[s, :], peer("c", 1 - core)))

        def s1(self):
            self.done()
            csb, crb, acc, s1b, r1 = self.refs[:5]

            def step(k, carry):
                s = pl.ds(pl.multiple_of(k * 256, 256), 256)
                v = acc[s, :] + crb[s, :].astype(F32)
                acc[s, :] = v
                s1b[s, :] = v.astype(BF16)
                return carry

            lax.fori_loop(0, self.rows // 256, step, 0)
            for o in (2, 1, 3):
                for p in range(3):
                    ax = orders[p][0]
                    j = ring(ax, o)
                    src = s1b.at[self.spread(1, p, j), :]
                    self.wait.append(remote(src, r1.at[p, o], peer(ax, j)))

        def s2(self):
            self.done()
            acc, r1, a1c, s2b, r2 = self.refs[2], *self.refs[4:8]
            for p in range(3):
                v = acc[self.spread(1, p, coords[orders[p][0]]), :]
                for o in range(1, 4):
                    v = v + r1[p, o].astype(F32)
                a1c[p] = v
                s2b[p] = v.astype(BF16)
            two = self.rows // 48
            for o in (2, 1, 3):
                for p in range(3):
                    ax = orders[p][1]
                    j = ring(ax, o)
                    src = s2b.at[p, pl.ds(pl.multiple_of(two * j, 16), two), :]
                    self.wait.append(remote(src, r2.at[p, o], peer(ax, j)))

        def s3(self):
            self.done()
            a1c, s2b, r2, x3 = self.refs[5:9]
            two = self.rows // 48
            for p in range(3):
                s = pl.ds(pl.multiple_of(two * coords[orders[p][1]], 16), two)
                v = a1c[p, s, :]
                for o in range(1, 4):
                    v = v + r2[p, o].astype(F32)
                x3[p, coords[orders[p][2]]] = v.astype(BF16)
            for o in (2, 1, 3):
                for p in range(3):
                    ax = orders[p][2]
                    ref = x3.at[p, coords[ax]]
                    self.wait.append(remote(ref, ref, peer(ax, ring(ax, o))))

        def g2(self):
            self.done()
            x3 = self.refs[8]
            for p in range(3):
                v = x3[p, 0].astype(F32)
                for j in range(1, 4):
                    v = v + x3[p, j].astype(F32)
                gat[self.n, core, self.spread(2, p, coords[orders[p][1]]), :] = v.astype(BF16)
            for o in (2, 1, 3):
                for p in range(3):
                    ax = orders[p][1]
                    ref = gat.at[self.n, core, self.spread(2, p, coords[ax]), :]
                    self.wait.append(remote(ref, ref, peer(ax, ring(ax, o))))

        def g1(self):
            self.done()
            one = self.rows // 12
            for o in (2, 1, 3):
                for p in range(3):
                    ax = orders[p][0]
                    s = pl.ds(pl.multiple_of(self.at + 4 * one * p + one * coords[ax], 16), one)
                    ref = gat.at[self.n, core, s, :]
                    self.wait.append(remote(ref, ref, peer(ax, ring(ax, o))))

        def gc(self):
            self.done()
            ref = gat.at[self.n, core, pl.ds(self.at, self.rows), :]
            self.wait.append(remote(ref, ref, peer("c", 1 - core)))

        def store(self):
            self.done()
            out = (o2, o1)[self.n]
            s = pl.ds(self.at, self.rows)
            for h in range(2):
                c = pltpu.make_async_copy(
                    gat.at[self.n, h, s, :], out.at[s, pl.ds(128 * h, 128)], lsem.at[7 + len(outs)]
                )
                c.start()
                outs.append(c)

    outs = []
    second = Piece(0)
    firsts = [Piece(1), Piece(2), Piece(3)]

    small_send(0, "c")
    grad_two = gp[128:128 + CELLS, :]
    for a in range(3):
        second.product(768 * a, a2t[:, 128 * a:128 * a + CELLS], grad_two)
    small_recv(0, "c")
    small_send(1, "x")

    gh_up.wait_recv()
    gh_dn.wait_recv()

    def build_grad(k, carry):
        s = pl.ds(pl.multiple_of(k * 128, 128), 128)
        row = t * ROWS - 2 + 2 * k + lax.div(iota((128, CH), 0), COLS)
        v = jnp.where((row >= 0) & (row < NT * ROWS), gp[s, :].astype(F32), 0.0)
        before, after = shifted(v, 2, 0, 0, 128)
        ag[s, 0:CH] = before
        ag[s, CH:2 * CH] = v.astype(BF16)
        ag[s, 2 * CH:3 * CH] = after
        return carry

    lax.fori_loop(0, 18, build_grad, 0)
    second.s1()

    def back(k, carry):
        n = 256
        total = None
        for a in range(3):
            s = pl.ds(pl.multiple_of(k * n + (2 - a) * 2 * COLS, 128), n)
            d = mm(ag[s, :], w2t[a])
            total = d if total is None else total + d
        h = a2[pl.ds(pl.multiple_of(128 + k * n, 128), n), CH:2 * CH].astype(F32)
        v = jnp.where(h > 0, total, 0.0).astype(BF16)
        xb[pl.ds(pl.multiple_of(k * n, n), n), :] = v
        return carry

    lax.fori_loop(0, 4, back, 0)
    small_recv(1, "x")
    small_send(2, "y")
    lax.fori_loop(4, 8, back, 0)
    second.s2()
    grad_one = xb[0:CELLS, :]
    firsts[0].product(0, a1e[:, 0:CELLS], grad_one)
    small_recv(2, "y")
    small_send(3, "z")
    firsts[1].product(0, a1o[...], grad_one)
    firsts[0].s1()
    second.s3()
    firsts[2].product(0, a1e[:, 128:128 + CELLS], grad_one)
    firsts[1].s1()
    firsts[2].s1()
    second.g2()
    small_recv(3, "z")
    for c in firsts:
        c.s2()
    second.g1()
    for c in firsts:
        c.s3()
    second.gc()
    ohead[:, 0:128] = small["head"][:64]
    ohead[:, 128:256] = small["head"][64:]
    oloss[...] = small["loss"]
    for c in firsts:
        c.g2()
    second.store()
    for c in firsts:
        c.g1()
    for c in firsts:
        c.gc()
    for c in firsts:
        c.store()
    for c in sent:
        c.wait_send()
    for c in outs:
        c.wait()


def widen(first, second, head, loss, out_first, out_second, out_head, out_loss):
    out_first[...] = first[...].astype(F32)
    out_second[...] = second[...].astype(F32)
    out_head[...] = head[...]
    out_loss[...] = loss[0:1, 0:1] * (1.0 / (NZ * NT * CELLS))


def body(teacher_logits, coverage, features, labels, first_weight, second_weight, head_weight):
    any_spec = pl.BlockSpec(memory_space=pl.ANY)
    vmem = pl.BlockSpec(memory_space=pltpu.VMEM)
    out = [
        jax.ShapeDtypeStruct((2304, 256), BF16),
        jax.ShapeDtypeStruct((2304, 256), BF16),
        jax.ShapeDtypeStruct((NCLS, CH), F32),
        jax.ShapeDtypeStruct((8, 128), F32),
    ]
    V = pltpu.VMEM
    scratch = [
        V((4, 4, 32, 4096), BF16),
        V((2432, CH), BF16),
        V((2432, 3 * CH), BF16),
        V((3 * CH, 2304), BF16),
        V((3 * CH, 2048), BF16),
        V((2304, 3 * CH), BF16),
        V((3 * CH, 2304), BF16),
        V((2304, 3 * CH), BF16),
        V((2304, CH), BF16),
        V((3, 3 * CH, CH), BF16),
        V((3, 3 * CH, CH), BF16),
        V((3, 3 * CH, CH), BF16),
        V((2, CELLS, 128), F32),
        V((2, CELLS, 128), F32),
        V((2, 2, 2304, 128), BF16),
        V((2, 32, 2048), BF16),
        V((2, 32, 2048), BF16),
        V((2, 2, 32, 2048), BF16),
        V((2, 32, 2048), BF16),
        V((2, 32, 2048), BF16),
        V((2, 32, 2048), F32),
        V((2, 32, 2048), F32),
        V((3, 32, 128), F32),
        V((3, 32, 128), F32),
        V((256, 640), BF16),
        V((NT, 16, 640), BF16),
        V((NT, 16, 640), BF16),
        V((640, 256), F32),
        V((4, 4, 128, 128), BF16),
        V((4, 4, 8, 128), F32),
        V((256, 256), BF16),
        V((256, 128), BF16),
        V((512, 256), BF16),
        pltpu.SemaphoreType.DMA((NSEM,)),
        pltpu.SemaphoreType.DMA((NSEM,)),
        pltpu.SemaphoreType.DMA((16,)),
    ]
    for rows in PIECES:
        scratch += [
            V((rows, 128), BF16),
            V((rows, 128), BF16),
            V((rows, 128), F32),
            V((rows, 128), BF16),
            V((3, 4, rows // 12, 128), BF16),
            V((3, rows // 12, 128), F32),
            V((3, rows // 12, 128), BF16),
            V((3, 4, rows // 48, 128), BF16),
            V((3, 4, rows // 48, 128), BF16),
        ]
    first, second, head, loss = pl.pallas_call(
        kernel,
        out_shape=out,
        in_specs=[any_spec, vmem, any_spec, vmem, any_spec, any_spec, vmem],
        out_specs=[any_spec, any_spec, vmem, vmem],
        scratch_shapes=scratch,
        compiler_params=pltpu.CompilerParams(
            collective_id=0, has_side_effects=True, vmem_limit_bytes=67043328
        ),
    )(
        teacher_logits,
        coverage.reshape(1, 128),
        features.reshape(CELLS, CH),
        labels.reshape(ROWS, COLS),
        first_weight.reshape(3, 3 * CH, CH),
        second_weight.reshape(3, 3 * CH, CH),
        head_weight.T,
    )
    steps, rows = 4, 2304 // 4
    big = pl.BlockSpec((rows, CH), lambda i: (i, 0))
    first, second, head, loss = pl.pallas_call(
        widen,
        grid=(steps,),
        out_shape=[
            jax.ShapeDtypeStruct((2304, CH), F32),
            jax.ShapeDtypeStruct((2304, CH), F32),
            jax.ShapeDtypeStruct((NCLS, CH), F32),
            jax.ShapeDtypeStruct((1, 1), F32),
        ],
        in_specs=[
            big, big, pl.BlockSpec((NCLS, CH), lambda i: (0, 0)), pl.BlockSpec((8, 128), lambda i: (0, 0))
        ],
        out_specs=[
            big, big, pl.BlockSpec((NCLS, CH), lambda i: (0, 0)), pl.BlockSpec((1, 1), lambda i: (0, 0))
        ],
    )(first, second, head, loss)
    return (
        first.reshape(3, 3, CH, CH), second.reshape(3, 3, CH, CH), head.T, loss.reshape(())
    )


def solution(mesh):
    return jax.shard_map(
        body,
        mesh=mesh,
        in_specs=(
            P("member", "tile", None),
            P("tile"),
            P("member", "tile", None, None),
            P("member", "tile", None),
            P(),
            P(),
            P(),
        ),
        out_specs=(P(), P(), P(), P()),
        check_vma=False,
    )
```

```python
import math

import jax
import jax.numpy as jnp
from jax import lax
from jax.experimental import pallas as pl
from jax.experimental.pallas import tpu as pltpu
from jax.sharding import PartitionSpec as P

F32 = jnp.float32
BF16 = jnp.bfloat16
I32 = jnp.int32
MESH = pl.DeviceIdType.MESH

CH = 256
NCLS = 64
NZ = 4
NT = 32
ROWS = 32
COLS = 64
CELLS = ROWS * COLS
NSEM = 46
PIECES = (2304, 768, 768, 768)


def iota(shape, dim):
    return lax.broadcasted_iota(I32, shape, dim)


def onehot(mask):
    return jnp.where(mask, 1.0, 0.0).astype(BF16)


def mm(a, b):
    return jnp.dot(a, b, preferred_element_type=F32)


def mm_dims(a, b, ca, cb):
    return lax.dot_general(a, b, (((ca,), (cb,)), ((), ())), preferred_element_type=F32)


def kernel(
    tl, cov, feat, lab, w1h, w2h, wh,
    o1, o2, ohead, oloss,
    tv, xb, a1, a1e, a1o, a2, a2t, ag, gp, w1, w2, w2t, hf, gf, gat,
    rel_s, rel_r, fin_s, fin_l, fin_r, own, part, sec_s, sec_r,
    mp, sb, rb, mean_t, hx, lx, wb, wq, pick_s,
    ssem, rsem, lsem, *piece_refs,
):
    z = lax.axis_index("member")
    t = lax.axis_index("tile")
    core = lax.rem(t, 2)
    xc = lax.rem(lax.div(t, 2), 4)
    yc = lax.div(t, 8)
    coords = {"x": xc, "y": yc, "z": z, "c": core}

    def peer(axis, j):
        if axis == "z":
            return (j, t)
        if axis == "x":
            return (z, yc * 8 + j * 2 + core)
        if axis == "y":
            return (z, j * 8 + xc * 2 + core)
        return (z, yc * 8 + xc * 2 + j)

    groups = []

    class Group:
        def __init__(self, total):
            self.total, self.index = total, len(groups)
            groups.append(self)

        def describe(self, src, dst, dev):
            return pltpu.make_async_remote_copy(
                src_ref=src, dst_ref=dst, send_sem=ssem.at[self.index],
                recv_sem=rsem.at[self.index], device_id=dev, device_id_type=MESH,
            )

        def send(self, src, dst, dev):
            self.dev = dev
            self.describe(src, dst, dev).start()

        def wait_recv(self):
            self.describe(self.total, self.total, self.dev).wait_recv()

        def wait_send(self):
            self.describe(self.total, self.total, self.dev).wait_send()

    def remote(src, dst, dev):
        group = Group(dst)
        group.send(src, dst, dev)
        return group

    def ring(axis, o):
        return lax.rem(coords[axis] + o, 4)

    barrier = pltpu.get_barrier_semaphore()
    for o in range(1, NT):
        pl.semaphore_signal(barrier, inc=1, device_id=(z, lax.rem(t + o, NT)), device_id_type=MESH)
    for o in range(1, NZ):
        pl.semaphore_signal(barrier, inc=1, device_id=(lax.rem(z + o, NZ), t), device_id_type=MESH)

    zr, zl, zf = lax.rem(z + 1, NZ), lax.rem(z + 3, NZ), lax.rem(z + 2, NZ)
    loads = []
    for ci, g in enumerate((zf, zr, zl, z)):
        c = pltpu.make_async_copy(
            tl.at[:, pl.ds(pl.multiple_of(g * 32, 32), 32), :], tv.at[ci], lsem.at[ci]
        )
        c.start()
        loads.append(c)
    load_x = pltpu.make_async_copy(feat, xb.at[pl.ds(192, CELLS), :], lsem.at[4])
    load_w1 = pltpu.make_async_copy(w1h, w1, lsem.at[5])
    load_w2 = pltpu.make_async_copy(w2h, w2, lsem.at[6])
    load_x.start()
    load_w1.start()
    load_w2.start()

    wb[...] = onehot(lax.div(iota((256, 256), 0), 64) == lax.div(iota((256, 256), 1), 64))
    wq[...] = onehot(lax.div(iota((256, 128), 0), 64) == iota((256, 128), 1))

    def cell_sums(v, half, total):
        hi = v.astype(BF16)
        lo = (v - hi.astype(F32)).astype(BF16)
        both = mm(jnp.concatenate([hi, lo], axis=0), wq[...])
        for j in range(8):
            s = both[32 * j:32 * (j + 1)] + both[256 + 32 * j:288 + 32 * j]
            shift = half * 32 + 4 * j
            total = total + (pltpu.roll(s, shift, 1) if shift else s)
        return total

    def soft(ci, half, put, sec):
        x = jnp.concatenate(
            [
                tv[ci, :, :, half * 2048 + 256 * j:half * 2048 + 256 * (j + 1)].reshape(128, 256)
                for j in range(8)
            ],
            axis=0,
        ).astype(F32)
        e4 = jnp.exp2(x * (math.log2(math.e) / 4.0))
        r = e4 / mm(e4.astype(BF16), wb[...])
        r2 = r * r
        e = (r2 * r2).astype(BF16)
        p = e.astype(F32) / mm(e, wb[...])
        p = p.reshape(8, 4, 32, 256)
        sq = p * p
        f = (p[:, 0] + p[:, 1]) + (p[:, 2] + p[:, 3])
        q = (sq[:, 0] + sq[:, 1]) + (sq[:, 2] + sq[:, 3])
        for j in range(8):
            put(j, f[j])
        return cell_sums(q.reshape(256, 256), half, sec)

    def put_to(ref, *lead):
        def put(j, v):
            ref[(*lead, slice(None), slice(256 * j, 256 * (j + 1)))] = v.astype(ref.dtype)

        return put

    zero_sec = jnp.zeros((32, 128), F32)
    loads[0].wait()
    sec_f = soft(0, 0, put_to(rel_s, 0), zero_sec)
    pl.semaphore_wait(barrier, NT - 1 + NZ - 1)
    relay_a = remote(rel_s.at[0], rel_r.at[0], (zr, t))
    up, down = lax.rem(t + 1, NT), lax.rem(t + NT - 1, NT)
    halo = Group(xb.at[pl.ds(0, 384), :])
    halo.send(feat.at[pl.ds(CELLS - 192, 192), :], xb.at[pl.ds(0, 192), :], (z, up))
    halo.send(feat.at[pl.ds(0, 192), :], xb.at[pl.ds(192 + CELLS, 192), :], (z, down))
    sec_f = soft(0, 1, put_to(rel_s, 1), sec_f)
    relay_b = remote(rel_s.at[1], rel_r.at[1], (zl, t))
    loads[1].wait()
    sec_1 = soft(1, 1, put_to(fin_s, 0, 1), zero_sec)
    f0 = remote(fin_s.at[0, 1], fin_l.at[1], (zr, t))
    loads[2].wait()
    sec_2 = soft(2, 0, put_to(fin_s, 1, 0), zero_sec)
    f1 = remote(fin_s.at[1, 0], fin_r.at[0], (zl, t))
    sec_1 = soft(1, 0, put_to(part, 0), sec_1)
    sec_2 = soft(2, 1, put_to(part, 1), sec_2)

    def add_relay(side, half):
        fin_s[side, half] = (part[side] + rel_r[half].astype(F32)).astype(BF16)

    relay_a.wait_recv()
    add_relay(0, 0)
    f2 = remote(fin_s.at[0, 0], fin_l.at[0], (zr, t))
    relay_b.wait_recv()
    add_relay(1, 1)
    f3 = remote(fin_s.at[1, 1], fin_r.at[1], (zl, t))
    sec_c = Group(sec_r)
    for i, (value, to) in enumerate(((sec_f, zf), (sec_1, zr), (sec_2, zl))):
        sec_s[i] = value
        sec_c.send(sec_s.at[i], sec_r.at[i], (to, t))
    loads[3].wait()
    sec_m = soft(3, 0, put_to(own, 0), zero_sec)
    sec_m = soft(3, 1, put_to(own, 1), sec_m)

    crow = cov[...]
    i0, i1 = iota((128, 128), 0), iota((128, 128), 1)
    ccol = jnp.sum(jnp.where(i0 == i1, crow, 0), axis=1, keepdims=True)
    same = (ccol == crow) & (lax.div(i0, 32) == lax.div(i1, 32)) & (i0 < i1)
    rank = jnp.sum(jnp.where(same, 1, 0), axis=0, keepdims=True)
    slot = jnp.broadcast_to(crow * 2 + rank, (8, 128)).astype(F32)
    lane8 = iota((8, 128), 1)
    mine = jnp.zeros((8, 128), F32)
    for g in range(NZ):
        moved = slot if g == 0 else pltpu.roll(slot, 128 - 32 * g, 1)
        mine = jnp.where(z == g, moved, mine)
    mine = jnp.where(lane8 < 32, mine, 0.0)
    mine = mine + pltpu.roll(mine, 32, 1)
    mine = mine + pltpu.roll(mine, 64, 1)
    slots = jnp.concatenate([mine, mine], axis=1)[0:1, :]
    j0, j1 = iota((512, 256), 0), iota((512, 256), 1)
    pick_s[...] = onehot(
        (lax.div(j0, 8).astype(F32) == slots) & (lax.rem(j0, 8) == lax.div(j1, 32))
    )

    def shifted(v, by, lo_col, hi_col, rows):
        col = lax.rem(iota((rows, CH), 0), COLS)
        before = jnp.where(col >= by, pltpu.roll(v, by, 0), 0.0)
        after = jnp.where(col < COLS - by, pltpu.roll(v, rows - by, 0), 0.0)
        return before.astype(BF16), after.astype(BF16)

    load_x.wait()
    load_w1.wait()
    halo.wait_recv()

    def build_one(k, carry):
        s = pl.ds(pl.multiple_of(k * 128, 128), 128)
        row = t * ROWS - 3 + 2 * k + lax.div(iota((128, CH), 0), COLS)
        v = xb[s, :].astype(F32)
        v = jnp.where((row >= 0) & (row < NT * ROWS), v, 0.0)
        before, after = shifted(v, 1, 0, 0, 128)
        a1[s, 0:CH] = before
        a1[s, CH:2 * CH] = v.astype(BF16)
        a1[s, 2 * CH:3 * CH] = after
        return carry

    lax.fori_loop(0, 19, build_one, 0)

    def conv_rows(a_ref, w_ref, start, rows, stride):
        total = None
        for a in range(3):
            s = pl.ds(pl.multiple_of(start + a * stride, 64), rows)
            d = mm(a_ref[s, :], w_ref[a])
            total = d if total is None else total + d
        return total

    def conv_one(k, carry):
        n = 256
        start = k * n
        pre = conv_rows(a1, w1, start, n, COLS)
        row = t * ROWS - 2 + 4 * k + lax.div(iota((n, CH), 0), COLS)
        h = jnp.where((row >= 0) & (row < NT * ROWS) & (pre > 0), pre, 0.0)
        h = h.astype(BF16).astype(F32)
        before, after = shifted(h, 2, 0, 0, n)
        s = pl.ds(pl.multiple_of(start, n), n)
        a2[s, 0:CH] = before
        a2[s, CH:2 * CH] = h.astype(BF16)
        a2[s, 2 * CH:3 * CH] = after
        a1e[:, s] = a1[pl.ds(pl.multiple_of(128 + start, 128), n), :].T
        odd = jnp.minimum(k, 7) * n
        a1o[:, pl.ds(pl.multiple_of(odd, n), n)] = a1[pl.ds(pl.multiple_of(192 + odd, 64), n), :].T
        return carry

    lax.fori_loop(0, 9, conv_one, 0)

    for c in (f0, f1, f2, f3, sec_c):
        c.wait_recv()

    msq = zero_sec
    for half in range(2):
        m = (
            own[half] + fin_l[half].astype(F32) + fin_r[half].astype(F32)
        ) * (1.0 / 16.0)
        squares = []
        for j in range(8):
            mj = m[:, 256 * j:256 * (j + 1)]
            row = (half * 4 + j // 2) * 32
            mp[row:row + 32, (j % 2) * 256:(j % 2 + 1) * 256] = mj.astype(BF16)
            squares.append(mj * mj)
        msq = cell_sums(jnp.concatenate(squares, axis=0), half, msq)
    second = (sec_m + sec_r[0]) + (sec_r[1] + sec_r[2])
    spread = second * (1.0 / 16.0) - msq
    lane = iota((32, 128), 1)
    slot_no = (iota((32, 128), 0) + 1).astype(F32)
    for a in range(8):
        sp = spread if a == 0 else pltpu.roll(spread, 128 - 8 * a, 1)
        sp = jnp.where(lane < 8, sp, 0.0)
        hi = sp.astype(BF16).astype(F32)
        mid = (sp - hi).astype(BF16).astype(F32)
        lo = sp - hi - mid
        ext = hi + pltpu.roll(mid, 8, 1) + pltpu.roll(lo, 16, 1)
        ext = jnp.where(lane == 24, slot_no, ext)
        mp[a * 32:(a + 1) * 32, 512:640] = ext.astype(BF16)

    sb[...] = mm(pick_s[...], mp[...]).astype(BF16).reshape(NT, 16, 640)
    exch = Group(rb.at[pl.ds(0, NT - 1)])
    for o in range(1, NT):
        d = lax.rem(t + o, NT)
        exch.send(sb.at[d], rb.at[t], (z, d))
    rb[t] = sb[t]

    load_w2.wait()

    def conv_two(k, carry):
        n = 256
        pre = conv_rows(a2, w2, k * n, n, 2 * COLS)
        h = jnp.where(pre > 0, pre, 0.0)
        s = pl.ds(pl.multiple_of(k * n, n), n)
        hf[0, s, :] = h[:, :128]
        hf[1, s, :] = h[:, 128:]
        a2t[:, s] = a2[s, :].T
        return carry

    lax.fori_loop(0, 8, conv_two, 0)
    a2t[:, CELLS:CELLS + 256] = a2[CELLS:CELLS + 256, :].T

    for a in range(3):
        for b in range(3):
            w2t[a, b * CH:(b + 1) * CH, :] = w2[a, (2 - b) * CH:(3 - b) * CH, :].T

    l_rep = onehot(lax.div(iota((256, 32), 0), 8) == iota((256, 32), 1))
    rep = mm(l_rep, lab[...].astype(F32).astype(BF16))
    rep = jnp.where(
        lax.div(iota((256, 64), 1), 8) == lax.rem(iota((256, 64), 0), 8), rep, 0.0
    ).astype(BF16)
    l_sel = onehot(lax.rem(iota((8, 64), 1), 8) == iota((8, 64), 0))
    labels = mm_dims(l_sel, rep, 1, 1)

    exch.wait_recv()
    got = rb[...].reshape(512, 640)
    from_slot = got[:, 512:640].astype(F32)[:, 24:25]
    n0, n1 = iota((512, 256), 0), iota((512, 256), 1)
    tile_no = (lax.div(n1, 64) * 8 + lax.rem(n1, 8) + 1).astype(F32)
    place = onehot((from_slot == tile_no) & (lax.rem(n0, 8) == lax.rem(lax.div(n1, 8), 8)))
    mean_t[...] = mm_dims(got, place, 0, 0)

    scale = 1.0 / math.sqrt(NZ * NT * CELLS)
    head_w = wh[...]
    classes = iota((NCLS, 256), 0)
    loss = jnp.zeros((1, 256), F32)
    head_t = jnp.zeros((NCLS, CH), F32)
    for b in range(8):
        s = pl.ds(b, 256, stride=8)
        h32 = jnp.concatenate([hf[0, s, :], hf[1, s, :]], axis=1)
        hb = h32.astype(BF16)
        logits = mm_dims(head_w, hb, 1, 1)
        top = jnp.max(logits, axis=0, keepdims=True)
        low = logits - top
        log_s = low - jnp.log(jnp.sum(jnp.exp(low), axis=0, keepdims=True))
        prob = jnp.exp(log_s)
        mean = mean_t[b * 64:(b + 1) * 64, :]
        spr = mean_t[512 + b:513 + b, :] + mean_t[520 + b:521 + b, :] + mean_t[528 + b:529 + b, :]
        wgt = 1.0 / (0.1 + spr)
        hot = classes.astype(F32) == labels[b:b + 1, :]
        ent = jnp.where(mean > 0, mean * jnp.log(jnp.where(mean > 0, mean, 1.0)), 0.0)
        kl = jnp.sum(ent - mean * log_s, axis=0, keepdims=True)
        nll = jnp.sum(jnp.where(hot, log_s, 0.0), axis=0, keepdims=True)
        loss = loss + (wgt * kl - nll)
        lg = ((wgt * (prob - mean) + prob - jnp.where(hot, 1.0, 0.0)) * scale).astype(BF16)
        head_t = head_t + mm(lg, hb)
        hg = mm_dims(lg, head_w, 0, 0)
        g2 = jnp.where(h32 > 0, hg, 0.0)
        gf[0, s, :] = g2[:, :128]
        gf[1, s, :] = g2[:, 128:]

    def round_grad(k, carry):
        s = pl.ds(pl.multiple_of(k * 128, 128), 128)
        d = pl.ds(pl.multiple_of(128 + k * 128, 128), 128)
        gp[d, 0:128] = gf[0, s, :].astype(BF16)
        gp[d, 128:256] = gf[1, s, :].astype(BF16)
        return carry

    lax.fori_loop(0, 16, round_grad, 0)
    edge = Group(gp.at[pl.ds(0, 256), :])
    edge.send(gp.at[pl.ds(CELLS, 128), :], gp.at[pl.ds(0, 128), :], (z, up))
    edge.send(gp.at[pl.ds(128, 128), :], gp.at[pl.ds(128 + CELLS, 128), :], (z, down))

    small = {"head": jnp.concatenate([head_t[:, :128], head_t[:, 128:]], axis=0),
             "loss": jnp.broadcast_to(jnp.sum(loss, axis=1, keepdims=True), (8, 128))}

    def small_send(n, axis):
        me = coords[axis]
        hx[n, me] = small["head"].astype(BF16)
        lx[n, me] = small["loss"]
        size = 2 if axis == "c" else 4
        h, l = Group(hx.at[n, pl.ds(1, size - 1)]), Group(lx.at[n, pl.ds(1, size - 1)])
        small["wait"] = [h, l]
        for o in range(1, size):
            dev = peer(axis, lax.rem(me + o, size))
            h.send(hx.at[n, me], hx.at[n, me], dev)
            l.send(lx.at[n, me], lx.at[n, me], dev)

    def small_recv(n, axis):
        for c in small["wait"]:
            c.wait_recv()
        size = 2 if axis == "c" else 4
        h, l = hx[n, 0].astype(F32), lx[n, 0]
        for j in range(1, size):
            h = h + hx[n, j].astype(F32)
            l = l + lx[n, j]
        small["head"], small["loss"] = h, l

    orders = (("x", "y", "z"), ("y", "z", "x"), ("z", "x", "y"))

    class Piece:
        def __init__(self, index):
            self.refs = piece_refs[9 * index:9 * index + 9]
            self.rows = PIECES[index]
            self.n, self.at = (0, 0) if index == 0 else (1, 768 * (index - 1))
            self.group = Group(self.refs[1])

        def done(self):
            self.group.wait_recv()

        def spread(self, level, p, j):
            one, two = self.rows // 12, self.rows // 48
            if level == 1:
                return pl.ds(pl.multiple_of(4 * one * p + one * j, 16), one)
            first = one * coords[orders[p][0]]
            return pl.ds(pl.multiple_of(self.at + 4 * one * p + first + two * j, 16), two)

        def product(self, row, lhs, rhs):
            csb, crb, acc = self.refs[:3]
            d = mm(lhs, rhs)
            low, high = d[:, :128], d[:, 128:]
            acc[row:row + 768, :] = jnp.where(core == 0, low, high)
            csb[row:row + 768, :] = jnp.where(core == 0, high, low).astype(BF16)
            s = pl.ds(row, 768)
            self.group.send(csb.at[s, :], crb.at[s, :], peer("c", 1 - core))

        def s1(self):
            self.done()
            csb, crb, acc, s1b, r1 = self.refs[:5]

            def step(k, carry):
                s = pl.ds(pl.multiple_of(k * 256, 256), 256)
                v = acc[s, :] + crb[s, :].astype(F32)
                acc[s, :] = v
                s1b[s, :] = v.astype(BF16)
                return carry

            lax.fori_loop(0, self.rows // 256, step, 0)
            self.group = Group(r1.at[:, pl.ds(1, 3)])
            for o in (2, 1, 3):
                for p in range(3):
                    ax = orders[p][0]
                    j = ring(ax, o)
                    src = s1b.at[self.spread(1, p, j), :]
                    self.group.send(src, r1.at[p, o], peer(ax, j))

        def s2(self):
            self.done()
            acc, r1, a1c, s2b, r2 = self.refs[2], *self.refs[4:8]
            for p in range(3):
                v = acc[self.spread(1, p, coords[orders[p][0]]), :]
                for o in range(1, 4):
                    v = v + r1[p, o].astype(F32)
                a1c[p] = v
                s2b[p] = v.astype(BF16)
            two = self.rows // 48
            self.group = Group(r2.at[:, pl.ds(1, 3)])
            for o in (2, 1, 3):
                for p in range(3):
                    ax = orders[p][1]
                    j = ring(ax, o)
                    src = s2b.at[p, pl.ds(pl.multiple_of(two * j, 16), two), :]
                    self.group.send(src, r2.at[p, o], peer(ax, j))

        def s3(self):
            self.done()
            a1c, s2b, r2, x3 = self.refs[5:9]
            two = self.rows // 48
            for p in range(3):
                s = pl.ds(pl.multiple_of(two * coords[orders[p][1]], 16), two)
                v = a1c[p, s, :]
                for o in range(1, 4):
                    v = v + r2[p, o].astype(F32)
                x3[p, coords[orders[p][2]]] = v.astype(BF16)
            self.group = Group(x3.at[:, pl.ds(1, 3)])
            for o in (2, 1, 3):
                for p in range(3):
                    ax = orders[p][2]
                    ref = x3.at[p, coords[ax]]
                    self.group.send(ref, ref, peer(ax, ring(ax, o)))

        def g2(self):
            self.done()
            x3 = self.refs[8]
            for p in range(3):
                v = x3[p, 0].astype(F32)
                for j in range(1, 4):
                    v = v + x3[p, j].astype(F32)
                gat[self.n, core, self.spread(2, p, coords[orders[p][1]]), :] = v.astype(BF16)
            self.group = Group(x3.at[:, pl.ds(1, 3)])
            for o in (2, 1, 3):
                for p in range(3):
                    ax = orders[p][1]
                    ref = gat.at[self.n, core, self.spread(2, p, coords[ax]), :]
                    self.group.send(ref, ref, peer(ax, ring(ax, o)))

        def g1(self):
            self.done()
            one = self.rows // 12
            self.group = Group(self.refs[4].at[:, pl.ds(1, 3)])
            for o in (2, 1, 3):
                for p in range(3):
                    ax = orders[p][0]
                    s = pl.ds(pl.multiple_of(self.at + 4 * one * p + one * coords[ax], 16), one)
                    ref = gat.at[self.n, core, s, :]
                    self.group.send(ref, ref, peer(ax, ring(ax, o)))

        def gc(self):
            self.done()
            ref = gat.at[self.n, core, pl.ds(self.at, self.rows), :]
            self.group = remote(ref, ref, peer("c", 1 - core))

        def store(self):
            self.done()
            out = (o2, o1)[self.n]
            s = pl.ds(self.at, self.rows)
            for h in range(2):
                c = pltpu.make_async_copy(
                    gat.at[self.n, h, s, :], out.at[s, pl.ds(128 * h, 128)], lsem.at[7 + len(outs)]
                )
                c.start()
                outs.append(c)

    outs = []
    second = Piece(0)
    firsts = [Piece(1), Piece(2), Piece(3)]

    small_send(0, "c")
    grad_two = gp[128:128 + CELLS, :]
    for a in range(3):
        second.product(768 * a, a2t[:, 128 * a:128 * a + CELLS], grad_two)
    small_recv(0, "c")
    small_send(1, "x")

    edge.wait_recv()

    def build_grad(k, carry):
        s = pl.ds(pl.multiple_of(k * 128, 128), 128)
        row = t * ROWS - 2 + 2 * k + lax.div(iota((128, CH), 0), COLS)
        v = jnp.where((row >= 0) & (row < NT * ROWS), gp[s, :].astype(F32), 0.0)
        before, after = shifted(v, 2, 0, 0, 128)
        ag[s, 0:CH] = before
        ag[s, CH:2 * CH] = v.astype(BF16)
        ag[s, 2 * CH:3 * CH] = after
        return carry

    lax.fori_loop(0, 18, build_grad, 0)
    second.s1()

    def back(k, carry):
        n = 256
        total = None
        for a in range(3):
            s = pl.ds(pl.multiple_of(k * n + (2 - a) * 2 * COLS, 128), n)
            d = mm(ag[s, :], w2t[a])
            total = d if total is None else total + d
        h = a2[pl.ds(pl.multiple_of(128 + k * n, 128), n), CH:2 * CH].astype(F32)
        v = jnp.where(h > 0, total, 0.0).astype(BF16)
        xb[pl.ds(pl.multiple_of(k * n, n), n), :] = v
        return carry

    lax.fori_loop(0, 4, back, 0)
    small_recv(1, "x")
    small_send(2, "y")
    lax.fori_loop(4, 8, back, 0)
    second.s2()
    grad_one = xb[0:CELLS, :]
    firsts[0].product(0, a1e[:, 0:CELLS], grad_one)
    small_recv(2, "y")
    small_send(3, "z")
    firsts[1].product(0, a1o[...], grad_one)
    firsts[0].s1()
    firsts[2].product(0, a1e[:, 128:128 + CELLS], grad_one)
    second.s3()
    firsts[1].s1()
    firsts[2].s1()
    second.g2()
    small_recv(3, "z")
    for c in firsts:
        c.s2()
    second.g1()
    for c in firsts:
        c.s3()
    second.gc()
    ohead[:, 0:128] = small["head"][:64]
    ohead[:, 128:256] = small["head"][64:]
    oloss[...] = small["loss"]
    for c in firsts:
        c.g2()
    second.store()
    for c in firsts:
        c.g1()
    for c in firsts:
        c.gc()
    for c in firsts:
        c.store()
    for c in groups:
        c.wait_send()
    for c in outs:
        c.wait()


def widen(first, second, head, loss, out_first, out_second, out_head, out_loss):
    out_first[...] = first[...].astype(F32)
    out_second[...] = second[...].astype(F32)
    out_head[...] = head[...]
    out_loss[...] = loss[0:1, 0:1] * (1.0 / (NZ * NT * CELLS))


def body(teacher_logits, coverage, features, labels, first_weight, second_weight, head_weight):
    any_spec = pl.BlockSpec(memory_space=pl.ANY)
    vmem = pl.BlockSpec(memory_space=pltpu.VMEM)
    out = [
        jax.ShapeDtypeStruct((2304, 256), BF16),
        jax.ShapeDtypeStruct((2304, 256), BF16),
        jax.ShapeDtypeStruct((NCLS, CH), F32),
        jax.ShapeDtypeStruct((8, 128), F32),
    ]
    V = pltpu.VMEM
    scratch = [
        V((4, 4, 32, 4096), BF16),
        V((2432, CH), BF16),
        V((2432, 3 * CH), BF16),
        V((3 * CH, 2304), BF16),
        V((3 * CH, 2048), BF16),
        V((2304, 3 * CH), BF16),
        V((3 * CH, 2304), BF16),
        V((2304, 3 * CH), BF16),
        V((2304, CH), BF16),
        V((3, 3 * CH, CH), BF16),
        V((3, 3 * CH, CH), BF16),
        V((3, 3 * CH, CH), BF16),
        V((2, CELLS, 128), F32),
        V((2, CELLS, 128), F32),
        V((2, 2, 2304, 128), BF16),
        V((2, 32, 2048), BF16),
        V((2, 32, 2048), BF16),
        V((2, 2, 32, 2048), BF16),
        V((2, 32, 2048), BF16),
        V((2, 32, 2048), BF16),
        V((2, 32, 2048), F32),
        V((2, 32, 2048), F32),
        V((3, 32, 128), F32),
        V((3, 32, 128), F32),
        V((256, 640), BF16),
        V((NT, 16, 640), BF16),
        V((NT, 16, 640), BF16),
        V((640, 256), F32),
        V((4, 4, 128, 128), BF16),
        V((4, 4, 8, 128), F32),
        V((256, 256), BF16),
        V((256, 128), BF16),
        V((512, 256), BF16),
        pltpu.SemaphoreType.DMA((NSEM,)),
        pltpu.SemaphoreType.DMA((NSEM,)),
        pltpu.SemaphoreType.DMA((16,)),
    ]
    for rows in PIECES:
        scratch += [
            V((rows, 128), BF16),
            V((rows, 128), BF16),
            V((rows, 128), F32),
            V((rows, 128), BF16),
            V((3, 4, rows // 12, 128), BF16),
            V((3, rows // 12, 128), F32),
            V((3, rows // 12, 128), BF16),
            V((3, 4, rows // 48, 128), BF16),
            V((3, 4, rows // 48, 128), BF16),
        ]
    first, second, head, loss = pl.pallas_call(
        kernel,
        out_shape=out,
        in_specs=[any_spec, vmem, any_spec, vmem, any_spec, any_spec, vmem],
        out_specs=[any_spec, any_spec, vmem, vmem],
        scratch_shapes=scratch,
        compiler_params=pltpu.CompilerParams(
            collective_id=0, has_side_effects=True, vmem_limit_bytes=67043328
        ),
    )(
        teacher_logits,
        coverage.reshape(1, 128),
        features.reshape(CELLS, CH),
        labels.reshape(ROWS, COLS),
        first_weight.reshape(3, 3 * CH, CH),
        second_weight.reshape(3, 3 * CH, CH),
        head_weight.T,
    )
    steps, rows = 4, 2304 // 4
    big = pl.BlockSpec((rows, CH), lambda i: (i, 0))
    first, second, head, loss = pl.pallas_call(
        widen,
        grid=(steps,),
        out_shape=[
            jax.ShapeDtypeStruct((2304, CH), F32),
            jax.ShapeDtypeStruct((2304, CH), F32),
            jax.ShapeDtypeStruct((NCLS, CH), F32),
            jax.ShapeDtypeStruct((1, 1), F32),
        ],
        in_specs=[
            big, big, pl.BlockSpec((NCLS, CH), lambda i: (0, 0)), pl.BlockSpec((8, 128), lambda i: (0, 0))
        ],
        out_specs=[
            big, big, pl.BlockSpec((NCLS, CH), lambda i: (0, 0)), pl.BlockSpec((1, 1), lambda i: (0, 0))
        ],
    )(first, second, head, loss)
    return (
        first.reshape(3, 3, CH, CH), second.reshape(3, 3, CH, CH), head.T, loss.reshape(())
    )


def solution(mesh):
    return jax.shard_map(
        body,
        mesh=mesh,
        in_specs=(
            P("member", "tile", None),
            P("tile"),
            P("member", "tile", None, None),
            P("member", "tile", None),
            P(),
            P(),
            P(),
        ),
        out_specs=(P(), P(), P(), P()),
        check_vma=False,
    )
```

```python
import math

import jax
import jax.numpy as jnp
from jax import lax
from jax.experimental import pallas as pl
from jax.experimental.pallas import tpu as pltpu
from jax.sharding import PartitionSpec as P

F32 = jnp.float32
BF16 = jnp.bfloat16
I32 = jnp.int32
MESH = pl.DeviceIdType.MESH

CH = 256
NCLS = 64
NZ = 4
NT = 32
ROWS = 32
COLS = 64
CELLS = ROWS * COLS
NSEM = 48
PIECES = (2304, 768, 768, 768)


def iota(shape, dim):
    return lax.broadcasted_iota(I32, shape, dim)


def onehot(mask):
    return jnp.where(mask, 1.0, 0.0).astype(BF16)


def mm(a, b):
    return jnp.dot(a, b, preferred_element_type=F32)


def mm_dims(a, b, ca, cb):
    return lax.dot_general(a, b, (((ca,), (cb,)), ((), ())), preferred_element_type=F32)


def kernel(
    tl, cov, feat, lab, w1h, w2h, wh,
    o1, o2, ohead, oloss,
    tv, xb, a1, a1e, a1o, a2, a2t, ag, gp, w1, w2, w2t, hf, gf, gat,
    rel_s, rel_r, fin_s, fin_l, fin_r, own, part, sec_s, sec_r,
    mp, sb, rb, mean_t, hx, lx, wb, wq, pick_s,
    ssem, rsem, lsem, *piece_refs,
):
    z = lax.axis_index("member")
    t = lax.axis_index("tile")
    core = lax.rem(t, 2)
    xc = lax.rem(lax.div(t, 2), 4)
    yc = lax.div(t, 8)
    coords = {"x": xc, "y": yc, "z": z, "c": core}

    def peer(axis, j):
        if axis == "z":
            return (j, t)
        if axis == "x":
            return (z, yc * 8 + j * 2 + core)
        if axis == "y":
            return (z, j * 8 + xc * 2 + core)
        return (z, yc * 8 + xc * 2 + j)

    groups = []

    class Group:
        def __init__(self, total):
            self.total, self.index = total, len(groups)
            groups.append(self)

        def describe(self, src, dst, dev):
            return pltpu.make_async_remote_copy(
                src_ref=src, dst_ref=dst, send_sem=ssem.at[self.index],
                recv_sem=rsem.at[self.index], device_id=dev, device_id_type=MESH,
            )

        def send(self, src, dst, dev):
            self.dev = dev
            self.describe(src, dst, dev).start()

        def wait_recv(self):
            self.describe(self.total, self.total, self.dev).wait_recv()

        def wait_send(self):
            self.describe(self.total, self.total, self.dev).wait_send()

    def remote(src, dst, dev):
        group = Group(dst)
        group.send(src, dst, dev)
        return group

    def ring(axis, o):
        return lax.rem(coords[axis] + o, 4)

    barrier = pltpu.get_barrier_semaphore()
    for o in range(1, NT):
        pl.semaphore_signal(barrier, inc=1, device_id=(z, lax.rem(t + o, NT)), device_id_type=MESH)
    for o in range(1, NZ):
        pl.semaphore_signal(barrier, inc=1, device_id=(lax.rem(z + o, NZ), t), device_id_type=MESH)

    zr, zl, zf = lax.rem(z + 1, NZ), lax.rem(z + 3, NZ), lax.rem(z + 2, NZ)
    loads = []
    for ci, g in enumerate((zf, zr, zl, z)):
        c = pltpu.make_async_copy(
            tl.at[:, pl.ds(pl.multiple_of(g * 32, 32), 32), :], tv.at[ci], lsem.at[ci]
        )
        c.start()
        loads.append(c)
    load_x = pltpu.make_async_copy(feat, xb.at[pl.ds(192, CELLS), :], lsem.at[4])
    load_w1 = pltpu.make_async_copy(w1h, w1, lsem.at[5])
    load_w2 = pltpu.make_async_copy(w2h, w2, lsem.at[6])
    load_x.start()
    load_w1.start()
    load_w2.start()

    wb[...] = onehot(lax.div(iota((256, 256), 0), 64) == lax.div(iota((256, 256), 1), 64))
    wq[...] = onehot(lax.div(iota((256, 128), 0), 64) == iota((256, 128), 1))

    def cell_sums(v):
        hi = v.astype(BF16)
        lo = (v - hi.astype(F32)).astype(BF16)
        both = mm(jnp.concatenate([hi, lo], axis=0), wq[...])
        total = None
        for j in range(8):
            s = both[32 * j:32 * (j + 1)] + both[256 + 32 * j:288 + 32 * j]
            total = pltpu.roll(s, 4 * j, 1) + total if j else s
        return total

    def pack_cells(v):
        out = v[0:8]
        for g in range(1, 4):
            out = out + pltpu.roll(v[8 * g:8 * (g + 1)], 32 * g, 1)
        return out

    def unpack_cells(v):
        low = iota((8, 128), 1) < 32
        return jnp.concatenate(
            [jnp.where(low, pltpu.roll(v, 128 - 32 * g, 1) if g else v, 0.0) for g in range(4)],
            axis=0,
        )

    def soft(ci, half, put):
        x = jnp.concatenate(
            [
                tv[ci, :, :, half * 2048 + 256 * j:half * 2048 + 256 * (j + 1)].reshape(128, 256)
                for j in range(8)
            ],
            axis=0,
        ).astype(F32)
        e4 = jnp.exp2(x * (math.log2(math.e) / 4.0))
        r = e4 / mm(e4.astype(BF16), wb[...])
        r2 = r * r
        e = (r2 * r2).astype(BF16)
        p = e.astype(F32) / mm(e, wb[...])
        p = p.reshape(8, 4, 32, 256)
        sq = p * p
        f = (p[:, 0] + p[:, 1]) + (p[:, 2] + p[:, 3])
        q = (sq[:, 0] + sq[:, 1]) + (sq[:, 2] + sq[:, 3])
        for j in range(8):
            put(j, f[j])
        return pack_cells(cell_sums(q.reshape(256, 256)))

    def put_to(*subs):
        def put(j, v):
            ref = subs[j // 4]
            ref[:, 256 * (j % 4):256 * (j % 4 + 1)] = v.astype(ref.dtype)

        return put

    fin = [None, None]
    relay = [None, None]

    def send_relay(h):
        relay[h] = (
            remote(rel_s.at[h, 0], rel_r.at[h, 0], (zr, t)),
            remote(rel_s.at[h, 1], rel_r.at[h, 1], (zl, t)),
        )
        fin[h] = Group(fin_l)

    def send_own(h, side):
        if side == 0:
            fin[h].send(fin_s.at[0, h, 1], fin_l.at[h, 1], (zr, t))
        else:
            fin[h].send(fin_s.at[1, h, 0], fin_r.at[h, 0], (zl, t))

    def soft_far(h):
        sec_s[h, 0] = soft(0, h, put_to(rel_s.at[h, 0], rel_s.at[h, 1]))

    def soft_right(h):
        sec_s[h, 1] = soft(1, h, put_to(part.at[h, 0], fin_s.at[0, h, 1]))

    def soft_left(h):
        sec_s[h, 2] = soft(2, h, put_to(fin_s.at[1, h, 0], part.at[h, 1]))

    def finish_relay(h):
        relay[h][0].wait_recv()
        fin_s[0, h, 0] = (part[h, 0] + rel_r[h, 0].astype(F32)).astype(BF16)
        fin[h].send(fin_s.at[0, h, 0], fin_l.at[h, 0], (zr, t))
        relay[h][1].wait_recv()
        fin_s[1, h, 1] = (part[h, 1] + rel_r[h, 1].astype(F32)).astype(BF16)
        fin[h].send(fin_s.at[1, h, 1], fin_r.at[h, 1], (zl, t))
        group = Group(sec_r.at[h])
        for i, to in enumerate((zf, zr, zl)):
            group.send(sec_s.at[h, i], sec_r.at[h, i], (to, t))
        return group

    loads[0].wait()
    soft_far(0)
    pl.semaphore_wait(barrier, NT - 1 + NZ - 1)
    send_relay(0)
    up, down = lax.rem(t + 1, NT), lax.rem(t + NT - 1, NT)
    halo = Group(xb.at[pl.ds(0, 384), :])
    halo.send(feat.at[pl.ds(CELLS - 192, 192), :], xb.at[pl.ds(0, 192), :], (z, up))
    halo.send(feat.at[pl.ds(0, 192), :], xb.at[pl.ds(192 + CELLS, 192), :], (z, down))
    loads[1].wait()
    soft_right(0)
    send_own(0, 0)
    loads[2].wait()
    soft_left(0)
    send_own(0, 1)
    soft_far(1)
    soft_right(1)
    soft_left(1)
    sec_c = [finish_relay(0), None]
    send_relay(1)
    send_own(1, 0)
    send_own(1, 1)
    loads[3].wait()
    sec_m = [soft(3, h, put_to(own.at[h, 0], own.at[h, 1])) for h in range(2)]

    crow = cov[...]
    i0, i1 = iota((128, 128), 0), iota((128, 128), 1)
    ccol = jnp.sum(jnp.where(i0 == i1, crow, 0), axis=1, keepdims=True)
    same = (ccol == crow) & (lax.div(i0, 32) == lax.div(i1, 32)) & (i0 < i1)
    rank = jnp.sum(jnp.where(same, 1, 0), axis=0, keepdims=True)
    slot = jnp.broadcast_to(crow * 2 + rank, (8, 128)).astype(F32)
    lane8 = iota((8, 128), 1)
    mine = jnp.zeros((8, 128), F32)
    for g in range(NZ):
        moved = slot if g == 0 else pltpu.roll(slot, 128 - 32 * g, 1)
        mine = jnp.where(z == g, moved, mine)
    mine = jnp.where(lane8 < 32, mine, 0.0)
    mine = mine + pltpu.roll(mine, 32, 1)
    mine = mine + pltpu.roll(mine, 64, 1)
    slots = mine[0:1, :]
    j0, j1 = iota((256, 128), 0), iota((256, 128), 1)
    pick_s[...] = onehot(
        (lax.div(j0, 4).astype(F32) == slots) & (lax.rem(j0, 4) == lax.div(j1, 32))
    )

    def shifted(v, by, lo_col, hi_col, rows):
        col = lax.rem(iota((rows, CH), 0), COLS)
        before = jnp.where(col >= by, pltpu.roll(v, by, 0), 0.0)
        after = jnp.where(col < COLS - by, pltpu.roll(v, rows - by, 0), 0.0)
        return before.astype(BF16), after.astype(BF16)

    load_x.wait()
    load_w1.wait()
    halo.wait_recv()

    def build_one(k, carry):
        s = pl.ds(pl.multiple_of(k * 128, 128), 128)
        row = t * ROWS - 3 + 2 * k + lax.div(iota((128, CH), 0), COLS)
        v = xb[s, :].astype(F32)
        v = jnp.where((row >= 0) & (row < NT * ROWS), v, 0.0)
        before, after = shifted(v, 1, 0, 0, 128)
        a1[s, 0:CH] = before
        a1[s, CH:2 * CH] = v.astype(BF16)
        a1[s, 2 * CH:3 * CH] = after
        return carry

    lax.fori_loop(0, 19, build_one, 0)

    def conv_rows(a_ref, w_ref, start, rows, stride):
        total = None
        for a in range(3):
            s = pl.ds(pl.multiple_of(start + a * stride, 64), rows)
            d = mm(a_ref[s, :], w_ref[a])
            total = d if total is None else total + d
        return total

    def conv_one(k, carry):
        n = 256
        start = k * n
        pre = conv_rows(a1, w1, start, n, COLS)
        row = t * ROWS - 2 + 4 * k + lax.div(iota((n, CH), 0), COLS)
        h = jnp.where((row >= 0) & (row < NT * ROWS) & (pre > 0), pre, 0.0)
        h = h.astype(BF16).astype(F32)
        before, after = shifted(h, 2, 0, 0, n)
        s = pl.ds(pl.multiple_of(start, n), n)
        a2[s, 0:CH] = before
        a2[s, CH:2 * CH] = h.astype(BF16)
        a2[s, 2 * CH:3 * CH] = after
        a1e[:, s] = a1[pl.ds(pl.multiple_of(128 + start, 128), n), :].T
        odd = jnp.minimum(k, 7) * n
        a1o[:, pl.ds(pl.multiple_of(odd, n), n)] = a1[pl.ds(pl.multiple_of(192 + odd, 64), n), :].T
        return carry

    def send_tiles(h):
        fin[h].wait_recv()
        sec_c[h].wait_recv()
        squares = []
        for j in range(8):
            s = slice(256 * (j % 4), 256 * (j % 4 + 1))
            m = (
                own[h, j // 4, :, s] + fin_l[h, j // 4, :, s].astype(F32)
                + fin_r[h, j // 4, :, s].astype(F32)
            ) * (1.0 / 16.0)
            row = (j // 2) * 32
            mp[h, row:row + 32, (j % 2) * 256:(j % 2 + 1) * 256] = m.astype(BF16)
            squares.append(m * m)
        msq = cell_sums(jnp.concatenate(squares, axis=0))
        second = unpack_cells((sec_m[h] + sec_r[h, 0]) + (sec_r[h, 1] + sec_r[h, 2]))
        spread = second * (1.0 / 16.0) - msq
        lane = iota((32, 128), 1)
        slot_no = (iota((32, 128), 0) + 1).astype(F32)
        for a in range(4):
            sp = spread if a == 0 else pltpu.roll(spread, 128 - 8 * a, 1)
            sp = jnp.where(lane < 8, sp, 0.0)
            hi = sp.astype(BF16).astype(F32)
            mid = (sp - hi).astype(BF16).astype(F32)
            lo = sp - hi - mid
            ext = hi + pltpu.roll(mid, 8, 1) + pltpu.roll(lo, 16, 1)
            ext = jnp.where(lane == 24, slot_no, ext)
            mp[h, a * 32:(a + 1) * 32, 512:640] = ext.astype(BF16)
        sb[h] = mm(pick_s[...], mp[h]).astype(BF16).reshape(NT, 8, 640)
        group = Group(rb.at[h, pl.ds(0, NT - 1)])
        for o in range(1, NT):
            d = lax.rem(t + o, NT)
            group.send(sb.at[h, d], rb.at[h, t], (z, d))
        rb[h, t] = sb[h, t]
        return group

    exch = [send_tiles(0)]
    sec_c[1] = finish_relay(1)
    lax.fori_loop(0, 6, conv_one, 0)
    exch.append(send_tiles(1))
    lax.fori_loop(6, 9, conv_one, 0)


    load_w2.wait()

    def conv_two(k, carry):
        n = 256
        pre = conv_rows(a2, w2, k * n, n, 2 * COLS)
        h = jnp.where(pre > 0, pre, 0.0)
        s = pl.ds(pl.multiple_of(k * n, n), n)
        hf[0, s, :] = h[:, :128]
        hf[1, s, :] = h[:, 128:]
        a2t[:, s] = a2[s, :].T
        return carry

    lax.fori_loop(0, 8, conv_two, 0)
    a2t[:, CELLS:CELLS + 256] = a2[CELLS:CELLS + 256, :].T

    for a in range(3):
        for b in range(3):
            w2t[a, b * CH:(b + 1) * CH, :] = w2[a, (2 - b) * CH:(3 - b) * CH, :].T

    l_rep = onehot(lax.div(iota((256, 32), 0), 8) == iota((256, 32), 1))
    rep = mm(l_rep, lab[...].astype(F32).astype(BF16))
    rep = jnp.where(
        lax.div(iota((256, 64), 1), 8) == lax.rem(iota((256, 64), 0), 8), rep, 0.0
    ).astype(BF16)
    l_sel = onehot(lax.rem(iota((8, 64), 1), 8) == iota((8, 64), 0))
    labels = mm_dims(l_sel, rep, 1, 1)

    for c in exch:
        c.wait_recv()
    got = rb[...].reshape(512, 640)
    from_slot = got[:, 512:640].astype(F32)[:, 24:25]
    n0, n1 = iota((512, 256), 0), iota((512, 256), 1)
    tile_no = (lax.div(n1, 64) * 8 + lax.rem(n1, 8) + 1).astype(F32)
    place = onehot((from_slot == tile_no) & (lax.div(n0, 256) * 4 + lax.rem(n0, 4) == lax.rem(lax.div(n1, 8), 8)))
    mean_t[...] = mm_dims(got, place, 0, 0)

    scale = 1.0 / math.sqrt(NZ * NT * CELLS)
    head_w = wh[...]
    classes = iota((NCLS, 256), 0)
    loss = jnp.zeros((1, 256), F32)
    head_t = jnp.zeros((NCLS, CH), F32)
    for b in range(8):
        s = pl.ds(b, 256, stride=8)
        h32 = jnp.concatenate([hf[0, s, :], hf[1, s, :]], axis=1)
        hb = h32.astype(BF16)
        logits = mm_dims(head_w, hb, 1, 1)
        top = jnp.max(logits, axis=0, keepdims=True)
        low = logits - top
        log_s = low - jnp.log(jnp.sum(jnp.exp(low), axis=0, keepdims=True))
        prob = jnp.exp(log_s)
        mean = mean_t[b * 64:(b + 1) * 64, :]
        spr = mean_t[512 + b:513 + b, :] + mean_t[520 + b:521 + b, :] + mean_t[528 + b:529 + b, :]
        wgt = 1.0 / (0.1 + spr)
        hot = classes.astype(F32) == labels[b:b + 1, :]
        ent = jnp.where(mean > 0, mean * jnp.log(jnp.where(mean > 0, mean, 1.0)), 0.0)
        kl = jnp.sum(ent - mean * log_s, axis=0, keepdims=True)
        nll = jnp.sum(jnp.where(hot, log_s, 0.0), axis=0, keepdims=True)
        loss = loss + (wgt * kl - nll)
        lg = ((wgt * (prob - mean) + prob - jnp.where(hot, 1.0, 0.0)) * scale).astype(BF16)
        head_t = head_t + mm(lg, hb)
        hg = mm_dims(lg, head_w, 0, 0)
        g2 = jnp.where(h32 > 0, hg, 0.0)
        gf[0, s, :] = g2[:, :128]
        gf[1, s, :] = g2[:, 128:]

    def round_grad(k, carry):
        s = pl.ds(pl.multiple_of(k * 128, 128), 128)
        d = pl.ds(pl.multiple_of(128 + k * 128, 128), 128)
        gp[d, 0:128] = gf[0, s, :].astype(BF16)
        gp[d, 128:256] = gf[1, s, :].astype(BF16)
        return carry

    lax.fori_loop(0, 16, round_grad, 0)
    edge = Group(gp.at[pl.ds(0, 256), :])
    edge.send(gp.at[pl.ds(CELLS, 128), :], gp.at[pl.ds(0, 128), :], (z, up))
    edge.send(gp.at[pl.ds(128, 128), :], gp.at[pl.ds(128 + CELLS, 128), :], (z, down))

    small = {"head": jnp.concatenate([head_t[:, :128], head_t[:, 128:]], axis=0),
             "loss": jnp.broadcast_to(jnp.sum(loss, axis=1, keepdims=True), (8, 128))}

    def small_send(n, axis):
        me = coords[axis]
        hx[n, me] = small["head"].astype(BF16)
        lx[n, me] = small["loss"]
        size = 2 if axis == "c" else 4
        h, l = Group(hx.at[n, pl.ds(1, size - 1)]), Group(lx.at[n, pl.ds(1, size - 1)])
        small["wait"] = [h, l]
        for o in range(1, size):
            dev = peer(axis, lax.rem(me + o, size))
            h.send(hx.at[n, me], hx.at[n, me], dev)
            l.send(lx.at[n, me], lx.at[n, me], dev)

    def small_recv(n, axis):
        for c in small["wait"]:
            c.wait_recv()
        size = 2 if axis == "c" else 4
        h, l = hx[n, 0].astype(F32), lx[n, 0]
        for j in range(1, size):
            h = h + hx[n, j].astype(F32)
            l = l + lx[n, j]
        small["head"], small["loss"] = h, l

    orders = (("x", "y", "z"), ("y", "z", "x"), ("z", "x", "y"))

    class Piece:
        def __init__(self, index):
            self.refs = piece_refs[9 * index:9 * index + 9]
            self.rows = PIECES[index]
            self.n, self.at = (0, 0) if index == 0 else (1, 768 * (index - 1))
            self.group = Group(self.refs[1])

        def done(self):
            self.group.wait_recv()

        def spread(self, level, p, j):
            one, two = self.rows // 12, self.rows // 48
            if level == 1:
                return pl.ds(pl.multiple_of(4 * one * p + one * j, 16), one)
            first = one * coords[orders[p][0]]
            return pl.ds(pl.multiple_of(self.at + 4 * one * p + first + two * j, 16), two)

        def product(self, row, lhs, rhs):
            csb, crb, acc = self.refs[:3]
            d = mm(lhs, rhs)
            low, high = d[:, :128], d[:, 128:]
            acc[row:row + 768, :] = jnp.where(core == 0, low, high)
            csb[row:row + 768, :] = jnp.where(core == 0, high, low).astype(BF16)
            s = pl.ds(row, 768)
            self.group.send(csb.at[s, :], crb.at[s, :], peer("c", 1 - core))

        def s1(self):
            self.done()
            csb, crb, acc, s1b, r1 = self.refs[:5]

            def step(k, carry):
                s = pl.ds(pl.multiple_of(k * 256, 256), 256)
                v = acc[s, :] + crb[s, :].astype(F32)
                acc[s, :] = v
                s1b[s, :] = v.astype(BF16)
                return carry

            lax.fori_loop(0, self.rows // 256, step, 0)
            self.group = Group(r1.at[:, pl.ds(1, 3)])
            for o in (2, 1, 3):
                for p in range(3):
                    ax = orders[p][0]
                    j = ring(ax, o)
                    src = s1b.at[self.spread(1, p, j), :]
                    self.group.send(src, r1.at[p, o], peer(ax, j))

        def s2(self):
            self.done()
            acc, r1, a1c, s2b, r2 = self.refs[2], *self.refs[4:8]
            for p in range(3):
                v = acc[self.spread(1, p, coords[orders[p][0]]), :]
                for o in range(1, 4):
                    v = v + r1[p, o].astype(F32)
                a1c[p] = v
                s2b[p] = v.astype(BF16)
            two = self.rows // 48
            self.group = Group(r2.at[:, pl.ds(1, 3)])
            for o in (2, 1, 3):
                for p in range(3):
                    ax = orders[p][1]
                    j = ring(ax, o)
                    src = s2b.at[p, pl.ds(pl.multiple_of(two * j, 16), two), :]
                    self.group.send(src, r2.at[p, o], peer(ax, j))

        def s3(self):
            self.done()
            a1c, s2b, r2, x3 = self.refs[5:9]
            two = self.rows // 48
            for p in range(3):
                s = pl.ds(pl.multiple_of(two * coords[orders[p][1]], 16), two)
                v = a1c[p, s, :]
                for o in range(1, 4):
                    v = v + r2[p, o].astype(F32)
                x3[p, coords[orders[p][2]]] = v.astype(BF16)
            self.group = Group(x3.at[:, pl.ds(1, 3)])
            for o in (2, 1, 3):
                for p in range(3):
                    ax = orders[p][2]
                    ref = x3.at[p, coords[ax]]
                    self.group.send(ref, ref, peer(ax, ring(ax, o)))

        def g2(self):
            self.done()
            x3 = self.refs[8]
            for p in range(3):
                v = x3[p, 0].astype(F32)
                for j in range(1, 4):
                    v = v + x3[p, j].astype(F32)
                gat[self.n, core, self.spread(2, p, coords[orders[p][1]]), :] = v.astype(BF16)
            self.group = Group(x3.at[:, pl.ds(1, 3)])
            for o in (2, 1, 3):
                for p in range(3):
                    ax = orders[p][1]
                    ref = gat.at[self.n, core, self.spread(2, p, coords[ax]), :]
                    self.group.send(ref, ref, peer(ax, ring(ax, o)))

        def g1(self):
            self.done()
            one = self.rows // 12
            self.group = Group(self.refs[4].at[:, pl.ds(1, 3)])
            for o in (2, 1, 3):
                for p in range(3):
                    ax = orders[p][0]
                    s = pl.ds(pl.multiple_of(self.at + 4 * one * p + one * coords[ax], 16), one)
                    ref = gat.at[self.n, core, s, :]
                    self.group.send(ref, ref, peer(ax, ring(ax, o)))

        def gc(self):
            self.done()
            ref = gat.at[self.n, core, pl.ds(self.at, self.rows), :]
            self.group = remote(ref, ref, peer("c", 1 - core))

        def store(self):
            self.done()
            out = (o2, o1)[self.n]
            s = pl.ds(self.at, self.rows)
            for h in range(2):
                c = pltpu.make_async_copy(
                    gat.at[self.n, h, s, :], out.at[s, pl.ds(128 * h, 128)], lsem.at[7 + len(outs)]
                )
                c.start()
                outs.append(c)

    outs = []
    second = Piece(0)
    firsts = [Piece(1), Piece(2), Piece(3)]

    small_send(0, "c")
    grad_two = gp[128:128 + CELLS, :]
    for a in range(3):
        second.product(768 * a, a2t[:, 128 * a:128 * a + CELLS], grad_two)
    small_recv(0, "c")
    small_send(1, "x")

    edge.wait_recv()

    def build_grad(k, carry):
        s = pl.ds(pl.multiple_of(k * 128, 128), 128)
        row = t * ROWS - 2 + 2 * k + lax.div(iota((128, CH), 0), COLS)
        v = jnp.where((row >= 0) & (row < NT * ROWS), gp[s, :].astype(F32), 0.0)
        before, after = shifted(v, 2, 0, 0, 128)
        ag[s, 0:CH] = before
        ag[s, CH:2 * CH] = v.astype(BF16)
        ag[s, 2 * CH:3 * CH] = after
        return carry

    lax.fori_loop(0, 18, build_grad, 0)
    second.s1()

    def back(k, carry):
        n = 256
        total = None
        for a in range(3):
            s = pl.ds(pl.multiple_of(k * n + (2 - a) * 2 * COLS, 128), n)
            d = mm(ag[s, :], w2t[a])
            total = d if total is None else total + d
        h = a2[pl.ds(pl.multiple_of(128 + k * n, 128), n), CH:2 * CH].astype(F32)
        v = jnp.where(h > 0, total, 0.0).astype(BF16)
        xb[pl.ds(pl.multiple_of(k * n, n), n), :] = v
        return carry

    lax.fori_loop(0, 4, back, 0)
    small_recv(1, "x")
    small_send(2, "y")
    lax.fori_loop(4, 8, back, 0)
    second.s2()
    grad_one = xb[0:CELLS, :]
    firsts[0].product(0, a1e[:, 0:CELLS], grad_one)
    small_recv(2, "y")
    small_send(3, "z")
    firsts[1].product(0, a1o[...], grad_one)
    firsts[0].s1()
    firsts[2].product(0, a1e[:, 128:128 + CELLS], grad_one)
    second.s3()
    firsts[1].s1()
    firsts[2].s1()
    second.g2()
    small_recv(3, "z")
    for c in firsts:
        c.s2()
    second.g1()
    for c in firsts:
        c.s3()
    second.gc()
    ohead[:, 0:128] = small["head"][:64]
    ohead[:, 128:256] = small["head"][64:]
    oloss[...] = small["loss"]
    for c in firsts:
        c.g2()
    second.store()
    for c in firsts:
        c.g1()
    for c in firsts:
        c.gc()
    for c in firsts:
        c.store()
    for c in groups:
        c.wait_send()
    for c in outs:
        c.wait()


def widen(first, second, head, loss, out_first, out_second, out_head, out_loss):
    out_first[...] = first[...].astype(F32)
    out_second[...] = second[...].astype(F32)
    out_head[...] = head[...]
    out_loss[...] = loss[0:1, 0:1] * (1.0 / (NZ * NT * CELLS))


def body(teacher_logits, coverage, features, labels, first_weight, second_weight, head_weight):
    any_spec = pl.BlockSpec(memory_space=pl.ANY)
    vmem = pl.BlockSpec(memory_space=pltpu.VMEM)
    out = [
        jax.ShapeDtypeStruct((2304, 256), BF16),
        jax.ShapeDtypeStruct((2304, 256), BF16),
        jax.ShapeDtypeStruct((NCLS, CH), F32),
        jax.ShapeDtypeStruct((8, 128), F32),
    ]
    V = pltpu.VMEM
    scratch = [
        V((4, 4, 32, 4096), BF16),
        V((2432, CH), BF16),
        V((2432, 3 * CH), BF16),
        V((3 * CH, 2304), BF16),
        V((3 * CH, 2048), BF16),
        V((2304, 3 * CH), BF16),
        V((3 * CH, 2304), BF16),
        V((2304, 3 * CH), BF16),
        V((2304, CH), BF16),
        V((3, 3 * CH, CH), BF16),
        V((3, 3 * CH, CH), BF16),
        V((3, 3 * CH, CH), BF16),
        V((2, CELLS, 128), F32),
        V((2, CELLS, 128), F32),
        V((2, 2, 2304, 128), BF16),
        V((2, 2, 32, 1024), BF16),
        V((2, 2, 32, 1024), BF16),
        V((2, 2, 2, 32, 1024), BF16),
        V((2, 2, 32, 1024), BF16),
        V((2, 2, 32, 1024), BF16),
        V((2, 2, 32, 1024), F32),
        V((2, 2, 32, 1024), F32),
        V((2, 3, 8, 128), F32),
        V((2, 3, 8, 128), F32),
        V((2, 128, 640), BF16),
        V((2, NT, 8, 640), BF16),
        V((2, NT, 8, 640), BF16),
        V((640, 256), F32),
        V((4, 4, 128, 128), BF16),
        V((4, 4, 8, 128), F32),
        V((256, 256), BF16),
        V((256, 128), BF16),
        V((256, 128), BF16),
        pltpu.SemaphoreType.DMA((NSEM,)),
        pltpu.SemaphoreType.DMA((NSEM,)),
        pltpu.SemaphoreType.DMA((16,)),
    ]
    for rows in PIECES:
        scratch += [
            V((rows, 128), BF16),
            V((rows, 128), BF16),
            V((rows, 128), F32),
            V((rows, 128), BF16),
            V((3, 4, rows // 12, 128), BF16),
            V((3, rows // 12, 128), F32),
            V((3, rows // 12, 128), BF16),
            V((3, 4, rows // 48, 128), BF16),
            V((3, 4, rows // 48, 128), BF16),
        ]
    first, second, head, loss = pl.pallas_call(
        kernel,
        out_shape=out,
        in_specs=[any_spec, vmem, any_spec, vmem, any_spec, any_spec, vmem],
        out_specs=[any_spec, any_spec, vmem, vmem],
        scratch_shapes=scratch,
        compiler_params=pltpu.CompilerParams(
            collective_id=0, has_side_effects=True, vmem_limit_bytes=67043328
        ),
    )(
        teacher_logits,
        coverage.reshape(1, 128),
        features.reshape(CELLS, CH),
        labels.reshape(ROWS, COLS),
        first_weight.reshape(3, 3 * CH, CH),
        second_weight.reshape(3, 3 * CH, CH),
        head_weight.T,
    )
    steps, rows = 4, 2304 // 4
    big = pl.BlockSpec((rows, CH), lambda i: (i, 0))
    first, second, head, loss = pl.pallas_call(
        widen,
        grid=(steps,),
        out_shape=[
            jax.ShapeDtypeStruct((2304, CH), F32),
            jax.ShapeDtypeStruct((2304, CH), F32),
            jax.ShapeDtypeStruct((NCLS, CH), F32),
            jax.ShapeDtypeStruct((1, 1), F32),
        ],
        in_specs=[
            big, big, pl.BlockSpec((NCLS, CH), lambda i: (0, 0)), pl.BlockSpec((8, 128), lambda i: (0, 0))
        ],
        out_specs=[
            big, big, pl.BlockSpec((NCLS, CH), lambda i: (0, 0)), pl.BlockSpec((1, 1), lambda i: (0, 0))
        ],
    )(first, second, head, loss)
    return (
        first.reshape(3, 3, CH, CH), second.reshape(3, 3, CH, CH), head.T, loss.reshape(())
    )


def solution(mesh):
    return jax.shard_map(
        body,
        mesh=mesh,
        in_specs=(
            P("member", "tile", None),
            P("tile"),
            P("member", "tile", None, None),
            P("member", "tile", None),
            P(),
            P(),
            P(),
        ),
        out_specs=(P(), P(), P(), P()),
        check_vma=False,
    )
```

```python
import math

import jax
import jax.numpy as jnp
from jax import lax
from jax.experimental import pallas as pl
from jax.experimental.pallas import tpu as pltpu
from jax.sharding import PartitionSpec as P

F32 = jnp.float32
BF16 = jnp.bfloat16
I32 = jnp.int32
MESH = pl.DeviceIdType.MESH

CH = 256
NCLS = 64
NZ = 4
NT = 32
ROWS = 32
COLS = 64
CELLS = ROWS * COLS
NSEM = 41
PIECES = (2304, 1536, 768)


def iota(shape, dim):
    return lax.broadcasted_iota(I32, shape, dim)


def onehot(mask):
    return jnp.where(mask, 1.0, 0.0).astype(BF16)


def mm(a, b):
    return jnp.dot(a, b, preferred_element_type=F32)


def mm_dims(a, b, ca, cb):
    return lax.dot_general(a, b, (((ca,), (cb,)), ((), ())), preferred_element_type=F32)


def kernel(
    tl, cov, feat, lab, w1h, w2h, wh,
    o1, o2, ohead, oloss,
    tv, xb, a1, a1e, a1o, a2, a2t, ag, gp, w1, w2, w2t, hf, gf, gat,
    rel_s, rel_r, fin_s, fin_l, fin_r, own, part, sec_s, sec_r,
    mp, sb, rb, mean_t, hx, lx, wb, wq, pick_s,
    ssem, rsem, lsem, *piece_refs,
):
    z = lax.axis_index("member")
    t = lax.axis_index("tile")
    core = lax.rem(t, 2)
    xc = lax.rem(lax.div(t, 2), 4)
    yc = lax.div(t, 8)
    coords = {"x": xc, "y": yc, "z": z, "c": core}

    def peer(axis, j):
        if axis == "z":
            return (j, t)
        if axis == "x":
            return (z, yc * 8 + j * 2 + core)
        if axis == "y":
            return (z, j * 8 + xc * 2 + core)
        return (z, yc * 8 + xc * 2 + j)

    groups = []

    class Group:
        def __init__(self, total):
            self.total, self.index = total, len(groups)
            groups.append(self)

        def describe(self, src, dst, dev):
            return pltpu.make_async_remote_copy(
                src_ref=src, dst_ref=dst, send_sem=ssem.at[self.index],
                recv_sem=rsem.at[self.index], device_id=dev, device_id_type=MESH,
            )

        def send(self, src, dst, dev):
            self.dev = dev
            self.describe(src, dst, dev).start()

        def wait_recv(self):
            self.describe(self.total, self.total, self.dev).wait_recv()

        def wait_send(self):
            self.describe(self.total, self.total, self.dev).wait_send()

    def remote(src, dst, dev):
        group = Group(dst)
        group.send(src, dst, dev)
        return group

    def ring(axis, o):
        return lax.rem(coords[axis] + o, 4)

    barrier = pltpu.get_barrier_semaphore()
    for o in range(1, NT):
        pl.semaphore_signal(barrier, inc=1, device_id=(z, lax.rem(t + o, NT)), device_id_type=MESH)
    for o in range(1, NZ):
        pl.semaphore_signal(barrier, inc=1, device_id=(lax.rem(z + o, NZ), t), device_id_type=MESH)

    zr, zl, zf = lax.rem(z + 1, NZ), lax.rem(z + 3, NZ), lax.rem(z + 2, NZ)
    loads = []
    for ci, g in enumerate((zf, zr, zl, z)):
        c = pltpu.make_async_copy(
            tl.at[:, pl.ds(pl.multiple_of(g * 32, 32), 32), :], tv.at[ci], lsem.at[ci]
        )
        c.start()
        loads.append(c)
    load_x = pltpu.make_async_copy(feat, xb.at[pl.ds(192, CELLS), :], lsem.at[4])
    load_w1 = pltpu.make_async_copy(w1h, w1, lsem.at[5])
    load_w2 = pltpu.make_async_copy(w2h, w2, lsem.at[6])
    load_x.start()
    load_w1.start()
    load_w2.start()

    wb[...] = onehot(lax.div(iota((256, 256), 0), 64) == lax.div(iota((256, 256), 1), 64))
    wq[...] = onehot(lax.div(iota((256, 128), 0), 64) == iota((256, 128), 1))

    def cell_sums(v):
        hi = v.astype(BF16)
        lo = (v - hi.astype(F32)).astype(BF16)
        both = mm(jnp.concatenate([hi, lo], axis=0), wq[...])
        total = None
        for j in range(8):
            s = both[32 * j:32 * (j + 1)] + both[256 + 32 * j:288 + 32 * j]
            total = pltpu.roll(s, 4 * j, 1) + total if j else s
        return total

    def pack_cells(v):
        out = v[0:8]
        for g in range(1, 4):
            out = out + pltpu.roll(v[8 * g:8 * (g + 1)], 32 * g, 1)
        return out

    def unpack_cells(v):
        low = iota((8, 128), 1) < 32
        return jnp.concatenate(
            [jnp.where(low, pltpu.roll(v, 128 - 32 * g, 1) if g else v, 0.0) for g in range(4)],
            axis=0,
        )

    def soft(ci, half, put):
        x = jnp.concatenate(
            [
                tv[ci, :, :, half * 2048 + 256 * j:half * 2048 + 256 * (j + 1)].reshape(128, 256)
                for j in range(8)
            ],
            axis=0,
        ).astype(F32)
        e4 = jnp.exp2(x * (math.log2(math.e) / 4.0))
        r = e4 / mm(e4.astype(BF16), wb[...])
        r2 = r * r
        e = (r2 * r2).astype(BF16)
        p = e.astype(F32) / mm(e, wb[...])
        p = p.reshape(8, 4, 32, 256)
        sq = p * p
        f = (p[:, 0] + p[:, 1]) + (p[:, 2] + p[:, 3])
        q = (sq[:, 0] + sq[:, 1]) + (sq[:, 2] + sq[:, 3])
        for j in range(8):
            put(j, f[j])
        return pack_cells(cell_sums(q.reshape(256, 256)))

    def put_to(*subs):
        def put(j, v):
            ref = subs[j // 4]
            ref[:, 256 * (j % 4):256 * (j % 4 + 1)] = v.astype(ref.dtype)

        return put

    fin = [None, None]
    relay = [None, None]

    def send_relay(h):
        relay[h] = (
            remote(rel_s.at[h, 0], rel_r.at[h, 0], (zr, t)),
            remote(rel_s.at[h, 1], rel_r.at[h, 1], (zl, t)),
        )
        fin[h] = Group(fin_l)

    def send_own(h, side):
        if side == 0:
            fin[h].send(fin_s.at[0, h, 1], fin_l.at[h, 1], (zr, t))
        else:
            fin[h].send(fin_s.at[1, h, 0], fin_r.at[h, 0], (zl, t))

    def soft_far(h):
        sec_s[h, 0] = soft(0, h, put_to(rel_s.at[h, 0], rel_s.at[h, 1]))

    def soft_right(h):
        sec_s[h, 1] = soft(1, h, put_to(part.at[h, 0], fin_s.at[0, h, 1]))

    def soft_left(h):
        sec_s[h, 2] = soft(2, h, put_to(fin_s.at[1, h, 0], part.at[h, 1]))

    def finish_relay(h):
        relay[h][0].wait_recv()
        fin_s[0, h, 0] = (part[h, 0] + rel_r[h, 0].astype(F32)).astype(BF16)
        fin[h].send(fin_s.at[0, h, 0], fin_l.at[h, 0], (zr, t))
        relay[h][1].wait_recv()
        fin_s[1, h, 1] = (part[h, 1] + rel_r[h, 1].astype(F32)).astype(BF16)
        fin[h].send(fin_s.at[1, h, 1], fin_r.at[h, 1], (zl, t))
        group = Group(sec_r.at[h])
        for i, to in enumerate((zf, zr, zl)):
            group.send(sec_s.at[h, i], sec_r.at[h, i], (to, t))
        return group

    loads[0].wait()
    soft_far(0)
    pl.semaphore_wait(barrier, NT - 1 + NZ - 1)
    send_relay(0)
    up, down = lax.rem(t + 1, NT), lax.rem(t + NT - 1, NT)
    halo = Group(xb.at[pl.ds(0, 384), :])
    halo.send(feat.at[pl.ds(CELLS - 192, 192), :], xb.at[pl.ds(0, 192), :], (z, up))
    halo.send(feat.at[pl.ds(0, 192), :], xb.at[pl.ds(192 + CELLS, 192), :], (z, down))
    loads[1].wait()
    soft_right(0)
    send_own(0, 0)
    loads[2].wait()
    soft_left(0)
    send_own(0, 1)
    soft_far(1)
    soft_right(1)
    soft_left(1)
    sec_c = [finish_relay(0), None]
    send_relay(1)
    send_own(1, 0)
    send_own(1, 1)
    loads[3].wait()
    sec_m = [soft(3, h, put_to(own.at[h, 0], own.at[h, 1])) for h in range(2)]

    crow = cov[...]
    i0, i1 = iota((128, 128), 0), iota((128, 128), 1)
    ccol = jnp.sum(jnp.where(i0 == i1, crow, 0), axis=1, keepdims=True)
    same = (ccol == crow) & (lax.div(i0, 32) == lax.div(i1, 32)) & (i0 < i1)
    rank = jnp.sum(jnp.where(same, 1, 0), axis=0, keepdims=True)
    slot = jnp.broadcast_to(crow * 2 + rank, (8, 128)).astype(F32)
    lane8 = iota((8, 128), 1)
    mine = jnp.zeros((8, 128), F32)
    for g in range(NZ):
        moved = slot if g == 0 else pltpu.roll(slot, 128 - 32 * g, 1)
        mine = jnp.where(z == g, moved, mine)
    mine = jnp.where(lane8 < 32, mine, 0.0)
    mine = mine + pltpu.roll(mine, 32, 1)
    mine = mine + pltpu.roll(mine, 64, 1)
    slots = mine[0:1, :]
    j0, j1 = iota((256, 128), 0), iota((256, 128), 1)
    pick_s[...] = onehot(
        (lax.div(j0, 4).astype(F32) == slots) & (lax.rem(j0, 4) == lax.div(j1, 32))
    )

    def shifted(v, by, lo_col, hi_col, rows):
        col = lax.rem(iota((rows, CH), 0), COLS)
        before = jnp.where(col >= by, pltpu.roll(v, by, 0), 0.0)
        after = jnp.where(col < COLS - by, pltpu.roll(v, rows - by, 0), 0.0)
        return before.astype(BF16), after.astype(BF16)

    load_x.wait()
    load_w1.wait()
    halo.wait_recv()

    def build_one(k, carry):
        s = pl.ds(pl.multiple_of(k * 128, 128), 128)
        row = t * ROWS - 3 + 2 * k + lax.div(iota((128, CH), 0), COLS)
        v = xb[s, :].astype(F32)
        v = jnp.where((row >= 0) & (row < NT * ROWS), v, 0.0)
        before, after = shifted(v, 1, 0, 0, 128)
        a1[s, 0:CH] = before
        a1[s, CH:2 * CH] = v.astype(BF16)
        a1[s, 2 * CH:3 * CH] = after
        return carry

    lax.fori_loop(0, 19, build_one, 0)

    def conv_rows(a_ref, w_ref, start, rows, stride):
        total = None
        for a in range(3):
            s = pl.ds(pl.multiple_of(start + a * stride, 64), rows)
            d = mm(a_ref[s, :], w_ref[a])
            total = d if total is None else total + d
        return total

    def conv_one(k, carry):
        n = 256
        start = k * n
        pre = conv_rows(a1, w1, start, n, COLS)
        row = t * ROWS - 2 + 4 * k + lax.div(iota((n, CH), 0), COLS)
        h = jnp.where((row >= 0) & (row < NT * ROWS) & (pre > 0), pre, 0.0)
        h = h.astype(BF16).astype(F32)
        before, after = shifted(h, 2, 0, 0, n)
        s = pl.ds(pl.multiple_of(start, n), n)
        a2[s, 0:CH] = before
        a2[s, CH:2 * CH] = h.astype(BF16)
        a2[s, 2 * CH:3 * CH] = after
        a1e[:, s] = a1[pl.ds(pl.multiple_of(128 + start, 128), n), :].T
        odd = jnp.minimum(k, 7) * n
        a1o[:, pl.ds(pl.multiple_of(odd, n), n)] = a1[pl.ds(pl.multiple_of(192 + odd, 64), n), :].T
        return carry

    def send_tiles(h):
        fin[h].wait_recv()
        sec_c[h].wait_recv()
        squares = []
        for j in range(8):
            s = slice(256 * (j % 4), 256 * (j % 4 + 1))
            m = (
                own[h, j // 4, :, s] + fin_l[h, j // 4, :, s].astype(F32)
                + fin_r[h, j // 4, :, s].astype(F32)
            ) * (1.0 / 16.0)
            row = (j // 2) * 32
            mp[h, row:row + 32, (j % 2) * 256:(j % 2 + 1) * 256] = m.astype(BF16)
            squares.append(m * m)
        msq = cell_sums(jnp.concatenate(squares, axis=0))
        second = unpack_cells((sec_m[h] + sec_r[h, 0]) + (sec_r[h, 1] + sec_r[h, 2]))
        spread = second * (1.0 / 16.0) - msq
        lane = iota((32, 128), 1)
        slot_no = (iota((32, 128), 0) + 1).astype(F32)
        for a in range(4):
            sp = spread if a == 0 else pltpu.roll(spread, 128 - 8 * a, 1)
            sp = jnp.where(lane < 8, sp, 0.0)
            hi = sp.astype(BF16).astype(F32)
            mid = (sp - hi).astype(BF16).astype(F32)
            lo = sp - hi - mid
            ext = hi + pltpu.roll(mid, 8, 1) + pltpu.roll(lo, 16, 1)
            ext = jnp.where(lane == 24, slot_no, ext)
            mp[h, a * 32:(a + 1) * 32, 512:640] = ext.astype(BF16)
        sb[h] = mm(pick_s[...], mp[h]).astype(BF16).reshape(NT, 8, 640)
        group = Group(rb.at[h, pl.ds(0, NT - 1)])
        for o in range(1, NT):
            d = lax.rem(t + o, NT)
            group.send(sb.at[h, d], rb.at[h, t], (z, d))
        rb[h, t] = sb[h, t]
        return group

    exch = [send_tiles(0)]
    sec_c[1] = finish_relay(1)
    lax.fori_loop(0, 6, conv_one, 0)
    exch.append(send_tiles(1))
    lax.fori_loop(6, 9, conv_one, 0)


    load_w2.wait()

    def conv_two(k, carry):
        n = 512
        pre = conv_rows(a2, w2, k * n, n, 2 * COLS)
        h = jnp.where(pre > 0, pre, 0.0)
        s = pl.ds(pl.multiple_of(k * n, n), n)
        hf[0, s, :] = h[:, :128]
        hf[1, s, :] = h[:, 128:]
        a2t[:, s] = a2[s, :].T
        return carry

    lax.fori_loop(0, 4, conv_two, 0)
    a2t[:, CELLS:CELLS + 256] = a2[CELLS:CELLS + 256, :].T

    for a in range(3):
        for b in range(3):
            w2t[a, b * CH:(b + 1) * CH, :] = w2[a, (2 - b) * CH:(3 - b) * CH, :].T

    l_rep = onehot(lax.div(iota((256, 32), 0), 8) == iota((256, 32), 1))
    rep = mm(l_rep, lab[...].astype(F32).astype(BF16))
    rep = jnp.where(
        lax.div(iota((256, 64), 1), 8) == lax.rem(iota((256, 64), 0), 8), rep, 0.0
    ).astype(BF16)
    l_sel = onehot(lax.rem(iota((8, 64), 1), 8) == iota((8, 64), 0))
    labels = mm_dims(l_sel, rep, 1, 1)

    for c in exch:
        c.wait_recv()
    got = rb[...].reshape(512, 640)
    from_slot = got[:, 512:640].astype(F32)[:, 24:25]
    n0, n1 = iota((512, 256), 0), iota((512, 256), 1)
    tile_no = (lax.div(n1, 64) * 8 + lax.rem(n1, 8) + 1).astype(F32)
    place = onehot((from_slot == tile_no) & (lax.div(n0, 256) * 4 + lax.rem(n0, 4) == lax.rem(lax.div(n1, 8), 8)))
    mean_t[...] = mm_dims(got, place, 0, 0)

    scale = 1.0 / math.sqrt(NZ * NT * CELLS)
    head_w = wh[...]
    classes = iota((NCLS, 256), 0)
    loss = jnp.zeros((1, 256), F32)
    head_t = jnp.zeros((NCLS, CH), F32)
    for b in range(8):
        s = pl.ds(b, 256, stride=8)
        h32 = jnp.concatenate([hf[0, s, :], hf[1, s, :]], axis=1)
        hb = h32.astype(BF16)
        logits = mm_dims(head_w, hb, 1, 1)
        top = jnp.max(logits, axis=0, keepdims=True)
        low = logits - top
        log_s = low - jnp.log(jnp.sum(jnp.exp(low), axis=0, keepdims=True))
        prob = jnp.exp(log_s)
        mean = mean_t[b * 64:(b + 1) * 64, :]
        spr = mean_t[512 + b:513 + b, :] + mean_t[520 + b:521 + b, :] + mean_t[528 + b:529 + b, :]
        wgt = 1.0 / (0.1 + spr)
        hot = classes.astype(F32) == labels[b:b + 1, :]
        ent = jnp.where(mean > 0, mean * jnp.log(jnp.where(mean > 0, mean, 1.0)), 0.0)
        kl = jnp.sum(ent - mean * log_s, axis=0, keepdims=True)
        nll = jnp.sum(jnp.where(hot, log_s, 0.0), axis=0, keepdims=True)
        loss = loss + (wgt * kl - nll)
        lg = ((wgt * (prob - mean) + prob - jnp.where(hot, 1.0, 0.0)) * scale).astype(BF16)
        head_t = head_t + mm(lg, hb)
        hg = mm_dims(lg, head_w, 0, 0)
        g2 = jnp.where(h32 > 0, hg, 0.0)
        gf[0, s, :] = g2[:, :128]
        gf[1, s, :] = g2[:, 128:]

    def round_grad(k, carry):
        s = pl.ds(pl.multiple_of(k * 128, 128), 128)
        d = pl.ds(pl.multiple_of(128 + k * 128, 128), 128)
        gp[d, 0:128] = gf[0, s, :].astype(BF16)
        gp[d, 128:256] = gf[1, s, :].astype(BF16)
        return carry

    lax.fori_loop(0, 16, round_grad, 0)
    edge = Group(gp.at[pl.ds(0, 256), :])
    edge.send(gp.at[pl.ds(CELLS, 128), :], gp.at[pl.ds(0, 128), :], (z, up))
    edge.send(gp.at[pl.ds(128, 128), :], gp.at[pl.ds(128 + CELLS, 128), :], (z, down))

    small = {"head": jnp.concatenate([head_t[:, :128], head_t[:, 128:]], axis=0),
             "loss": jnp.broadcast_to(jnp.sum(loss, axis=1, keepdims=True), (8, 128))}

    def small_send(n, axis):
        me = coords[axis]
        hx[n, me] = small["head"].astype(BF16)
        lx[n, me] = small["loss"]
        size = 2 if axis == "c" else 4
        h, l = Group(hx.at[n, pl.ds(1, size - 1)]), Group(lx.at[n, pl.ds(1, size - 1)])
        small["wait"] = [h, l]
        for o in range(1, size):
            dev = peer(axis, lax.rem(me + o, size))
            h.send(hx.at[n, me], hx.at[n, me], dev)
            l.send(lx.at[n, me], lx.at[n, me], dev)

    def small_recv(n, axis):
        for c in small["wait"]:
            c.wait_recv()
        size = 2 if axis == "c" else 4
        h, l = hx[n, 0].astype(F32), lx[n, 0]
        for j in range(1, size):
            h = h + hx[n, j].astype(F32)
            l = l + lx[n, j]
        small["head"], small["loss"] = h, l

    orders = (("x", "y", "z"), ("y", "z", "x"), ("z", "x", "y"))

    class Piece:
        def __init__(self, index):
            self.refs = piece_refs[9 * index:9 * index + 9]
            self.rows = PIECES[index]
            self.n, self.at = ((0, 0), (1, 0), (1, 1536))[index]
            self.group = Group(self.refs[1])

        def done(self):
            self.group.wait_recv()

        def spread(self, level, p, j):
            one, two = self.rows // 12, self.rows // 48
            if level == 1:
                return pl.ds(pl.multiple_of(4 * one * p + one * j, 16), one)
            first = one * coords[orders[p][0]]
            return pl.ds(pl.multiple_of(self.at + 4 * one * p + first + two * j, 16), two)

        def product(self, row, lhs, rhs):
            csb, crb, acc = self.refs[:3]
            d = mm(lhs, rhs)
            low, high = d[:, :128], d[:, 128:]
            acc[row:row + 768, :] = jnp.where(core == 0, low, high)
            csb[row:row + 768, :] = jnp.where(core == 0, high, low).astype(BF16)
            s = pl.ds(row, 768)
            self.group.send(csb.at[s, :], crb.at[s, :], peer("c", 1 - core))

        def s1(self):
            self.done()
            csb, crb, acc, s1b, r1 = self.refs[:5]

            def step(k, carry):
                s = pl.ds(pl.multiple_of(k * 256, 256), 256)
                v = acc[s, :] + crb[s, :].astype(F32)
                acc[s, :] = v
                s1b[s, :] = v.astype(BF16)
                return carry

            lax.fori_loop(0, self.rows // 256, step, 0)
            self.group = Group(r1.at[:, pl.ds(1, 3)])
            for o in (2, 1, 3):
                for p in range(3):
                    ax = orders[p][0]
                    j = ring(ax, o)
                    src = s1b.at[self.spread(1, p, j), :]
                    self.group.send(src, r1.at[p, o], peer(ax, j))

        def s2(self):
            self.done()
            acc, r1, a1c, s2b, r2 = self.refs[2], *self.refs[4:8]
            for p in range(3):
                v = acc[self.spread(1, p, coords[orders[p][0]]), :]
                for o in range(1, 4):
                    v = v + r1[p, o].astype(F32)
                a1c[p] = v
                s2b[p] = v.astype(BF16)
            two = self.rows // 48
            self.group = Group(r2.at[:, pl.ds(1, 3)])
            for o in (2, 1, 3):
                for p in range(3):
                    ax = orders[p][1]
                    j = ring(ax, o)
                    src = s2b.at[p, pl.ds(pl.multiple_of(two * j, 16), two), :]
                    self.group.send(src, r2.at[p, o], peer(ax, j))

        def s3(self):
            self.done()
            a1c, s2b, r2, x3 = self.refs[5:9]
            two = self.rows // 48
            for p in range(3):
                s = pl.ds(pl.multiple_of(two * coords[orders[p][1]], 16), two)
                v = a1c[p, s, :]
                for o in range(1, 4):
                    v = v + r2[p, o].astype(F32)
                x3[p, coords[orders[p][2]]] = v.astype(BF16)
            self.group = Group(x3.at[:, pl.ds(1, 3)])
            for o in (2, 1, 3):
                for p in range(3):
                    ax = orders[p][2]
                    ref = x3.at[p, coords[ax]]
                    self.group.send(ref, ref, peer(ax, ring(ax, o)))

        def g2(self):
            self.done()
            x3 = self.refs[8]
            for p in range(3):
                v = x3[p, 0].astype(F32)
                for j in range(1, 4):
                    v = v + x3[p, j].astype(F32)
                gat[self.n, core, self.spread(2, p, coords[orders[p][1]]), :] = v.astype(BF16)
            self.group = Group(x3.at[:, pl.ds(1, 3)])
            for o in (2, 1, 3):
                for p in range(3):
                    ax = orders[p][1]
                    ref = gat.at[self.n, core, self.spread(2, p, coords[ax]), :]
                    self.group.send(ref, ref, peer(ax, ring(ax, o)))

        def g1(self):
            self.done()
            one = self.rows // 12
            self.group = Group(self.refs[4].at[:, pl.ds(1, 3)])
            for o in (2, 1, 3):
                for p in range(3):
                    ax = orders[p][0]
                    s = pl.ds(pl.multiple_of(self.at + 4 * one * p + one * coords[ax], 16), one)
                    ref = gat.at[self.n, core, s, :]
                    self.group.send(ref, ref, peer(ax, ring(ax, o)))

        def gc(self):
            self.done()
            ref = gat.at[self.n, core, pl.ds(self.at, self.rows), :]
            self.group = remote(ref, ref, peer("c", 1 - core))

        def store(self):
            self.done()
            out = (o2, o1)[self.n]
            s = pl.ds(self.at, self.rows)
            for h in range(2):
                c = pltpu.make_async_copy(
                    gat.at[self.n, h, s, :], out.at[s, pl.ds(128 * h, 128)], lsem.at[7 + len(outs)]
                )
                c.start()
                outs.append(c)

    outs = []
    second = Piece(0)
    firsts = [Piece(1), Piece(2)]

    small_send(0, "c")
    grad_two = gp[128:128 + CELLS, :]
    for a in range(3):
        second.product(768 * a, a2t[:, 128 * a:128 * a + CELLS], grad_two)
    small_recv(0, "c")
    small_send(1, "x")

    edge.wait_recv()

    def build_grad(k, carry):
        s = pl.ds(pl.multiple_of(k * 128, 128), 128)
        row = t * ROWS - 2 + 2 * k + lax.div(iota((128, CH), 0), COLS)
        v = jnp.where((row >= 0) & (row < NT * ROWS), gp[s, :].astype(F32), 0.0)
        before, after = shifted(v, 2, 0, 0, 128)
        ag[s, 0:CH] = before
        ag[s, CH:2 * CH] = v.astype(BF16)
        ag[s, 2 * CH:3 * CH] = after
        return carry

    lax.fori_loop(0, 18, build_grad, 0)
    second.s1()

    def back(k, carry):
        n = 512
        total = None
        for a in range(3):
            s = pl.ds(pl.multiple_of(k * n + (2 - a) * 2 * COLS, 128), n)
            d = mm(ag[s, :], w2t[a])
            total = d if total is None else total + d
        h = a2[pl.ds(pl.multiple_of(128 + k * n, 128), n), CH:2 * CH].astype(F32)
        v = jnp.where(h > 0, total, 0.0).astype(BF16)
        xb[pl.ds(pl.multiple_of(k * n, n), n), :] = v
        return carry

    lax.fori_loop(0, 2, back, 0)
    small_recv(1, "x")
    small_send(2, "y")
    lax.fori_loop(2, 4, back, 0)
    second.s2()
    grad_one = xb[0:CELLS, :]
    firsts[0].product(0, a1e[:, 0:CELLS], grad_one)
    small_recv(2, "y")
    small_send(3, "z")
    firsts[0].product(768, a1o[...], grad_one)
    firsts[1].product(0, a1e[:, 128:128 + CELLS], grad_one)
    second.s3()
    firsts[0].s1()
    firsts[1].s1()
    second.g2()
    small_recv(3, "z")
    for c in firsts:
        c.s2()
    second.g1()
    for c in firsts:
        c.s3()
    ohead[:, 0:128] = small["head"][:64]
    ohead[:, 128:256] = small["head"][64:]
    oloss[...] = small["loss"]
    for c in firsts:
        c.g2()
    second.gc()
    second.store()
    for c in firsts:
        c.g1()
    for c in firsts:
        c.gc()
    for c in firsts:
        c.store()
    for c in groups:
        c.wait_send()
    for c in outs:
        c.wait()


def widen(first, second, head, loss, out_first, out_second, out_head, out_loss):
    out_first[...] = first[...].astype(F32)
    out_second[...] = second[...].astype(F32)
    out_head[...] = head[...]
    out_loss[...] = loss[0:1, 0:1] * (1.0 / (NZ * NT * CELLS))


def body(teacher_logits, coverage, features, labels, first_weight, second_weight, head_weight):
    any_spec = pl.BlockSpec(memory_space=pl.ANY)
    vmem = pl.BlockSpec(memory_space=pltpu.VMEM)
    out = [
        jax.ShapeDtypeStruct((2304, 256), BF16),
        jax.ShapeDtypeStruct((2304, 256), BF16),
        jax.ShapeDtypeStruct((NCLS, CH), F32),
        jax.ShapeDtypeStruct((8, 128), F32),
    ]
    V = pltpu.VMEM
    scratch = [
        V((4, 4, 32, 4096), BF16),
        V((2432, CH), BF16),
        V((2432, 3 * CH), BF16),
        V((3 * CH, 2304), BF16),
        V((3 * CH, 2048), BF16),
        V((2304, 3 * CH), BF16),
        V((3 * CH, 2304), BF16),
        V((2304, 3 * CH), BF16),
        V((2304, CH), BF16),
        V((3, 3 * CH, CH), BF16),
        V((3, 3 * CH, CH), BF16),
        V((3, 3 * CH, CH), BF16),
        V((2, CELLS, 128), F32),
        V((2, CELLS, 128), F32),
        V((2, 2, 2304, 128), BF16),
        V((2, 2, 32, 1024), BF16),
        V((2, 2, 32, 1024), BF16),
        V((2, 2, 2, 32, 1024), BF16),
        V((2, 2, 32, 1024), BF16),
        V((2, 2, 32, 1024), BF16),
        V((2, 2, 32, 1024), F32),
        V((2, 2, 32, 1024), F32),
        V((2, 3, 8, 128), F32),
        V((2, 3, 8, 128), F32),
        V((2, 128, 640), BF16),
        V((2, NT, 8, 640), BF16),
        V((2, NT, 8, 640), BF16),
        V((640, 256), F32),
        V((4, 4, 128, 128), BF16),
        V((4, 4, 8, 128), F32),
        V((256, 256), BF16),
        V((256, 128), BF16),
        V((256, 128), BF16),
        pltpu.SemaphoreType.DMA((NSEM,)),
        pltpu.SemaphoreType.DMA((NSEM,)),
        pltpu.SemaphoreType.DMA((16,)),
    ]
    for rows in PIECES:
        scratch += [
            V((rows, 128), BF16),
            V((rows, 128), BF16),
            V((rows, 128), F32),
            V((rows, 128), BF16),
            V((3, 4, rows // 12, 128), BF16),
            V((3, rows // 12, 128), F32),
            V((3, rows // 12, 128), BF16),
            V((3, 4, rows // 48, 128), BF16),
            V((3, 4, rows // 48, 128), BF16),
        ]
    first, second, head, loss = pl.pallas_call(
        kernel,
        out_shape=out,
        in_specs=[any_spec, vmem, any_spec, vmem, any_spec, any_spec, vmem],
        out_specs=[any_spec, any_spec, vmem, vmem],
        scratch_shapes=scratch,
        compiler_params=pltpu.CompilerParams(
            collective_id=0, has_side_effects=True, vmem_limit_bytes=67043328
        ),
    )(
        teacher_logits,
        coverage.reshape(1, 128),
        features.reshape(CELLS, CH),
        labels.reshape(ROWS, COLS),
        first_weight.reshape(3, 3 * CH, CH),
        second_weight.reshape(3, 3 * CH, CH),
        head_weight.T,
    )
    steps, rows = 4, 2304 // 4
    big = pl.BlockSpec((rows, CH), lambda i: (i, 0))
    first, second, head, loss = pl.pallas_call(
        widen,
        grid=(steps,),
        out_shape=[
            jax.ShapeDtypeStruct((2304, CH), F32),
            jax.ShapeDtypeStruct((2304, CH), F32),
            jax.ShapeDtypeStruct((NCLS, CH), F32),
            jax.ShapeDtypeStruct((1, 1), F32),
        ],
        in_specs=[
            big, big, pl.BlockSpec((NCLS, CH), lambda i: (0, 0)), pl.BlockSpec((8, 128), lambda i: (0, 0))
        ],
        out_specs=[
            big, big, pl.BlockSpec((NCLS, CH), lambda i: (0, 0)), pl.BlockSpec((1, 1), lambda i: (0, 0))
        ],
    )(first, second, head, loss)
    return (
        first.reshape(3, 3, CH, CH), second.reshape(3, 3, CH, CH), head.T, loss.reshape(())
    )


def solution(mesh):
    return jax.shard_map(
        body,
        mesh=mesh,
        in_specs=(
            P("member", "tile", None),
            P("tile"),
            P("member", "tile", None, None),
            P("member", "tile", None),
            P(),
            P(),
            P(),
        ),
        out_specs=(P(), P(), P(), P()),
        check_vma=False,
    )
```

```python
import math

import jax
import jax.numpy as jnp
from jax import lax
from jax.experimental import pallas as pl
from jax.experimental.pallas import tpu as pltpu
from jax.sharding import PartitionSpec as P

F32 = jnp.float32
BF16 = jnp.bfloat16
I32 = jnp.int32
MESH = pl.DeviceIdType.MESH

CH = 256
NCLS = 64
NZ = 4
NT = 32
ROWS = 32
COLS = 64
CELLS = ROWS * COLS
NSEM = 48
PIECES = (2304, 768, 768, 768)


def iota(shape, dim):
    return lax.broadcasted_iota(I32, shape, dim)


def onehot(mask):
    return jnp.where(mask, 1.0, 0.0).astype(BF16)


def mm(a, b):
    return jnp.dot(a, b, preferred_element_type=F32)


def mm_dims(a, b, ca, cb):
    return lax.dot_general(a, b, (((ca,), (cb,)), ((), ())), preferred_element_type=F32)


def kernel(
    tl, cov_h, feat, lab_h, w1h, w2h, wh_h,
    o1, o2, ohead, oloss,
    tv, xb, a1, a1e, a1o, a2, a2t, ag, gp, w1, w2, w2t, hf, gf, gat,
    rel_s, rel_r, fin_s, fin_l, fin_r, own, part, sec_s, sec_r,
    mp, sb, rb, mean_t, hx, lx, wb, wq, pick_s,
    cov, lab, wh, head_v, loss_v,
    ssem, rsem, lsem, *piece_refs,
):
    z = lax.axis_index("member")
    t = lax.axis_index("tile")
    core = lax.rem(t, 2)
    xc = lax.rem(lax.div(t, 2), 4)
    yc = lax.div(t, 8)
    coords = {"x": xc, "y": yc, "z": z, "c": core}

    def peer(axis, j):
        if axis == "z":
            return (j, t)
        if axis == "x":
            return (z, yc * 8 + j * 2 + core)
        if axis == "y":
            return (z, j * 8 + xc * 2 + core)
        return (z, yc * 8 + xc * 2 + j)

    groups = []

    class Group:
        def __init__(self, total):
            self.total, self.index = total, len(groups)
            groups.append(self)

        def describe(self, src, dst, dev):
            return pltpu.make_async_remote_copy(
                src_ref=src, dst_ref=dst, send_sem=ssem.at[self.index],
                recv_sem=rsem.at[self.index], device_id=dev, device_id_type=MESH,
            )

        def send(self, src, dst, dev):
            self.dev = dev
            self.describe(src, dst, dev).start()

        def wait_recv(self):
            self.describe(self.total, self.total, self.dev).wait_recv()

        def wait_send(self):
            self.describe(self.total, self.total, self.dev).wait_send()

    def remote(src, dst, dev):
        group = Group(dst)
        group.send(src, dst, dev)
        return group

    def ring(axis, o):
        return lax.rem(coords[axis] + o, 4)

    barrier = pltpu.get_barrier_semaphore()
    for o in range(1, NT):
        pl.semaphore_signal(barrier, inc=1, device_id=(z, lax.rem(t + o, NT)), device_id_type=MESH)
    for o in range(1, NZ):
        pl.semaphore_signal(barrier, inc=1, device_id=(lax.rem(z + o, NZ), t), device_id_type=MESH)

    zr, zl, zf = lax.rem(z + 1, NZ), lax.rem(z + 3, NZ), lax.rem(z + 2, NZ)
    loads = []
    for ci, g in enumerate((zf, zr, zl, z)):
        c = pltpu.make_async_copy(
            tl.at[:, pl.ds(pl.multiple_of(g * 32, 32), 32), :], tv.at[ci], lsem.at[ci]
        )
        c.start()
        loads.append(c)
    load_x = pltpu.make_async_copy(feat, xb.at[pl.ds(192, CELLS), :], lsem.at[4])
    load_w1 = pltpu.make_async_copy(w1h, w1, lsem.at[5])
    load_w2 = pltpu.make_async_copy(w2h, w2, lsem.at[6])
    load_x.start()
    load_w1.start()
    load_w2.start()
    load_small = [
        pltpu.make_async_copy(a, b, lsem.at[16 + i])
        for i, (a, b) in enumerate(((cov_h, cov), (lab_h, lab), (wh_h, wh)))
    ]
    for c in load_small:
        c.start()

    wb[...] = onehot(lax.div(iota((256, 256), 0), 64) == lax.div(iota((256, 256), 1), 64))
    wq[...] = onehot(lax.div(iota((256, 128), 0), 64) == iota((256, 128), 1))

    def cell_sums(v):
        hi = v.astype(BF16)
        lo = (v - hi.astype(F32)).astype(BF16)
        both = mm(jnp.concatenate([hi, lo], axis=0), wq[...])
        total = None
        for j in range(8):
            s = both[32 * j:32 * (j + 1)] + both[256 + 32 * j:288 + 32 * j]
            total = pltpu.roll(s, 4 * j, 1) + total if j else s
        return total

    def pack_cells(v):
        out = v[0:8]
        for g in range(1, 4):
            out = out + pltpu.roll(v[8 * g:8 * (g + 1)], 32 * g, 1)
        return out

    def unpack_cells(v):
        low = iota((8, 128), 1) < 32
        return jnp.concatenate(
            [jnp.where(low, pltpu.roll(v, 128 - 32 * g, 1) if g else v, 0.0) for g in range(4)],
            axis=0,
        )

    def soft(ci, half, put):
        x = jnp.concatenate(
            [
                tv[ci, :, :, half * 2048 + 256 * j:half * 2048 + 256 * (j + 1)].reshape(128, 256)
                for j in range(8)
            ],
            axis=0,
        ).astype(F32)
        e4 = jnp.exp2(x * (math.log2(math.e) / 4.0))
        r = e4 / mm(e4.astype(BF16), wb[...])
        r2 = r * r
        e = (r2 * r2).astype(BF16)
        p = e.astype(F32) / mm(e, wb[...])
        p = p.reshape(8, 4, 32, 256)
        sq = p * p
        f = (p[:, 0] + p[:, 1]) + (p[:, 2] + p[:, 3])
        q = (sq[:, 0] + sq[:, 1]) + (sq[:, 2] + sq[:, 3])
        for j in range(8):
            put(j, f[j])
        return pack_cells(cell_sums(q.reshape(256, 256)))

    def put_to(*subs):
        def put(j, v):
            ref = subs[j // 4]
            ref[:, 256 * (j % 4):256 * (j % 4 + 1)] = v.astype(ref.dtype)

        return put

    fin = [None, None]
    relay = [None, None]

    def send_relay(h):
        relay[h] = (
            remote(rel_s.at[h, 0], rel_r.at[h, 0], (zr, t)),
            remote(rel_s.at[h, 1], rel_r.at[h, 1], (zl, t)),
        )
        fin[h] = Group(fin_l)

    def send_own(h, side):
        if side == 0:
            fin[h].send(fin_s.at[0, h, 1], fin_l.at[h, 1], (zr, t))
        else:
            fin[h].send(fin_s.at[1, h, 0], fin_r.at[h, 0], (zl, t))

    def soft_far(h):
        sec_s[h, 0] = soft(0, h, put_to(rel_s.at[h, 0], rel_s.at[h, 1]))

    def soft_right(h):
        sec_s[h, 1] = soft(1, h, put_to(part.at[h, 0], fin_s.at[0, h, 1]))

    def soft_left(h):
        sec_s[h, 2] = soft(2, h, put_to(fin_s.at[1, h, 0], part.at[h, 1]))

    def finish_relay(h):
        relay[h][0].wait_recv()
        fin_s[0, h, 0] = (part[h, 0] + rel_r[h, 0].astype(F32)).astype(BF16)
        fin[h].send(fin_s.at[0, h, 0], fin_l.at[h, 0], (zr, t))
        relay[h][1].wait_recv()
        fin_s[1, h, 1] = (part[h, 1] + rel_r[h, 1].astype(F32)).astype(BF16)
        fin[h].send(fin_s.at[1, h, 1], fin_r.at[h, 1], (zl, t))
        group = Group(sec_r.at[h])
        for i, to in enumerate((zf, zr, zl)):
            group.send(sec_s.at[h, i], sec_r.at[h, i], (to, t))
        return group

    loads[0].wait()
    soft_far(0)
    pl.semaphore_wait(barrier, NT - 1 + NZ - 1)
    send_relay(0)
    up, down = lax.rem(t + 1, NT), lax.rem(t + NT - 1, NT)
    halo = Group(xb.at[pl.ds(0, 384), :])
    halo.send(feat.at[pl.ds(CELLS - 192, 192), :], xb.at[pl.ds(0, 192), :], (z, up))
    halo.send(feat.at[pl.ds(0, 192), :], xb.at[pl.ds(192 + CELLS, 192), :], (z, down))
    loads[1].wait()
    soft_right(0)
    send_own(0, 0)
    loads[2].wait()
    soft_left(0)
    send_own(0, 1)
    soft_far(1)
    soft_right(1)
    soft_left(1)
    sec_c = [finish_relay(0), None]
    send_relay(1)
    send_own(1, 0)
    send_own(1, 1)
    loads[3].wait()
    sec_m = [soft(3, h, put_to(own.at[h, 0], own.at[h, 1])) for h in range(2)]

    for c in load_small:
        c.wait()
    crow = cov[...]
    i0, i1 = iota((128, 128), 0), iota((128, 128), 1)
    ccol = jnp.sum(jnp.where(i0 == i1, crow, 0), axis=1, keepdims=True)
    same = (ccol == crow) & (lax.div(i0, 32) == lax.div(i1, 32)) & (i0 < i1)
    rank = jnp.sum(jnp.where(same, 1, 0), axis=0, keepdims=True)
    slot = jnp.broadcast_to(crow * 2 + rank, (8, 128)).astype(F32)
    lane8 = iota((8, 128), 1)
    mine = jnp.zeros((8, 128), F32)
    for g in range(NZ):
        moved = slot if g == 0 else pltpu.roll(slot, 128 - 32 * g, 1)
        mine = jnp.where(z == g, moved, mine)
    mine = jnp.where(lane8 < 32, mine, 0.0)
    mine = mine + pltpu.roll(mine, 32, 1)
    mine = mine + pltpu.roll(mine, 64, 1)
    slots = mine[0:1, :]
    j0, j1 = iota((256, 128), 0), iota((256, 128), 1)
    pick_s[...] = onehot(
        (lax.div(j0, 4).astype(F32) == slots) & (lax.rem(j0, 4) == lax.div(j1, 32))
    )

    def shifted(v, by, lo_col, hi_col, rows):
        col = lax.rem(iota((rows, CH), 0), COLS)
        before = jnp.where(col >= by, pltpu.roll(v, by, 0), 0.0)
        after = jnp.where(col < COLS - by, pltpu.roll(v, rows - by, 0), 0.0)
        return before.astype(BF16), after.astype(BF16)

    load_x.wait()
    load_w1.wait()
    halo.wait_recv()

    def build_one(k, carry):
        s = pl.ds(pl.multiple_of(k * 128, 128), 128)
        row = t * ROWS - 3 + 2 * k + lax.div(iota((128, CH), 0), COLS)
        v = xb[s, :].astype(F32)
        v = jnp.where((row >= 0) & (row < NT * ROWS), v, 0.0)
        before, after = shifted(v, 1, 0, 0, 128)
        a1[s, 0:CH] = before
        a1[s, CH:2 * CH] = v.astype(BF16)
        a1[s, 2 * CH:3 * CH] = after
        return carry

    lax.fori_loop(0, 19, build_one, 0)

    def conv_rows(a_ref, w_ref, start, rows, stride):
        total = None
        for a in range(3):
            s = pl.ds(pl.multiple_of(start + a * stride, 64), rows)
            d = mm(a_ref[s, :], w_ref[a])
            total = d if total is None else total + d
        return total

    def conv_one(k, carry):
        n = 256
        start = k * n
        pre = conv_rows(a1, w1, start, n, COLS)
        row = t * ROWS - 2 + 4 * k + lax.div(iota((n, CH), 0), COLS)
        h = jnp.where((row >= 0) & (row < NT * ROWS) & (pre > 0), pre, 0.0)
        h = h.astype(BF16).astype(F32)
        before, after = shifted(h, 2, 0, 0, n)
        s = pl.ds(pl.multiple_of(start, n), n)
        a2[s, 0:CH] = before
        a2[s, CH:2 * CH] = h.astype(BF16)
        a2[s, 2 * CH:3 * CH] = after
        a1e[:, s] = a1[pl.ds(pl.multiple_of(128 + start, 128), n), :].T
        odd = jnp.minimum(k, 7) * n
        a1o[:, pl.ds(pl.multiple_of(odd, n), n)] = a1[pl.ds(pl.multiple_of(192 + odd, 64), n), :].T
        return carry

    def send_tiles(h):
        fin[h].wait_recv()
        sec_c[h].wait_recv()
        squares = []
        for j in range(8):
            s = slice(256 * (j % 4), 256 * (j % 4 + 1))
            m = (
                own[h, j // 4, :, s] + fin_l[h, j // 4, :, s].astype(F32)
                + fin_r[h, j // 4, :, s].astype(F32)
            ) * (1.0 / 16.0)
            row = (j // 2) * 32
            mp[h, row:row + 32, (j % 2) * 256:(j % 2 + 1) * 256] = m.astype(BF16)
            squares.append(m * m)
        msq = cell_sums(jnp.concatenate(squares, axis=0))
        second = unpack_cells((sec_m[h] + sec_r[h, 0]) + (sec_r[h, 1] + sec_r[h, 2]))
        spread = second * (1.0 / 16.0) - msq
        lane = iota((32, 128), 1)
        slot_no = (iota((32, 128), 0) + 1).astype(F32)
        for a in range(4):
            sp = spread if a == 0 else pltpu.roll(spread, 128 - 8 * a, 1)
            sp = jnp.where(lane < 8, sp, 0.0)
            hi = sp.astype(BF16).astype(F32)
            mid = (sp - hi).astype(BF16).astype(F32)
            lo = sp - hi - mid
            ext = hi + pltpu.roll(mid, 8, 1) + pltpu.roll(lo, 16, 1)
            ext = jnp.where(lane == 24, slot_no, ext)
            mp[h, a * 32:(a + 1) * 32, 512:640] = ext.astype(BF16)
        sb[h] = mm(pick_s[...], mp[h]).astype(BF16).reshape(NT, 8, 640)
        group = Group(rb.at[h, pl.ds(0, NT - 1)])
        for o in range(1, NT):
            d = lax.rem(t + o, NT)
            group.send(sb.at[h, d], rb.at[h, t], (z, d))
        rb[h, t] = sb[h, t]
        return group

    exch = [send_tiles(0)]
    sec_c[1] = finish_relay(1)
    lax.fori_loop(0, 6, conv_one, 0)
    exch.append(send_tiles(1))
    lax.fori_loop(6, 9, conv_one, 0)


    load_w2.wait()

    def conv_two(k, carry):
        n = 256
        pre = conv_rows(a2, w2, k * n, n, 2 * COLS)
        h = jnp.where(pre > 0, pre, 0.0)
        s = pl.ds(pl.multiple_of(k * n, n), n)
        hf[0, s, :] = h[:, :128]
        hf[1, s, :] = h[:, 128:]
        a2t[:, s] = a2[s, :].T
        return carry

    lax.fori_loop(0, 8, conv_two, 0)
    a2t[:, CELLS:CELLS + 256] = a2[CELLS:CELLS + 256, :].T

    for a in range(3):
        for b in range(3):
            w2t[a, b * CH:(b + 1) * CH, :] = w2[a, (2 - b) * CH:(3 - b) * CH, :].T

    l_rep = onehot(lax.div(iota((256, 32), 0), 8) == iota((256, 32), 1))
    rep = mm(l_rep, lab[...].astype(F32).astype(BF16))
    rep = jnp.where(
        lax.div(iota((256, 64), 1), 8) == lax.rem(iota((256, 64), 0), 8), rep, 0.0
    ).astype(BF16)
    l_sel = onehot(lax.rem(iota((8, 64), 1), 8) == iota((8, 64), 0))
    labels = mm_dims(l_sel, rep, 1, 1)

    for c in exch:
        c.wait_recv()
    got = rb[...].reshape(512, 640)
    from_slot = got[:, 512:640].astype(F32)[:, 24:25]
    n0, n1 = iota((512, 256), 0), iota((512, 256), 1)
    tile_no = (lax.div(n1, 64) * 8 + lax.rem(n1, 8) + 1).astype(F32)
    place = onehot((from_slot == tile_no) & (lax.div(n0, 256) * 4 + lax.rem(n0, 4) == lax.rem(lax.div(n1, 8), 8)))
    mean_t[...] = mm_dims(got, place, 0, 0)

    scale = 1.0 / math.sqrt(NZ * NT * CELLS)
    head_w = wh[...]
    classes = iota((NCLS, 256), 0)
    loss = jnp.zeros((1, 256), F32)
    head_t = jnp.zeros((NCLS, CH), F32)
    for b in range(8):
        s = pl.ds(b, 256, stride=8)
        h32 = jnp.concatenate([hf[0, s, :], hf[1, s, :]], axis=1)
        hb = h32.astype(BF16)
        logits = mm_dims(head_w, hb, 1, 1)
        top = jnp.max(logits, axis=0, keepdims=True)
        low = logits - top
        log_s = low - jnp.log(jnp.sum(jnp.exp(low), axis=0, keepdims=True))
        prob = jnp.exp(log_s)
        mean = mean_t[b * 64:(b + 1) * 64, :]
        spr = mean_t[512 + b:513 + b, :] + mean_t[520 + b:521 + b, :] + mean_t[528 + b:529 + b, :]
        wgt = 1.0 / (0.1 + spr)
        hot = classes.astype(F32) == labels[b:b + 1, :]
        ent = jnp.where(mean > 0, mean * jnp.log(jnp.where(mean > 0, mean, 1.0)), 0.0)
        kl = jnp.sum(ent - mean * log_s, axis=0, keepdims=True)
        nll = jnp.sum(jnp.where(hot, log_s, 0.0), axis=0, keepdims=True)
        loss = loss + (wgt * kl - nll)
        lg = ((wgt * (prob - mean) + prob - jnp.where(hot, 1.0, 0.0)) * scale).astype(BF16)
        head_t = head_t + mm(lg, hb)
        hg = mm_dims(lg, head_w, 0, 0)
        g2 = jnp.where(h32 > 0, hg, 0.0)
        gf[0, s, :] = g2[:, :128]
        gf[1, s, :] = g2[:, 128:]

    def round_grad(k, carry):
        s = pl.ds(pl.multiple_of(k * 128, 128), 128)
        d = pl.ds(pl.multiple_of(128 + k * 128, 128), 128)
        gp[d, 0:128] = gf[0, s, :].astype(BF16)
        gp[d, 128:256] = gf[1, s, :].astype(BF16)
        return carry

    lax.fori_loop(0, 16, round_grad, 0)
    edge = Group(gp.at[pl.ds(0, 256), :])
    edge.send(gp.at[pl.ds(CELLS, 128), :], gp.at[pl.ds(0, 128), :], (z, up))
    edge.send(gp.at[pl.ds(128, 128), :], gp.at[pl.ds(128 + CELLS, 128), :], (z, down))

    small = {"head": jnp.concatenate([head_t[:, :128], head_t[:, 128:]], axis=0),
             "loss": jnp.broadcast_to(jnp.sum(loss, axis=1, keepdims=True), (8, 128))}

    def small_send(n, axis):
        me = coords[axis]
        hx[n, me] = small["head"].astype(BF16)
        lx[n, me] = small["loss"]
        size = 2 if axis == "c" else 4
        h, l = Group(hx.at[n, pl.ds(1, size - 1)]), Group(lx.at[n, pl.ds(1, size - 1)])
        small["wait"] = [h, l]
        for o in range(1, size):
            dev = peer(axis, lax.rem(me + o, size))
            h.send(hx.at[n, me], hx.at[n, me], dev)
            l.send(lx.at[n, me], lx.at[n, me], dev)

    def small_recv(n, axis):
        for c in small["wait"]:
            c.wait_recv()
        size = 2 if axis == "c" else 4
        h, l = hx[n, 0].astype(F32), lx[n, 0]
        for j in range(1, size):
            h = h + hx[n, j].astype(F32)
            l = l + lx[n, j]
        small["head"], small["loss"] = h, l

    orders = (("x", "y", "z"), ("y", "z", "x"), ("z", "x", "y"))

    class Piece:
        def __init__(self, index):
            self.refs = piece_refs[9 * index:9 * index + 9]
            self.rows = PIECES[index]
            self.n, self.at = (0, 0) if index == 0 else (1, 768 * (index - 1))
            self.group = Group(self.refs[1])

        def done(self):
            self.group.wait_recv()

        def spread(self, level, p, j):
            one, two = self.rows // 12, self.rows // 48
            if level == 1:
                return pl.ds(pl.multiple_of(4 * one * p + one * j, 16), one)
            first = one * coords[orders[p][0]]
            return pl.ds(pl.multiple_of(self.at + 4 * one * p + first + two * j, 16), two)

        def product(self, row, lhs, rhs):
            csb, crb, acc = self.refs[:3]
            d = mm(lhs, rhs)
            low, high = d[:, :128], d[:, 128:]
            acc[row:row + 768, :] = jnp.where(core == 0, low, high)
            csb[row:row + 768, :] = jnp.where(core == 0, high, low).astype(BF16)
            s = pl.ds(row, 768)
            self.group.send(csb.at[s, :], crb.at[s, :], peer("c", 1 - core))

        def s1(self):
            self.done()
            csb, crb, acc, s1b, r1 = self.refs[:5]

            def step(k, carry):
                s = pl.ds(pl.multiple_of(k * 256, 256), 256)
                v = acc[s, :] + crb[s, :].astype(F32)
                acc[s, :] = v
                s1b[s, :] = v.astype(BF16)
                return carry

            lax.fori_loop(0, self.rows // 256, step, 0)
            self.group = Group(r1.at[:, pl.ds(1, 3)])
            for o in (2, 1, 3):
                for p in range(3):
                    ax = orders[p][0]
                    j = ring(ax, o)
                    src = s1b.at[self.spread(1, p, j), :]
                    self.group.send(src, r1.at[p, o], peer(ax, j))

        def s2(self):
            self.done()
            acc, r1, a1c, s2b, r2 = self.refs[2], *self.refs[4:8]
            for p in range(3):
                v = acc[self.spread(1, p, coords[orders[p][0]]), :]
                for o in range(1, 4):
                    v = v + r1[p, o].astype(F32)
                a1c[p] = v
                s2b[p] = v.astype(BF16)
            two = self.rows // 48
            self.group = Group(r2.at[:, pl.ds(1, 3)])
            for o in (2, 1, 3):
                for p in range(3):
                    ax = orders[p][1]
                    j = ring(ax, o)
                    src = s2b.at[p, pl.ds(pl.multiple_of(two * j, 16), two), :]
                    self.group.send(src, r2.at[p, o], peer(ax, j))

        def s3(self):
            self.done()
            a1c, s2b, r2, x3 = self.refs[5:9]
            two = self.rows // 48
            for p in range(3):
                s = pl.ds(pl.multiple_of(two * coords[orders[p][1]], 16), two)
                v = a1c[p, s, :]
                for o in range(1, 4):
                    v = v + r2[p, o].astype(F32)
                x3[p, coords[orders[p][2]]] = v.astype(BF16)
            self.group = Group(x3.at[:, pl.ds(1, 3)])
            for o in (2, 1, 3):
                for p in range(3):
                    ax = orders[p][2]
                    ref = x3.at[p, coords[ax]]
                    self.group.send(ref, ref, peer(ax, ring(ax, o)))

        def g2(self):
            self.done()
            x3 = self.refs[8]
            for p in range(3):
                v = x3[p, 0].astype(F32)
                for j in range(1, 4):
                    v = v + x3[p, j].astype(F32)
                gat[self.n, core, self.spread(2, p, coords[orders[p][1]]), :] = v.astype(BF16)
            self.group = Group(x3.at[:, pl.ds(1, 3)])
            for o in (2, 1, 3):
                for p in range(3):
                    ax = orders[p][1]
                    ref = gat.at[self.n, core, self.spread(2, p, coords[ax]), :]
                    self.group.send(ref, ref, peer(ax, ring(ax, o)))

        def g1(self):
            self.done()
            one = self.rows // 12
            self.group = Group(self.refs[4].at[:, pl.ds(1, 3)])
            for o in (2, 1, 3):
                for p in range(3):
                    ax = orders[p][0]
                    s = pl.ds(pl.multiple_of(self.at + 4 * one * p + one * coords[ax], 16), one)
                    ref = gat.at[self.n, core, s, :]
                    self.group.send(ref, ref, peer(ax, ring(ax, o)))

        def gc(self):
            self.done()
            ref = gat.at[self.n, core, pl.ds(self.at, self.rows), :]
            self.group = remote(ref, ref, peer("c", 1 - core))

        def store(self):
            self.done()
            out = (o2, o1)[self.n]
            s = pl.ds(self.at, self.rows)
            for h in range(2):
                c = pltpu.make_async_copy(
                    gat.at[self.n, h, s, :], out.at[s, pl.ds(128 * h, 128)], lsem.at[7 + len(outs)]
                )
                c.start()
                outs.append(c)

    outs, late = [], []
    second = Piece(0)
    firsts = [Piece(1), Piece(2), Piece(3)]

    small_send(0, "c")
    grad_two = gp[128:128 + CELLS, :]
    for a in range(3):
        second.product(768 * a, a2t[:, 128 * a:128 * a + CELLS], grad_two)
    small_recv(0, "c")
    small_send(1, "x")

    edge.wait_recv()

    def build_grad(k, carry):
        s = pl.ds(pl.multiple_of(k * 128, 128), 128)
        row = t * ROWS - 2 + 2 * k + lax.div(iota((128, CH), 0), COLS)
        v = jnp.where((row >= 0) & (row < NT * ROWS), gp[s, :].astype(F32), 0.0)
        before, after = shifted(v, 2, 0, 0, 128)
        ag[s, 0:CH] = before
        ag[s, CH:2 * CH] = v.astype(BF16)
        ag[s, 2 * CH:3 * CH] = after
        return carry

    lax.fori_loop(0, 18, build_grad, 0)
    second.s1()

    def back(k, carry):
        n = 256
        total = None
        for a in range(3):
            s = pl.ds(pl.multiple_of(k * n + (2 - a) * 2 * COLS, 128), n)
            d = mm(ag[s, :], w2t[a])
            total = d if total is None else total + d
        h = a2[pl.ds(pl.multiple_of(128 + k * n, 128), n), CH:2 * CH].astype(F32)
        v = jnp.where(h > 0, total, 0.0).astype(BF16)
        xb[pl.ds(pl.multiple_of(k * n, n), n), :] = v
        return carry

    lax.fori_loop(0, 8, back, 0)
    second.s2()
    grad_one = xb[0:CELLS, :]
    firsts[0].product(0, a1e[:, 0:CELLS], grad_one)
    firsts[1].product(0, a1o[...], grad_one)
    firsts[0].s1()
    firsts[2].product(0, a1e[:, 128:128 + CELLS], grad_one)
    second.s3()
    firsts[1].s1()
    firsts[2].s1()
    small_recv(1, "x")
    small_send(2, "y")
    second.g2()
    for c in firsts:
        c.s2()
    small_recv(2, "y")
    small_send(3, "z")
    second.g1()
    for c in firsts:
        c.s3()
    small_recv(3, "z")
    head_v[:, 0:128] = small["head"][:64]
    head_v[:, 128:256] = small["head"][64:]
    loss_v[...] = small["loss"]
    for i, (a, b) in enumerate(((head_v, ohead), (loss_v, oloss))):
        c = pltpu.make_async_copy(a, b, lsem.at[19 + i])
        c.start()
        late.append(c)
    for c in firsts:
        c.g2()
    second.gc()
    for c in firsts:
        c.g1()
    second.store()
    for c in firsts:
        c.gc()
    for c in firsts:
        c.store()
    for c in groups:
        c.wait_send()
    for c in outs + late:
        c.wait()


def widen(first, second, head, loss, out_first, out_second, out_head, out_loss):
    out_first[...] = first[...].astype(F32)
    out_second[...] = second[...].astype(F32)
    out_head[...] = head[...]
    out_loss[...] = loss[0:1, 0:1] * (1.0 / (NZ * NT * CELLS))


def body(teacher_logits, coverage, features, labels, first_weight, second_weight, head_weight):
    any_spec = pl.BlockSpec(memory_space=pl.ANY)
    out = [
        jax.ShapeDtypeStruct((2304, 256), BF16),
        jax.ShapeDtypeStruct((2304, 256), BF16),
        jax.ShapeDtypeStruct((NCLS, CH), F32),
        jax.ShapeDtypeStruct((8, 128), F32),
    ]
    V = pltpu.VMEM
    scratch = [
        V((4, 4, 32, 4096), BF16),
        V((2432, CH), BF16),
        V((2432, 3 * CH), BF16),
        V((3 * CH, 2304), BF16),
        V((3 * CH, 2048), BF16),
        V((2304, 3 * CH), BF16),
        V((3 * CH, 2304), BF16),
        V((2304, 3 * CH), BF16),
        V((2304, CH), BF16),
        V((3, 3 * CH, CH), BF16),
        V((3, 3 * CH, CH), BF16),
        V((3, 3 * CH, CH), BF16),
        V((2, CELLS, 128), F32),
        V((2, CELLS, 128), F32),
        V((2, 2, 2304, 128), BF16),
        V((2, 2, 32, 1024), BF16),
        V((2, 2, 32, 1024), BF16),
        V((2, 2, 2, 32, 1024), BF16),
        V((2, 2, 32, 1024), BF16),
        V((2, 2, 32, 1024), BF16),
        V((2, 2, 32, 1024), F32),
        V((2, 2, 32, 1024), F32),
        V((2, 3, 8, 128), F32),
        V((2, 3, 8, 128), F32),
        V((2, 128, 640), BF16),
        V((2, NT, 8, 640), BF16),
        V((2, NT, 8, 640), BF16),
        V((640, 256), F32),
        V((4, 4, 128, 128), BF16),
        V((4, 4, 8, 128), F32),
        V((256, 256), BF16),
        V((256, 128), BF16),
        V((256, 128), BF16),
        V((1, 128), I32),
        V((ROWS, COLS), I32),
        V((NCLS, CH), BF16),
        V((NCLS, CH), F32),
        V((8, 128), F32),
        pltpu.SemaphoreType.DMA((NSEM,)),
        pltpu.SemaphoreType.DMA((NSEM,)),
        pltpu.SemaphoreType.DMA((21,)),
    ]
    for rows in PIECES:
        scratch += [
            V((rows, 128), BF16),
            V((rows, 128), BF16),
            V((rows, 128), F32),
            V((rows, 128), BF16),
            V((3, 4, rows // 12, 128), BF16),
            V((3, rows // 12, 128), F32),
            V((3, rows // 12, 128), BF16),
            V((3, 4, rows // 48, 128), BF16),
            V((3, 4, rows // 48, 128), BF16),
        ]
    first, second, head, loss = pl.pallas_call(
        kernel,
        out_shape=out,
        in_specs=[any_spec] * 7,
        out_specs=[any_spec] * 4,
        scratch_shapes=scratch,
        compiler_params=pltpu.CompilerParams(
            collective_id=0, has_side_effects=True, vmem_limit_bytes=67043328
        ),
    )(
        teacher_logits,
        coverage.reshape(1, 128),
        features.reshape(CELLS, CH),
        labels.reshape(ROWS, COLS),
        first_weight.reshape(3, 3 * CH, CH),
        second_weight.reshape(3, 3 * CH, CH),
        head_weight.T,
    )
    steps, rows = 4, 2304 // 4
    big = pl.BlockSpec((rows, CH), lambda i: (i, 0))
    first, second, head, loss = pl.pallas_call(
        widen,
        grid=(steps,),
        out_shape=[
            jax.ShapeDtypeStruct((2304, CH), F32),
            jax.ShapeDtypeStruct((2304, CH), F32),
            jax.ShapeDtypeStruct((NCLS, CH), F32),
            jax.ShapeDtypeStruct((1, 1), F32),
        ],
        in_specs=[
            big, big, pl.BlockSpec((NCLS, CH), lambda i: (0, 0)), pl.BlockSpec((8, 128), lambda i: (0, 0))
        ],
        out_specs=[
            big, big, pl.BlockSpec((NCLS, CH), lambda i: (0, 0)), pl.BlockSpec((1, 1), lambda i: (0, 0))
        ],
    )(first, second, head, loss)
    return (
        first.reshape(3, 3, CH, CH), second.reshape(3, 3, CH, CH), head.T, loss.reshape(())
    )


def solution(mesh):
    return jax.shard_map(
        body,
        mesh=mesh,
        in_specs=(
            P("member", "tile", None),
            P("tile"),
            P("member", "tile", None, None),
            P("member", "tile", None),
            P(),
            P(),
            P(),
        ),
        out_specs=(P(), P(), P(), P()),
        check_vma=False,
    )
```

```python
import math

import jax
import jax.numpy as jnp
from jax import lax
from jax.experimental import pallas as pl
from jax.experimental.pallas import tpu as pltpu
from jax.sharding import PartitionSpec as P

F32 = jnp.float32
BF16 = jnp.bfloat16
I32 = jnp.int32
MESH = pl.DeviceIdType.MESH

CH = 256
NCLS = 64
NZ = 4
NT = 32
ROWS = 32
COLS = 64
CELLS = ROWS * COLS
NSEM = 48
PIECES = (2304, 768, 768, 768)


def iota(shape, dim):
    return lax.broadcasted_iota(I32, shape, dim)


def onehot(mask):
    return jnp.where(mask, 1.0, 0.0).astype(BF16)


def mm(a, b):
    return jnp.dot(a, b, preferred_element_type=F32)


def mm_dims(a, b, ca, cb):
    return lax.dot_general(a, b, (((ca,), (cb,)), ((), ())), preferred_element_type=F32)


def kernel(
    tl, cov_h, feat, lab_h, w1h, w2h, wh_h,
    o1, o2, ohead, oloss,
    tv, xb, a1, a1e, a1o, a2, a2t, ag, gp, w1, w2, w2t, hf, gf, gat,
    rel_s, rel_r, fin_s, fin_l, fin_r, own, part, sec_s, sec_r,
    mp, sb, rb, mean_t, hx, lx, wb, wq, pick_s,
    cov, lab, wh, head_v, loss_v,
    ssem, rsem, lsem, *piece_refs,
):
    z = lax.axis_index("member")
    t = lax.axis_index("tile")
    core = lax.rem(t, 2)
    xc = lax.rem(lax.div(t, 2), 4)
    yc = lax.div(t, 8)
    coords = {"x": xc, "y": yc, "z": z, "c": core}

    def peer(axis, j):
        if axis == "z":
            return (j, t)
        if axis == "x":
            return (z, yc * 8 + j * 2 + core)
        if axis == "y":
            return (z, j * 8 + xc * 2 + core)
        return (z, yc * 8 + xc * 2 + j)

    groups = []

    class Group:
        def __init__(self, total):
            self.total, self.index = total, len(groups)
            groups.append(self)

        def describe(self, src, dst, dev):
            return pltpu.make_async_remote_copy(
                src_ref=src, dst_ref=dst, send_sem=ssem.at[self.index],
                recv_sem=rsem.at[self.index], device_id=dev, device_id_type=MESH,
            )

        def send(self, src, dst, dev):
            self.dev = dev
            self.describe(src, dst, dev).start()

        def wait_recv(self):
            self.describe(self.total, self.total, self.dev).wait_recv()

        def wait_send(self):
            self.describe(self.total, self.total, self.dev).wait_send()

    def remote(src, dst, dev):
        group = Group(dst)
        group.send(src, dst, dev)
        return group

    def ring(axis, o):
        return lax.rem(coords[axis] + o, 4)

    barrier = pltpu.get_barrier_semaphore()
    for o in range(1, NT):
        pl.semaphore_signal(barrier, inc=1, device_id=(z, lax.rem(t + o, NT)), device_id_type=MESH)
    for o in range(1, NZ):
        pl.semaphore_signal(barrier, inc=1, device_id=(lax.rem(z + o, NZ), t), device_id_type=MESH)

    zr, zl, zf = lax.rem(z + 1, NZ), lax.rem(z + 3, NZ), lax.rem(z + 2, NZ)
    loads = []
    for ci, g in enumerate((zf, zr, zl, z)):
        c = pltpu.make_async_copy(
            tl.at[:, pl.ds(pl.multiple_of(g * 32, 32), 32), :], tv.at[ci], lsem.at[ci]
        )
        c.start()
        loads.append(c)
    load_x = pltpu.make_async_copy(feat, xb.at[pl.ds(192, CELLS), :], lsem.at[4])
    load_w1 = pltpu.make_async_copy(w1h, w1, lsem.at[5])
    load_w2 = pltpu.make_async_copy(w2h, w2, lsem.at[6])
    load_x.start()
    load_w1.start()
    load_w2.start()
    load_small = [
        pltpu.make_async_copy(a, b, lsem.at[16 + i])
        for i, (a, b) in enumerate(((cov_h, cov), (lab_h, lab), (wh_h, wh)))
    ]
    for c in load_small:
        c.start()

    wb[...] = onehot(lax.div(iota((256, 256), 0), 64) == lax.div(iota((256, 256), 1), 64))
    wq[...] = onehot(lax.div(iota((256, 128), 0), 64) == iota((256, 128), 1))

    def cell_sums(v):
        hi = v.astype(BF16)
        lo = (v - hi.astype(F32)).astype(BF16)
        both = mm(jnp.concatenate([hi, lo], axis=0), wq[...])
        total = None
        for j in range(8):
            s = both[32 * j:32 * (j + 1)] + both[256 + 32 * j:288 + 32 * j]
            total = pltpu.roll(s, 4 * j, 1) + total if j else s
        return total

    def pack_cells(v):
        out = v[0:8]
        for g in range(1, 4):
            out = out + pltpu.roll(v[8 * g:8 * (g + 1)], 32 * g, 1)
        return out

    def unpack_cells(v):
        low = iota((8, 128), 1) < 32
        return jnp.concatenate(
            [jnp.where(low, pltpu.roll(v, 128 - 32 * g, 1) if g else v, 0.0) for g in range(4)],
            axis=0,
        )

    def soft(ci, half, put):
        x = jnp.concatenate(
            [
                tv[ci, :, :, half * 2048 + 256 * j:half * 2048 + 256 * (j + 1)].reshape(128, 256)
                for j in range(8)
            ],
            axis=0,
        ).astype(F32)
        e4 = jnp.exp2(x * (math.log2(math.e) / 4.0))
        r = e4 / mm(e4.astype(BF16), wb[...])
        r2 = r * r
        e = (r2 * r2).astype(BF16)
        p = e.astype(F32) / mm(e, wb[...])
        p = p.reshape(8, 4, 32, 256)
        sq = p * p
        f = (p[:, 0] + p[:, 1]) + (p[:, 2] + p[:, 3])
        q = (sq[:, 0] + sq[:, 1]) + (sq[:, 2] + sq[:, 3])
        for j in range(8):
            put(j, f[j])
        return pack_cells(cell_sums(q.reshape(256, 256)))

    def put_to(*subs):
        def put(j, v):
            ref = subs[j // 4]
            ref[:, 256 * (j % 4):256 * (j % 4 + 1)] = v.astype(ref.dtype)

        return put

    fin = [None, None]
    relay = [None, None]

    def send_relay(h):
        relay[h] = (
            remote(rel_s.at[h, 0], rel_r.at[h, 0], (zr, t)),
            remote(rel_s.at[h, 1], rel_r.at[h, 1], (zl, t)),
        )
        fin[h] = Group(fin_l)

    def send_own(h, side):
        if side == 0:
            fin[h].send(fin_s.at[0, h, 1], fin_l.at[h, 1], (zr, t))
        else:
            fin[h].send(fin_s.at[1, h, 0], fin_r.at[h, 0], (zl, t))

    def soft_far(h):
        sec_s[h, 0] = soft(0, h, put_to(rel_s.at[h, 0], rel_s.at[h, 1]))

    def soft_right(h):
        sec_s[h, 1] = soft(1, h, put_to(part.at[h, 0], fin_s.at[0, h, 1]))

    def soft_left(h):
        sec_s[h, 2] = soft(2, h, put_to(fin_s.at[1, h, 0], part.at[h, 1]))

    def finish_relay(h):
        relay[h][0].wait_recv()
        fin_s[0, h, 0] = (part[h, 0] + rel_r[h, 0].astype(F32)).astype(BF16)
        fin[h].send(fin_s.at[0, h, 0], fin_l.at[h, 0], (zr, t))
        relay[h][1].wait_recv()
        fin_s[1, h, 1] = (part[h, 1] + rel_r[h, 1].astype(F32)).astype(BF16)
        fin[h].send(fin_s.at[1, h, 1], fin_r.at[h, 1], (zl, t))
        group = Group(sec_r.at[h])
        for i, to in enumerate((zf, zr, zl)):
            group.send(sec_s.at[h, i], sec_r.at[h, i], (to, t))
        return group

    loads[0].wait()
    soft_far(0)
    pl.semaphore_wait(barrier, NT - 1 + NZ - 1)
    send_relay(0)
    up, down = lax.rem(t + 1, NT), lax.rem(t + NT - 1, NT)
    halo = Group(xb.at[pl.ds(0, 384), :])
    halo.send(feat.at[pl.ds(CELLS - 192, 192), :], xb.at[pl.ds(0, 192), :], (z, up))
    halo.send(feat.at[pl.ds(0, 192), :], xb.at[pl.ds(192 + CELLS, 192), :], (z, down))
    loads[1].wait()
    soft_right(0)
    send_own(0, 0)
    loads[2].wait()
    soft_left(0)
    send_own(0, 1)
    soft_far(1)
    soft_right(1)
    soft_left(1)
    sec_c = [finish_relay(0), None]
    send_relay(1)
    send_own(1, 0)
    send_own(1, 1)
    loads[3].wait()
    sec_m = [soft(3, h, put_to(own.at[h, 0], own.at[h, 1])) for h in range(2)]

    for c in load_small:
        c.wait()
    crow = cov[...]
    i0, i1 = iota((128, 128), 0), iota((128, 128), 1)
    ccol = jnp.sum(jnp.where(i0 == i1, crow, 0), axis=1, keepdims=True)
    same = (ccol == crow) & (lax.div(i0, 32) == lax.div(i1, 32)) & (i0 < i1)
    rank = jnp.sum(jnp.where(same, 1, 0), axis=0, keepdims=True)
    slot = jnp.broadcast_to(crow * 2 + rank, (8, 128)).astype(F32)
    lane8 = iota((8, 128), 1)
    mine = jnp.zeros((8, 128), F32)
    for g in range(NZ):
        moved = slot if g == 0 else pltpu.roll(slot, 128 - 32 * g, 1)
        mine = jnp.where(z == g, moved, mine)
    mine = jnp.where(lane8 < 32, mine, 0.0)
    mine = mine + pltpu.roll(mine, 32, 1)
    mine = mine + pltpu.roll(mine, 64, 1)
    slots = mine[0:1, :]
    j0, j1 = iota((256, 128), 0), iota((256, 128), 1)
    pick_s[...] = onehot(
        (lax.div(j0, 4).astype(F32) == slots) & (lax.rem(j0, 4) == lax.div(j1, 32))
    )

    def shifted(v, by, lo_col, hi_col, rows):
        col = lax.rem(iota((rows, CH), 0), COLS)
        before = jnp.where(col >= by, pltpu.roll(v, by, 0), 0.0)
        after = jnp.where(col < COLS - by, pltpu.roll(v, rows - by, 0), 0.0)
        return before.astype(BF16), after.astype(BF16)

    load_x.wait()
    load_w1.wait()
    halo.wait_recv()

    def build_one(k, carry):
        s = pl.ds(pl.multiple_of(k * 128, 128), 128)
        row = t * ROWS - 3 + 2 * k + lax.div(iota((128, CH), 0), COLS)
        v = xb[s, :].astype(F32)
        v = jnp.where((row >= 0) & (row < NT * ROWS), v, 0.0)
        before, after = shifted(v, 1, 0, 0, 128)
        a1[s, 0:CH] = before
        a1[s, CH:2 * CH] = v.astype(BF16)
        a1[s, 2 * CH:3 * CH] = after
        return carry

    lax.fori_loop(0, 19, build_one, 0)

    def conv_rows(a_ref, w_ref, start, rows, stride):
        total = None
        for a in range(3):
            s = pl.ds(pl.multiple_of(start + a * stride, 64), rows)
            d = mm(a_ref[s, :], w_ref[a])
            total = d if total is None else total + d
        return total

    def conv_one(k, carry):
        n = 256
        start = k * n
        pre = conv_rows(a1, w1, start, n, COLS)
        row = t * ROWS - 2 + 4 * k + lax.div(iota((n, CH), 0), COLS)
        h = jnp.where((row >= 0) & (row < NT * ROWS) & (pre > 0), pre, 0.0)
        h = h.astype(BF16).astype(F32)
        before, after = shifted(h, 2, 0, 0, n)
        s = pl.ds(pl.multiple_of(start, n), n)
        a2[s, 0:CH] = before
        a2[s, CH:2 * CH] = h.astype(BF16)
        a2[s, 2 * CH:3 * CH] = after
        a1e[:, s] = a1[pl.ds(pl.multiple_of(128 + start, 128), n), :].T
        odd = jnp.minimum(k, 7) * n
        a1o[:, pl.ds(pl.multiple_of(odd, n), n)] = a1[pl.ds(pl.multiple_of(192 + odd, 64), n), :].T
        return carry

    def send_tiles(h):
        fin[h].wait_recv()
        sec_c[h].wait_recv()
        squares = []
        for j in range(8):
            s = slice(256 * (j % 4), 256 * (j % 4 + 1))
            m = (
                own[h, j // 4, :, s] + fin_l[h, j // 4, :, s].astype(F32)
                + fin_r[h, j // 4, :, s].astype(F32)
            ) * (1.0 / 16.0)
            row = (j // 2) * 32
            mp[h, row:row + 32, (j % 2) * 256:(j % 2 + 1) * 256] = m.astype(BF16)
            squares.append(m * m)
        msq = cell_sums(jnp.concatenate(squares, axis=0))
        second = unpack_cells((sec_m[h] + sec_r[h, 0]) + (sec_r[h, 1] + sec_r[h, 2]))
        spread = second * (1.0 / 16.0) - msq
        lane = iota((32, 128), 1)
        slot_no = (iota((32, 128), 0) + 1).astype(F32)
        for a in range(4):
            sp = spread if a == 0 else pltpu.roll(spread, 128 - 8 * a, 1)
            sp = jnp.where(lane < 8, sp, 0.0)
            hi = sp.astype(BF16).astype(F32)
            mid = (sp - hi).astype(BF16).astype(F32)
            lo = sp - hi - mid
            ext = hi + pltpu.roll(mid, 8, 1) + pltpu.roll(lo, 16, 1)
            ext = jnp.where(lane == 24, slot_no, ext)
            mp[h, a * 32:(a + 1) * 32, 512:640] = ext.astype(BF16)
        sb[h] = mm(pick_s[...], mp[h]).astype(BF16).reshape(NT, 8, 640)
        group = Group(rb.at[h, pl.ds(0, NT - 1)])
        for o in range(1, NT):
            d = lax.rem(t + o, NT)
            group.send(sb.at[h, d], rb.at[h, t], (z, d))
        rb[h, t] = sb[h, t]
        return group

    exch = [send_tiles(0)]
    sec_c[1] = finish_relay(1)
    lax.fori_loop(0, 6, conv_one, 0)
    exch.append(send_tiles(1))
    lax.fori_loop(6, 9, conv_one, 0)


    load_w2.wait()

    def conv_two(k, carry):
        n = 256
        pre = conv_rows(a2, w2, k * n, n, 2 * COLS)
        h = jnp.where(pre > 0, pre, 0.0)
        s = pl.ds(pl.multiple_of(k * n, n), n)
        hf[0, s, :] = h[:, :128]
        hf[1, s, :] = h[:, 128:]
        a2t[:, s] = a2[s, :].T
        return carry

    lax.fori_loop(0, 8, conv_two, 0)
    a2t[:, CELLS:CELLS + 256] = a2[CELLS:CELLS + 256, :].T

    for a in range(3):
        for b in range(3):
            w2t[a, b * CH:(b + 1) * CH, :] = w2[a, (2 - b) * CH:(3 - b) * CH, :].T

    l_rep = onehot(lax.div(iota((256, 32), 0), 8) == iota((256, 32), 1))
    rep = mm(l_rep, lab[...].astype(F32).astype(BF16))
    rep = jnp.where(
        lax.div(iota((256, 64), 1), 8) == lax.rem(iota((256, 64), 0), 8), rep, 0.0
    ).astype(BF16)
    l_sel = onehot(lax.rem(iota((8, 64), 1), 8) == iota((8, 64), 0))
    labels = mm_dims(l_sel, rep, 1, 1)

    for c in exch:
        c.wait_recv()
    got = rb[...].reshape(512, 640)
    from_slot = got[:, 512:640].astype(F32)[:, 24:25]
    n0, n1 = iota((512, 256), 0), iota((512, 256), 1)
    tile_no = (lax.div(n1, 64) * 8 + lax.rem(n1, 8) + 1).astype(F32)
    place = onehot((from_slot == tile_no) & (lax.div(n0, 256) * 4 + lax.rem(n0, 4) == lax.rem(lax.div(n1, 8), 8)))
    mean_t[...] = mm_dims(got, place, 0, 0)

    scale = 1.0 / math.sqrt(NZ * NT * CELLS)
    head_w = wh[...]
    classes = iota((NCLS, 256), 0)
    loss = jnp.zeros((1, 256), F32)
    head_t = jnp.zeros((NCLS, CH), F32)
    for b in range(8):
        s = pl.ds(b, 256, stride=8)
        h32 = jnp.concatenate([hf[0, s, :], hf[1, s, :]], axis=1)
        hb = h32.astype(BF16)
        logits = mm_dims(head_w, hb, 1, 1)
        top = jnp.max(logits, axis=0, keepdims=True)
        low = logits - top
        log_s = low - jnp.log(jnp.sum(jnp.exp(low), axis=0, keepdims=True))
        prob = jnp.exp(log_s)
        mean = mean_t[b * 64:(b + 1) * 64, :]
        spr = mean_t[512 + b:513 + b, :] + mean_t[520 + b:521 + b, :] + mean_t[528 + b:529 + b, :]
        wgt = 1.0 / (0.1 + spr)
        hot = classes.astype(F32) == labels[b:b + 1, :]
        ent = jnp.where(mean > 0, mean * jnp.log(jnp.where(mean > 0, mean, 1.0)), 0.0)
        kl = jnp.sum(ent - mean * log_s, axis=0, keepdims=True)
        nll = jnp.sum(jnp.where(hot, log_s, 0.0), axis=0, keepdims=True)
        loss = loss + (wgt * kl - nll)
        lg = ((wgt * (prob - mean) + prob - jnp.where(hot, 1.0, 0.0)) * scale).astype(BF16)
        head_t = head_t + mm(lg, hb)
        hg = mm_dims(lg, head_w, 0, 0)
        g2 = jnp.where(h32 > 0, hg, 0.0)
        gf[0, s, :] = g2[:, :128]
        gf[1, s, :] = g2[:, 128:]

    def round_grad(k, carry):
        s = pl.ds(pl.multiple_of(k * 128, 128), 128)
        d = pl.ds(pl.multiple_of(128 + k * 128, 128), 128)
        gp[d, 0:128] = gf[0, s, :].astype(BF16)
        gp[d, 128:256] = gf[1, s, :].astype(BF16)
        return carry

    lax.fori_loop(0, 16, round_grad, 0)
    edge = Group(gp.at[pl.ds(0, 256), :])
    edge.send(gp.at[pl.ds(CELLS, 128), :], gp.at[pl.ds(0, 128), :], (z, up))
    edge.send(gp.at[pl.ds(128, 128), :], gp.at[pl.ds(128 + CELLS, 128), :], (z, down))

    small = {"head": jnp.concatenate([head_t[:, :128], head_t[:, 128:]], axis=0),
             "loss": jnp.broadcast_to(jnp.sum(loss, axis=1, keepdims=True), (8, 128))}

    def small_send(n, axis):
        me = coords[axis]
        hx[n, me] = small["head"].astype(BF16)
        lx[n, me] = small["loss"]
        size = 2 if axis == "c" else 4
        h, l = Group(hx.at[n, pl.ds(1, size - 1)]), Group(lx.at[n, pl.ds(1, size - 1)])
        small["wait"] = [h, l]
        for o in range(1, size):
            dev = peer(axis, lax.rem(me + o, size))
            h.send(hx.at[n, me], hx.at[n, me], dev)
            l.send(lx.at[n, me], lx.at[n, me], dev)

    def small_recv(n, axis):
        for c in small["wait"]:
            c.wait_recv()
        size = 2 if axis == "c" else 4
        h, l = hx[n, 0].astype(F32), lx[n, 0]
        for j in range(1, size):
            h = h + hx[n, j].astype(F32)
            l = l + lx[n, j]
        small["head"], small["loss"] = h, l

    orders = (("x", "y", "z"), ("y", "z", "x"), ("z", "x", "y"))

    class Piece:
        def __init__(self, index):
            self.refs = piece_refs[9 * index:9 * index + 9]
            self.rows = PIECES[index]
            self.n, self.at = (0, 0) if index == 0 else (1, 768 * (index - 1))
            self.group = Group(self.refs[1])

        def done(self):
            self.group.wait_recv()

        def spread(self, level, p, j):
            one, two = self.rows // 12, self.rows // 48
            if level == 1:
                return pl.ds(pl.multiple_of(4 * one * p + one * j, 16), one)
            first = one * coords[orders[p][0]]
            return pl.ds(pl.multiple_of(self.at + 4 * one * p + first + two * j, 16), two)

        def product(self, row, lhs, rhs):
            csb, crb, acc = self.refs[:3]
            d = mm(lhs, rhs)
            low, high = d[:, :128], d[:, 128:]
            acc[row:row + 768, :] = jnp.where(core == 0, low, high)
            csb[row:row + 768, :] = jnp.where(core == 0, high, low).astype(BF16)
            s = pl.ds(row, 768)
            self.group.send(csb.at[s, :], crb.at[s, :], peer("c", 1 - core))

        def s1(self):
            self.done()
            csb, crb, acc, s1b, r1 = self.refs[:5]

            def step(k, carry):
                s = pl.ds(pl.multiple_of(k * 256, 256), 256)
                v = acc[s, :] + crb[s, :].astype(F32)
                acc[s, :] = v
                s1b[s, :] = v.astype(BF16)
                return carry

            lax.fori_loop(0, self.rows // 256, step, 0)
            self.group = Group(r1.at[:, pl.ds(1, 3)])
            for o in (2, 1, 3):
                for p in range(3):
                    ax = orders[p][0]
                    j = ring(ax, o)
                    src = s1b.at[self.spread(1, p, j), :]
                    self.group.send(src, r1.at[p, o], peer(ax, j))

        def s2(self):
            self.done()
            acc, r1, a1c, s2b, r2 = self.refs[2], *self.refs[4:8]
            for p in range(3):
                v = acc[self.spread(1, p, coords[orders[p][0]]), :]
                for o in range(1, 4):
                    v = v + r1[p, o].astype(F32)
                a1c[p] = v
                s2b[p] = v.astype(BF16)
            two = self.rows // 48
            self.group = Group(r2.at[:, pl.ds(1, 3)])
            for o in (2, 1, 3):
                for p in range(3):
                    ax = orders[p][1]
                    j = ring(ax, o)
                    src = s2b.at[p, pl.ds(pl.multiple_of(two * j, 16), two), :]
                    self.group.send(src, r2.at[p, o], peer(ax, j))

        def s3(self):
            self.done()
            a1c, s2b, r2, x3 = self.refs[5:9]
            two = self.rows // 48
            for p in range(3):
                s = pl.ds(pl.multiple_of(two * coords[orders[p][1]], 16), two)
                v = a1c[p, s, :]
                for o in range(1, 4):
                    v = v + r2[p, o].astype(F32)
                x3[p, coords[orders[p][2]]] = v.astype(BF16)
            self.group = Group(x3.at[:, pl.ds(1, 3)])
            for o in (2, 1, 3):
                for p in range(3):
                    ax = orders[p][2]
                    ref = x3.at[p, coords[ax]]
                    self.group.send(ref, ref, peer(ax, ring(ax, o)))

        def g2(self):
            self.done()
            x3 = self.refs[8]
            for p in range(3):
                v = x3[p, 0].astype(F32)
                for j in range(1, 4):
                    v = v + x3[p, j].astype(F32)
                gat[self.n, core, self.spread(2, p, coords[orders[p][1]]), :] = v.astype(BF16)
            self.group = Group(x3.at[:, pl.ds(1, 3)])
            for o in (2, 1, 3):
                for p in range(3):
                    ax = orders[p][1]
                    ref = gat.at[self.n, core, self.spread(2, p, coords[ax]), :]
                    self.group.send(ref, ref, peer(ax, ring(ax, o)))

        def g1(self):
            self.done()
            one = self.rows // 12
            self.group = Group(self.refs[4].at[:, pl.ds(1, 3)])
            for o in (2, 1, 3):
                for p in range(3):
                    ax = orders[p][0]
                    s = pl.ds(pl.multiple_of(self.at + 4 * one * p + one * coords[ax], 16), one)
                    ref = gat.at[self.n, core, s, :]
                    self.group.send(ref, ref, peer(ax, ring(ax, o)))

        def gc(self):
            self.done()
            ref = gat.at[self.n, core, pl.ds(self.at, self.rows), :]
            self.group = remote(ref, ref, peer("c", 1 - core))

        def store(self):
            self.done()
            out = (o2, o1)[self.n]
            s = pl.ds(self.at, self.rows)
            for h in range(2):
                c = pltpu.make_async_copy(
                    gat.at[self.n, h, s, :], out.at[s, pl.ds(128 * h, 128)], lsem.at[7 + len(outs)]
                )
                c.start()
                outs.append(c)

    outs, late = [], []
    second = Piece(0)
    firsts = [Piece(1), Piece(2), Piece(3)]

    small_send(0, "c")
    grad_two = gp[128:128 + CELLS, :]
    for a in range(3):
        second.product(768 * a, a2t[:, 128 * a:128 * a + CELLS], grad_two)
    small_recv(0, "c")
    small_send(1, "x")

    edge.wait_recv()

    def build_grad(k, carry):
        s = pl.ds(pl.multiple_of(k * 128, 128), 128)
        row = t * ROWS - 2 + 2 * k + lax.div(iota((128, CH), 0), COLS)
        v = jnp.where((row >= 0) & (row < NT * ROWS), gp[s, :].astype(F32), 0.0)
        before, after = shifted(v, 2, 0, 0, 128)
        ag[s, 0:CH] = before
        ag[s, CH:2 * CH] = v.astype(BF16)
        ag[s, 2 * CH:3 * CH] = after
        return carry

    lax.fori_loop(0, 18, build_grad, 0)
    second.s1()

    def back(k, carry):
        n = 256
        total = None
        for a in range(3):
            s = pl.ds(pl.multiple_of(k * n + (2 - a) * 2 * COLS, 128), n)
            d = mm(ag[s, :], w2t[a])
            total = d if total is None else total + d
        h = a2[pl.ds(pl.multiple_of(128 + k * n, 128), n), CH:2 * CH].astype(F32)
        v = jnp.where(h > 0, total, 0.0).astype(BF16)
        xb[pl.ds(pl.multiple_of(k * n, n), n), :] = v
        return carry

    lax.fori_loop(0, 8, back, 0)
    second.s2()
    grad_one = xb[0:CELLS, :]
    firsts[0].product(0, a1e[:, 0:CELLS], grad_one)
    firsts[1].product(0, a1o[...], grad_one)
    firsts[0].s1()
    firsts[2].product(0, a1e[:, 128:128 + CELLS], grad_one)
    second.s3()
    firsts[1].s1()
    firsts[2].s1()
    small_recv(1, "x")
    small_send(2, "y")
    second.g2()
    for c in firsts:
        c.s2()
    small_recv(2, "y")
    small_send(3, "z")
    second.g1()
    for c in firsts:
        c.s3()
    small_recv(3, "z")
    head_v[:, 0:128] = small["head"][:64]
    head_v[:, 128:256] = small["head"][64:]
    loss_v[...] = small["loss"]
    for i, (a, b) in enumerate(((head_v, ohead), (loss_v, oloss))):
        c = pltpu.make_async_copy(a, b, lsem.at[19 + i])
        c.start()
        late.append(c)
    for c in firsts:
        c.g2()
    second.gc()
    for c in firsts:
        c.g1()
    second.store()
    for c in firsts:
        c.gc()
    for c in firsts:
        c.store()
    for c in groups:
        c.wait_send()
    for c in outs + late:
        c.wait()


def widen(first, second, head, loss, out_first, out_second, out_head, out_loss,
          narrow, wide, head_v, loss_v, sem_in, sem_out):
    rows = 2304 // 4
    reads, writes = [], []
    for i in range(8):
        s = pl.ds(rows * (i // 2), rows)
        reads.append(
            pltpu.make_async_copy((first, second)[i % 2].at[s, :], narrow.at[i % 2, s, :], sem_in.at[i])
        )
        writes.append(
            pltpu.make_async_copy(
                wide.at[i % 2, s, :], (out_first, out_second)[i % 2].at[s, :], sem_out.at[i]
            )
        )
    read_loss = pltpu.make_async_copy(loss, loss_v, sem_in.at[8])
    read_head = pltpu.make_async_copy(head, head_v, sem_in.at[9])
    write_head = pltpu.make_async_copy(head_v, out_head, sem_out.at[8])
    for c in (*reads, read_loss, read_head):
        c.start()
    for i in range(8):
        s = pl.ds(rows * (i // 2), rows)
        reads[i].wait()
        wide[i % 2, s, :] = narrow[i % 2, s, :].astype(F32)
        writes[i].start()
    read_head.wait()
    write_head.start()
    read_loss.wait()
    out_loss[...] = loss_v[0:1, 0:1] * (1.0 / (NZ * NT * CELLS))
    for c in (*writes, write_head):
        c.wait()


def body(teacher_logits, coverage, features, labels, first_weight, second_weight, head_weight):
    any_spec = pl.BlockSpec(memory_space=pl.ANY)
    out = [
        jax.ShapeDtypeStruct((2304, 256), BF16),
        jax.ShapeDtypeStruct((2304, 256), BF16),
        jax.ShapeDtypeStruct((NCLS, CH), F32),
        jax.ShapeDtypeStruct((8, 128), F32),
    ]
    V = pltpu.VMEM
    scratch = [
        V((4, 4, 32, 4096), BF16),
        V((2432, CH), BF16),
        V((2432, 3 * CH), BF16),
        V((3 * CH, 2304), BF16),
        V((3 * CH, 2048), BF16),
        V((2304, 3 * CH), BF16),
        V((3 * CH, 2304), BF16),
        V((2304, 3 * CH), BF16),
        V((2304, CH), BF16),
        V((3, 3 * CH, CH), BF16),
        V((3, 3 * CH, CH), BF16),
        V((3, 3 * CH, CH), BF16),
        V((2, CELLS, 128), F32),
        V((2, CELLS, 128), F32),
        V((2, 2, 2304, 128), BF16),
        V((2, 2, 32, 1024), BF16),
        V((2, 2, 32, 1024), BF16),
        V((2, 2, 2, 32, 1024), BF16),
        V((2, 2, 32, 1024), BF16),
        V((2, 2, 32, 1024), BF16),
        V((2, 2, 32, 1024), F32),
        V((2, 2, 32, 1024), F32),
        V((2, 3, 8, 128), F32),
        V((2, 3, 8, 128), F32),
        V((2, 128, 640), BF16),
        V((2, NT, 8, 640), BF16),
        V((2, NT, 8, 640), BF16),
        V((640, 256), F32),
        V((4, 4, 128, 128), BF16),
        V((4, 4, 8, 128), F32),
        V((256, 256), BF16),
        V((256, 128), BF16),
        V((256, 128), BF16),
        V((1, 128), I32),
        V((ROWS, COLS), I32),
        V((NCLS, CH), BF16),
        V((NCLS, CH), F32),
        V((8, 128), F32),
        pltpu.SemaphoreType.DMA((NSEM,)),
        pltpu.SemaphoreType.DMA((NSEM,)),
        pltpu.SemaphoreType.DMA((21,)),
    ]
    for rows in PIECES:
        scratch += [
            V((rows, 128), BF16),
            V((rows, 128), BF16),
            V((rows, 128), F32),
            V((rows, 128), BF16),
            V((3, 4, rows // 12, 128), BF16),
            V((3, rows // 12, 128), F32),
            V((3, rows // 12, 128), BF16),
            V((3, 4, rows // 48, 128), BF16),
            V((3, 4, rows // 48, 128), BF16),
        ]
    first, second, head, loss = pl.pallas_call(
        kernel,
        out_shape=out,
        in_specs=[any_spec] * 7,
        out_specs=[any_spec] * 4,
        scratch_shapes=scratch,
        compiler_params=pltpu.CompilerParams(
            collective_id=0, has_side_effects=True, vmem_limit_bytes=67043328
        ),
    )(
        teacher_logits,
        coverage.reshape(1, 128),
        features.reshape(CELLS, CH),
        labels.reshape(ROWS, COLS),
        first_weight.reshape(3, 3 * CH, CH),
        second_weight.reshape(3, 3 * CH, CH),
        head_weight.T,
    )
    first, second, head, loss = pl.pallas_call(
        widen,
        out_shape=[
            jax.ShapeDtypeStruct((2304, CH), F32),
            jax.ShapeDtypeStruct((2304, CH), F32),
            jax.ShapeDtypeStruct((NCLS, CH), F32),
            jax.ShapeDtypeStruct((1, 1), F32),
        ],
        in_specs=[any_spec] * 4,
        out_specs=[any_spec] * 3 + [pl.BlockSpec(memory_space=pltpu.VMEM)],
        scratch_shapes=[
            V((2, 2304, CH), BF16),
            V((2, 2304, CH), F32),
            V((NCLS, CH), F32),
            V((8, 128), F32),
            pltpu.SemaphoreType.DMA((10,)),
            pltpu.SemaphoreType.DMA((9,)),
        ],
    )(first, second, head, loss)
    return (
        first.reshape(3, 3, CH, CH), second.reshape(3, 3, CH, CH), head.T, loss.reshape(())
    )


def solution(mesh):
    return jax.shard_map(
        body,
        mesh=mesh,
        in_specs=(
            P("member", "tile", None),
            P("tile"),
            P("member", "tile", None, None),
            P("member", "tile", None),
            P(),
            P(),
            P(),
        ),
        out_specs=(P(), P(), P(), P()),
        check_vma=False,
    )
```
